256 devices in a mesh: rcv: 4 (over z_lo), shot: 64 (over z_hi, y, x, core).
Axes of the slice: x: 4, y: 4, z: 8 (z_hi: 2, z_lo: 4; z = z_hi * 4 + z_lo), core: 2. Of those that a mesh axis runs over, the one named last changes fastest.
Arguments:
- traces: bfloat16 [16, 2000, 8192], P('rcv', None, 'shot'), may hold values from -6 to 6
- first_trace_taps: bfloat16 [8, 16], replicated, may hold values from -1.5 to 1.5
- first_time_taps: bfloat16 [8, 64], replicated, may hold values from -0.25 to 0.25
- second_trace_taps: bfloat16 [8, 16], replicated, may hold values from -1.5 to 1.5
- second_time_taps: bfloat16 [8, 64], replicated, may hold values from -0.25 to 0.25
- dest_row: int32 [16, 64], P('rcv', 'shot'), may hold values from 0 to 15, as said below
Outputs:
- filtered: float32 [16, 2000, 8192], P('rcv', None, 'shot')
The draws below stay inside these ranges and needn't reach their ends.
Inputs may be any that keep to these rules, and one draw needn't show every extreme that they name: For each column c, dest_row[:, c] is a permutation of the gathers; the rows r * 4 to (r + 1) * 4 - 1 of a column send at most 2 blocks into the rows o * 4 to (o + 1) * 4 - 1 for any o, and exactly 2 into some such range.
All inputs are finite; a program needn't handle non-finite values.
Results may differ from the reference program's by a relative error of at most 0.005.
Values may be sent and summed in bfloat16 or wider, within the bound.
No kernel may reach another device: no remote copies, remote signals or barrier semaphores. Data moves between devices by JAX's collectives and lax.ppermute only.
A program may use at most 64 MiB of HBM per device.

```python
import jax
import jax.numpy as jnp
from jax import lax

SAMPLES = 2000
BLOCK_TR = 128
FANS = 8
TIME_TAPS = 64
TRACE_TAPS = 16
G_DEV = 4
GATHERS = 16
LINE = 8192


def draw_dest_row(key, part):
    blocks = G_DEV
    owners = GATHERS // G_DEV
    columns = LINE // BLOCK_TR
    slot_cap = blocks // 2
    total = owners * blocks

    def one_column(column_key):
        key_one, key_two, key_three = jax.random.split(column_key, 3)
        offsets = jax.random.permutation(key_one, owners)[:3]
        ranking = jax.vmap(lambda inner: jax.random.permutation(inner, blocks))(jax.random.split(key_two, owners))
        group = jnp.where(ranking < slot_cap, 0, 1 + (ranking - slot_cap) // (slot_cap // 2))
        source = jnp.arange(owners, dtype=jnp.int32)[:, None]
        target = ((source + offsets[group]) % owners).reshape(-1)
        score = target * total + jax.random.permutation(key_three, total)
        order = jnp.argsort(score)
        return jnp.zeros((total,), jnp.int32).at[order].set(jnp.arange(total, dtype=jnp.int32))
    return jax.vmap(one_column)(jax.random.split(key, columns)).T.astype(jnp.int32)


def levels(rng, extent, shards, low, top_value):
    loudness, own = 1.0, jax.random.fold_in(rng, 6)
    for axis_at, parts in shards:
        steps = jnp.exp(jax.random.uniform(jax.random.fold_in(own, axis_at), (parts,), jnp.float32, low / len(shards), top_value / len(shards)))
        loudness = loudness * jnp.repeat(steps, extent[axis_at] // parts).reshape([-1 if axis == axis_at else 1 for axis in range(len(extent))])
    return loudness


def bell_draw(own_key, shape, scale, most, cuts=(), held_as=jnp.bfloat16):
    values = scale * jax.random.normal(own_key, shape, jnp.float32)
    if cuts:
        values = values * levels(own_key, shape, cuts, -0.22, 0.18)
    return jnp.clip(values, -most, most).astype(held_as)


def setup_inputs(seed: int = 0) -> dict:
    arg_keys = jax.random.split(jax.random.key(seed), 7)
    traces = bell_draw(arg_keys[0], (GATHERS, SAMPLES, LINE), 1.0, 6.0, ((0, 4), (2, 64)))
    first_trace_taps = bell_draw(arg_keys[1], (FANS, TRACE_TAPS), TRACE_TAPS ** -0.5, 1.5)
    first_time_taps = bell_draw(arg_keys[2], (FANS, TIME_TAPS), (FANS * TIME_TAPS) ** -0.5, 0.25)
    second_trace_taps = bell_draw(arg_keys[3], (FANS, TRACE_TAPS), TRACE_TAPS ** -0.5, 1.5)
    second_time_taps = bell_draw(arg_keys[4], (FANS, TIME_TAPS), (FANS * TIME_TAPS) ** -0.5, 0.25)
    dest_row = draw_dest_row(jax.random.fold_in(arg_keys[6], 71), 0)
    return {"traces": traces, "first_trace_taps": first_trace_taps, "first_time_taps": first_time_taps, "second_trace_taps": second_trace_taps, "second_time_taps": second_time_taps, "dest_row": dest_row}


def trace_filter(gather, taps):
    width = taps.shape[1]
    lhs = gather.astype(jnp.float32)[None, None]
    rhs = taps.astype(jnp.float32)[:, None, None, :]
    result = lax.conv_general_dilated(lhs, rhs, (1, 1), ((0, 0), (width // 2, width - 1 - width // 2)), precision=lax.Precision.HIGHEST)
    return result[0].astype(jnp.bfloat16)


def time_filter(fanned, taps):
    width = taps.shape[1]
    lhs = fanned.astype(jnp.float32)[None]
    rhs = taps.astype(jnp.float32)[None, :, :, None]
    result = lax.conv_general_dilated(lhs, rhs, (1, 1), ((width // 2, width - 1 - width // 2), (0, 0)), precision=lax.Precision.HIGHEST)
    return result[0, 0]


def reference(traces, first_trace_taps, first_time_taps, second_trace_taps, second_time_taps, dest_row):
    first_pass = lax.map(lambda gather: time_filter(trace_filter(gather, first_trace_taps), first_time_taps).astype(jnp.bfloat16), traces)
    columns = LINE // BLOCK_TR
    split = first_pass.reshape(GATHERS, SAMPLES, columns, BLOCK_TR)
    column_ids = jnp.arange(columns, dtype=jnp.int32)[None, :]
    gather_ids = jnp.broadcast_to(jnp.arange(GATHERS, dtype=jnp.int32)[:, None], (GATHERS, columns))
    source = jnp.zeros((GATHERS, columns), jnp.int32).at[dest_row.astype(jnp.int32), jnp.broadcast_to(column_ids, (GATHERS, columns))].set(gather_ids)
    moved = split[source, :, column_ids, :]
    resorted = jnp.transpose(moved, (0, 2, 1, 3)).reshape(GATHERS, SAMPLES, LINE)
    return lax.map(lambda gather: time_filter(trace_filter(gather, second_trace_taps), second_time_taps), resorted)
```

```python
import functools

import jax
import jax.numpy as jnp
from jax import lax
from jax.experimental import pallas as pl
from jax.experimental.pallas import tpu as pltpu
from jax.sharding import PartitionSpec as P

LANES = 128
EDGE = 8
SPAN = 256
REACH = 64
WIDE = SPAN - REACH


PARAMS = pltpu.CompilerParams(vmem_limit_bytes=16 * 2**20)


def chunk_bounds(samples):
    sizes = [384, 576, 576]
    bounds = [0]
    for size in sizes:
        if bounds[-1] + size + REACH <= samples:
            bounds.append(bounds[-1] + size)
    bounds.append(samples)
    return bounds


def segment_plan(rows):
    count = -(-rows // WIDE)
    width = min(WIDE, -(-rows // (16 * count)) * 16)
    return count, width


def weights_kernel(trace_ref, time_ref, _, mats_ref, times_ref):
    fans = trace_ref.shape[0]
    blocks = mats_ref.shape[0]
    for fan in range(fans):
        row = jnp.broadcast_to(trace_ref[fan : fan + 1, :], (LANES, SPAN))
        own = pltpu.roll(row, 0, 1, stride=1, stride_axis=0)[:, :LANES]
        left = pltpu.roll(row[:EDGE], SPAN - EDGE, 1, stride=1, stride_axis=0)[:, :LANES]
        right = pltpu.roll(row[:EDGE], LANES, 1, stride=1, stride_axis=0)[:, :LANES]
        pair, half = fan // 2, fan % 2
        cols = slice(half * LANES, (half + 1) * LANES)
        for block in range(blocks):
            before, after = EDGE * block, EDGE * (blocks - 1 - block)
            parts = []
            for piece in (left, right):
                if before:
                    parts.append(jnp.zeros((before, LANES), jnp.float32))
                parts.append(piece)
                if after:
                    parts.append(jnp.zeros((after, LANES), jnp.float32))
            parts.append(jnp.zeros((LANES - 2 * EDGE * blocks, LANES), jnp.float32))
            mats_ref[block, pair, :LANES, cols] = own.astype(jnp.bfloat16)
            mats_ref[block, pair, LANES:, cols] = jnp.concatenate(parts, axis=0).astype(
                jnp.bfloat16
            )
        taps = jnp.broadcast_to(time_ref[fan : fan + 1, :], (WIDE, SPAN))
        times_ref[:, fan * SPAN : (fan + 1) * SPAN] = pltpu.roll(
            taps, 0, 1, stride=1, stride_axis=0
        ).astype(jnp.bfloat16)


def weights(trace_taps, time_taps, after, blocks):
    fans, width = trace_taps.shape
    turned = jnp.pad(trace_taps[:, ::-1].astype(jnp.float32), ((0, 0), (0, SPAN - width)))
    turned = jnp.roll(turned, width // 2 - width + 1, axis=1)
    late = jnp.pad(time_taps.astype(jnp.float32), ((0, 0), (0, SPAN - time_taps.shape[1])))
    whole = pl.BlockSpec(memory_space=pltpu.VMEM)
    return pl.pallas_call(
        weights_kernel,
        in_specs=[whole, whole, pl.BlockSpec(memory_space=pl.ANY)],
        out_shape=(
            jax.ShapeDtypeStruct((blocks, fans // 2, 2 * LANES, 2 * LANES), jnp.bfloat16),
            jax.ShapeDtypeStruct((WIDE, fans * SPAN), jnp.bfloat16),
        ),
        cost_estimate=pl.CostEstimate(flops=1, bytes_accessed=1, transcendentals=0),
        compiler_params=PARAMS,
        name="weights",
    )(turned, late, after)


def edges_dot(tiles, out_ref):
    blocks = len(tiles)
    lane = lax.broadcasted_iota(jnp.int32, (LANES, LANES), 1)
    trace = lax.broadcasted_iota(jnp.int32, (LANES, LANES), 0)
    total = None
    for block, tile in enumerate(tiles):
        at = lane - EDGE * block
        last = (at >= 0) & (at < EDGE) & (trace == at + LANES - EDGE)
        at = at - EDGE * blocks
        first = (at >= 0) & (at < EDGE) & (trace == at)
        pick = jnp.where(last | first, 1.0, 0.0).astype(jnp.bfloat16)
        part = jnp.dot(tile, pick, preferred_element_type=jnp.float32)
        total = part if total is None else total + part
    out_ref[...] = total.astype(jnp.bfloat16)


def first_edges_kernel(x_ref, out_ref):
    edges_dot([x_ref[block] for block in range(x_ref.shape[0])], out_ref)


def first_edges(traces, start, stop):
    blocks = traces.shape[0]
    rows = stop - start
    return pl.pallas_call(
        first_edges_kernel,
        grid=(1,),
        in_specs=[
            pl.BlockSpec(
                (pl.Element(blocks), pl.Element(rows), pl.Element(LANES)),
                lambda i: (0, start, 0),
            )
        ],
        out_specs=pl.BlockSpec((rows, LANES), lambda i: (0, 0)),
        out_shape=jax.ShapeDtypeStruct((rows, LANES), jnp.bfloat16),
        cost_estimate=pl.CostEstimate(
            flops=1,
            bytes_accessed=1,
            transcendentals=0,
        ),
        compiler_params=PARAMS,
        name="first_edges",
    )(traces)


def second_edges_kernel(slot_ref, *refs):
    parts, (_, sorted_ref, out_ref, sem) = refs[:-4], refs[-4:]
    blocks, slot_cap = sorted_ref.shape[0], parts[0].shape[0]
    for block in range(blocks):
        slot = slot_ref[block]
        for offset, part in enumerate(parts):

            @pl.when(slot // slot_cap == offset)
            def _():
                pltpu.make_async_copy(
                    part.at[slot % slot_cap], sorted_ref.at[block], sem.at[block]
                ).start()

    for block in range(blocks):
        pltpu.make_async_copy(parts[0].at[0], sorted_ref.at[block], sem.at[block]).wait()
    edges_dot([sorted_ref[block] for block in range(blocks)], out_ref)


def second_edges(slots, arrived, after, blocks):
    rows = arrived[0].shape[1]
    return pl.pallas_call(
        second_edges_kernel,
        grid_spec=pltpu.PrefetchScalarGridSpec(
            num_scalar_prefetch=1,
            grid=(1,),
            in_specs=[pl.BlockSpec(memory_space=pl.ANY)] * (len(arrived) + 1),
            out_specs=[
                pl.BlockSpec((blocks, rows, LANES), lambda i, slot: (0, 0, 0)),
                pl.BlockSpec((rows, LANES), lambda i, slot: (0, 0)),
            ],
            scratch_shapes=[pltpu.SemaphoreType.DMA((blocks,))],
        ),
        out_shape=[
            jax.ShapeDtypeStruct((blocks, rows, LANES), jnp.bfloat16),
            jax.ShapeDtypeStruct((rows, LANES), jnp.bfloat16),
        ],
        cost_estimate=pl.CostEstimate(
            flops=1,
            bytes_accessed=1,
            transcendentals=0,
        ),
        compiler_params=PARAMS,
        name="second_edges",
    )(slots, *arrived, after)


def swap_edges(edges):
    count = lax.axis_size("shot")
    forward = [(i, i + 1) for i in range(count - 1)]
    backward = [(target, source) for source, target in forward]
    return lax.ppermute(edges, "shot", forward), lax.ppermute(edges, "shot", backward)


def merge_edges(low, high, blocks):
    lane = lax.broadcasted_iota(jnp.int32, low.shape, 1)
    return jnp.where(lane < EDGE * blocks, low, high)


def filter_window(window, fans_ref, mats_ref, times_ref, rows, give):
    pairs = mats_ref.shape[1]
    count, width = segment_plan(rows)

    def trace_step(pair, carry):
        for half in range(2):
            both = jnp.dot(
                window[half], mats_ref[half, pair], preferred_element_type=jnp.float32
            ).astype(jnp.bfloat16)
            cols = slice(half * LANES, (half + 1) * LANES)
            fans_ref[2 * pair, :, cols] = both[:, :LANES]
            fans_ref[2 * pair + 1, :, cols] = both[:, LANES:]
        return carry

    lax.fori_loop(0, pairs, trace_step, 0)

    def time_step(step, carry):
        start = pl.multiple_of(jnp.minimum(step * width, rows - width), 16)
        total = None
        for fan in range(2 * pairs):
            part = jnp.dot(
                times_ref[:width, fan * SPAN : (fan + 1) * SPAN],
                fans_ref[fan, pl.ds(start, SPAN), :],
                preferred_element_type=jnp.float32,
            )
            total = part if total is None else total + part
        give(start, total)
        return carry

    lax.fori_loop(0, count, time_step, 0)


def window_rows(rows):
    count, width = segment_plan(rows)
    return rows - width + SPAN


def pass_cost(rows, tall, blocks, fans, byte_count):
    return pl.CostEstimate(
        flops=1,
        bytes_accessed=1,
        transcendentals=0,
    )


def first_kernel(
    lead, key_ref, x_ref, low_ref, high_ref, mats_ref, times_ref, after_ref, *refs
):
    outs, (window, fans_ref, done, sem) = refs[:-4], refs[-4:]
    step = pl.program_id(0)
    held, tall, rows = x_ref.shape[1], window.shape[1], done.shape[1]
    blocks = done.shape[0]
    slot_cap = outs[0].shape[0]
    merged = merge_edges(low_ref[...], high_ref[...], blocks)
    for half in range(2):
        if lead:
            window[half, :lead, :] = jnp.zeros((lead, 2 * LANES), jnp.bfloat16)
        window[half, lead : lead + held, :LANES] = x_ref[half]
        window[half, lead : lead + held, LANES:] = merged
        if tall > lead + held:
            window[half, lead + held :, :] = jnp.zeros(
                (tall - lead - held, 2 * LANES), jnp.bfloat16
            )

    def give(start, values):
        values = values.astype(jnp.bfloat16)
        for half in range(2):
            done[2 * step + half, pl.ds(start, values.shape[0]), :] = values[
                :, half * LANES : (half + 1) * LANES
            ]

    filter_window(window, fans_ref, mats_ref, times_ref, rows, give)

    for half in range(2):
        block = 2 * step + half
        key = key_ref[block]
        for offset, out_ref in enumerate(outs):

            @pl.when(key // slot_cap == offset)
            def _():
                pltpu.make_async_copy(
                    done.at[block], out_ref.at[key % slot_cap], sem.at[block]
                ).start()

    @pl.when(step == pl.num_programs(0) - 1)
    def _():
        for block in range(blocks):
            pltpu.make_async_copy(done.at[block], outs[0].at[0], sem.at[block]).wait()


def first_pass(keys, owners, traces, edges, edges_at, mats, times, after, start, stop):
    blocks, samples, _ = traces.shape
    fans = 2 * mats.shape[1]
    rows = stop - start
    tall = window_rows(rows)
    begin, end = max(0, start - REACH // 2), min(samples, stop + REACH // 2)
    held = end - begin
    edge_spec = pl.BlockSpec(
        (pl.Element(held), pl.Element(LANES)), lambda i, key: (begin - edges_at, 0)
    )
    sent = jax.ShapeDtypeStruct((blocks // 2, rows, LANES), jnp.bfloat16)
    return pl.pallas_call(
        functools.partial(first_kernel, begin - (start - REACH // 2)),
        grid_spec=pltpu.PrefetchScalarGridSpec(
            num_scalar_prefetch=1,
            grid=(blocks // 2,),
            in_specs=[
                pl.BlockSpec(
                    (pl.Element(2), pl.Element(held), pl.Element(LANES)),
                    lambda i, key: (2 * i, begin, 0),
                ),
                edge_spec,
                edge_spec,
                pl.BlockSpec((2,) + mats.shape[1:], lambda i, key: (i, 0, 0, 0)),
                pl.BlockSpec(times.shape, lambda i, key: (0, 0)),
                pl.BlockSpec(memory_space=pl.ANY),
            ],
            out_specs=[pl.BlockSpec(memory_space=pl.ANY)] * owners,
            scratch_shapes=[
                pltpu.VMEM((2, tall, 2 * LANES), jnp.bfloat16),
                pltpu.VMEM((fans, tall, 2 * LANES), jnp.bfloat16),
                pltpu.VMEM((blocks, rows, LANES), jnp.bfloat16),
                pltpu.SemaphoreType.DMA((blocks,)),
            ],
        ),
        out_shape=[sent] * owners,
        cost_estimate=pass_cost(rows, tall, blocks, fans, 2 * blocks * rows * LANES * 2),
        compiler_params=PARAMS,
        name="first_pass",
    )(keys, traces, *edges, mats, times, after)


def second_kernel(blocks, at, has_past, has_out, *refs):
    refs = list(refs)
    take = lambda: refs.pop(0)
    past = [take() for _ in range(3)] if has_past else None
    now = [take() for _ in range(3)]
    mats_ref, times_ref, _ = take(), take(), take()
    if has_out:
        take()
    out_ref, token_ref, window, fans_ref, done, sem = refs
    token_ref[...] = jnp.zeros_like(token_ref)
    step = pl.program_id(0)
    tall, rows = window.shape[1], done.shape[1]
    lead = REACH if has_past else REACH // 2
    held = now[0].shape[1]
    if has_past:
        old = merge_edges(past[1][...], past[2][...], blocks)
    merged = merge_edges(now[1][...], now[2][...], blocks)
    for half in range(2):
        if has_past:
            window[half, :lead, :LANES] = past[0][half]
            window[half, :lead, LANES:] = old
        else:
            window[half, :lead, :] = jnp.zeros((lead, 2 * LANES), jnp.bfloat16)
        window[half, lead : lead + held, :LANES] = now[0][half]
        window[half, lead : lead + held, LANES:] = merged
        if tall > lead + held:
            window[half, lead + held :, :] = jnp.zeros(
                (tall - lead - held, 2 * LANES), jnp.bfloat16
            )

    def give(start, values):
        for half in range(2):
            done[2 * step + half, pl.ds(start, values.shape[0]), :] = values[
                :, half * LANES : (half + 1) * LANES
            ]

    filter_window(window, fans_ref, mats_ref, times_ref, rows, give)

    def copy(block):
        return pltpu.make_async_copy(
            done.at[block], out_ref.at[block, pl.ds(at, rows), :], sem.at[block]
        )

    for half in range(2):
        copy(2 * step + half).start()

    @pl.when(step == pl.num_programs(0) - 1)
    def _():
        for block in range(blocks):
            copy(block).wait()


def second_pass(blocks, samples, past, now, mats, times, after, out, at, rows):
    fans = 2 * mats.shape[1]
    tall = window_rows(rows)
    specs, operands = [], []
    for group, last in ((past, True), (now, False)):
        if group is None:
            continue
        arrived, low, high = group
        size = REACH if last else arrived.shape[1]
        tail = arrived.shape[1] // size - 1
        specs.append(
            pl.BlockSpec((2, size, LANES), functools.partial(lambda t, i: (i, t, 0), tail))
        )
        operands.append(arrived)
        for edge in (low, high):
            specs.append(pl.BlockSpec((size, LANES), functools.partial(lambda t, i: (t, 0), tail)))
            operands.append(edge)
    specs += [
        pl.BlockSpec((2,) + mats.shape[1:], lambda i: (i, 0, 0, 0)),
        pl.BlockSpec(times.shape, lambda i: (0, 0)),
        pl.BlockSpec(memory_space=pl.ANY),
    ]
    operands += [mats, times, after]
    aliases = {}
    if out is not None:
        specs.append(pl.BlockSpec(memory_space=pl.ANY))
        operands.append(out)
        aliases = {len(operands) - 1: 0}
    return pl.pallas_call(
        functools.partial(second_kernel, blocks, at, past is not None, out is not None),
        grid=(blocks // 2,),
        in_specs=specs,
        out_specs=[
            pl.BlockSpec(memory_space=pl.ANY),
            pl.BlockSpec((8, LANES), lambda i: (0, 0)),
        ],
        scratch_shapes=[
            pltpu.VMEM((2, tall, 2 * LANES), jnp.bfloat16),
            pltpu.VMEM((fans, tall, 2 * LANES), jnp.bfloat16),
            pltpu.VMEM((blocks, rows, LANES), jnp.float32),
            pltpu.SemaphoreType.DMA((blocks,)),
        ],
        out_shape=[
            jax.ShapeDtypeStruct((blocks, samples, LANES), jnp.float32),
            jax.ShapeDtypeStruct((8, LANES), jnp.float32),
        ],
        input_output_aliases=aliases,
        cost_estimate=pass_cost(rows, tall, blocks, fans, 3 * blocks * rows * LANES * 2),
        compiler_params=PARAMS,
        name="second_pass",
    )(*operands)


def per_device(
    traces, first_trace_taps, first_time_taps, second_trace_taps, second_time_taps, dest_row
):
    blocks, samples, _ = traces.shape
    owners = lax.axis_size("rcv")
    me = lax.axis_index("rcv")
    slot_cap = blocks // 2

    target = dest_row[:, 0]
    ids = jnp.arange(blocks, dtype=jnp.int32)

    def ranks(owner):
        return jnp.sum(
            (
                (ids[:, None] > ids[None, :]) & (owner[..., :, None] == owner[..., None, :])
            ).astype(jnp.int32),
            axis=-1,
        )

    def send(values, offset):
        pairs = [(i, (i + offset) % owners) for i in range(owners)]
        return lax.ppermute(values, "rcv", pairs) if offset else values

    owner = target // blocks
    keys = (owner - me + owners) % owners * slot_cap + ranks(owner)

    bounds = chunk_bounds(samples)
    count = len(bounds) - 1
    near = min(samples, bounds[1] + REACH // 2)
    far = bounds[1] - REACH // 2
    edges = swap_edges(first_edges(traces, 0, near))
    mats, times = weights(first_trace_taps, first_time_taps, traces, blocks)

    column = jnp.stack([send(target, offset) for offset in range(owners)])
    place = jnp.arange(owners, dtype=jnp.int32)[:, None] * slot_cap + ranks(column // blocks)
    mine = column[None] == (me * blocks + ids)[:, None, None]
    slots = jnp.sum(jnp.where(mine, place[None], 0), axis=(1, 2))

    def first(step, edges, edges_at, after):
        return first_pass(
            keys, owners, traces, edges, edges_at, mats, times, after,
            bounds[step], bounds[step + 1],
        )

    def exchange(sent, before):
        arrived = []
        for offset, part in enumerate(sent):
            if offset and before is not None:
                part, before[offset] = lax.optimization_barrier((part, before[offset]))
            arrived.append(send(part, offset))
        return arrived

    sent = [first(0, edges, 0, mats)]
    arrived = [exchange(sent[0], None)]
    edges = swap_edges(first_edges(traces, far, samples))
    second_mats, second_times = weights(
        second_trace_taps, second_time_taps, sent[0][0], blocks
    )
    if count > 1:
        sent.append(first(1, edges, far, sent[0][0]))

    out, past, token = None, None, None
    for step in range(count):
        if step + 1 < count:
            arrived.append(exchange(sent[step + 1], arrived[step]))
        after = token if step else sent[-1][0]
        gathered, rims = second_edges(slots, arrived[step], after, blocks)
        now = (gathered, *swap_edges(rims))
        if step + 2 < count:
            sent.append(first(step + 2, edges, far, rims))
        at = max(0, bounds[step] - REACH // 2)
        stop = bounds[step + 1] - REACH // 2 if step + 1 < count else samples
        out, token = second_pass(
            blocks, samples, past, now, second_mats, second_times, sent[-1][0], out, at, stop - at
        )
        past = now
    return out


def solution(mesh):
    in_specs = (P("rcv", None, "shot"), P(), P(), P(), P(), P("rcv", "shot"))
    out_specs = P("rcv", None, "shot")
    return jax.shard_map(
        per_device, mesh=mesh, in_specs=in_specs, out_specs=out_specs, check_vma=False
    )
```

```python
import functools

import jax
import jax.numpy as jnp
from jax import lax
from jax.experimental import pallas as pl
from jax.experimental.pallas import tpu as pltpu
from jax.sharding import PartitionSpec as P

LANES = 128
EDGE = 8
SPAN = 256
REACH = 64
WIDE = SPAN - REACH
FOLD = 4
PARAMS = pltpu.CompilerParams(vmem_limit_bytes=16 * 2**20)
NO_COST = pl.CostEstimate(flops=1, bytes_accessed=1, transcendentals=0)
VMEM = pl.BlockSpec(memory_space=pltpu.VMEM)
SMEM = pl.BlockSpec(memory_space=pltpu.SMEM)
ANY = pl.BlockSpec(memory_space=pl.ANY)
HBM = pl.BlockSpec(memory_space=pltpu.HBM)
CHUNKS = (384, 576, 576)


def chunk_bounds(samples):
    bounds = [0]
    for size in CHUNKS:
        if bounds[-1] + size + REACH <= samples:
            bounds.append(bounds[-1] + size)
    bounds.append(samples)
    return bounds


def segment_plan(rows):
    count = -(-rows // WIDE)
    width = min(WIDE, -(-rows // (16 * count)) * 16)
    return count, width


def window_rows(rows):
    return rows - segment_plan(rows)[1] + SPAN


def folded_rows(rows):
    return -(-rows // (16 * FOLD)) * 16


def weights_kernel(even_ref, trace_ref, time_ref, *refs):
    mats_ref, times_ref = refs[-2:]
    fans = trace_ref.shape[0]
    blocks = mats_ref.shape[0]
    even = even_ref[0] == 1
    for fan in range(fans):
        row = jnp.broadcast_to(trace_ref[fan : fan + 1, :], (LANES, SPAN))
        own = pltpu.roll(row, 0, 1, stride=1, stride_axis=0)[:, :LANES]
        left = pltpu.roll(row[:EDGE], SPAN - EDGE, 1, stride=1, stride_axis=0)[:, :LANES]
        right = pltpu.roll(row[:EDGE], LANES, 1, stride=1, stride_axis=0)[:, :LANES]
        pieces = (jnp.where(even, right, left), jnp.where(even, left, right))
        pair, half = fan // 2, fan % 2
        cols = slice(half * LANES, (half + 1) * LANES)
        for block in range(blocks):
            before, after = EDGE * block, EDGE * (blocks - 1 - block)
            parts = []
            for piece in pieces:
                if before:
                    parts.append(jnp.zeros((before, LANES), jnp.float32))
                parts.append(piece)
                if after:
                    parts.append(jnp.zeros((after, LANES), jnp.float32))
            parts.append(jnp.zeros((LANES - 2 * EDGE * blocks, LANES), jnp.float32))
            mats_ref[block, pair, :LANES, cols] = own.astype(jnp.bfloat16)
            mats_ref[block, pair, LANES:, cols] = jnp.concatenate(parts, axis=0).astype(
                jnp.bfloat16
            )
        taps = jnp.broadcast_to(time_ref[fan : fan + 1, :], (WIDE, SPAN))
        times_ref[:, fan * SPAN : (fan + 1) * SPAN] = pltpu.roll(
            taps, 0, 1, stride=1, stride_axis=0
        ).astype(jnp.bfloat16)


def weights(even, trace_taps, time_taps, blocks, *after):
    fans, width = trace_taps.shape
    turned = jnp.pad(trace_taps[:, ::-1].astype(jnp.float32), ((0, 0), (0, SPAN - width)))
    turned = jnp.roll(turned, width // 2 - width + 1, axis=1)
    late = jnp.pad(time_taps.astype(jnp.float32), ((0, 0), (0, SPAN - time_taps.shape[1])))
    return pl.pallas_call(
        weights_kernel,
        in_specs=[SMEM, VMEM, VMEM] + [ANY] * len(after),
        out_specs=[VMEM, VMEM],
        out_shape=(
            jax.ShapeDtypeStruct((blocks, fans // 2, 2 * LANES, 2 * LANES), jnp.bfloat16),
            jax.ShapeDtypeStruct((WIDE, fans * SPAN), jnp.bfloat16),
        ),
        cost_estimate=NO_COST,
        compiler_params=PARAMS,
        name="weights",
    )(even, turned, late, *after)


def edge_picks(even, blocks):
    trace = lax.broadcasted_iota(jnp.int32, (2 * LANES, 2 * LANES), 0)
    lane = lax.broadcasted_iota(jnp.int32, (2 * LANES, 2 * LANES), 1)
    last = jnp.where(even, 1, 0)
    begin = jnp.where(lane < LANES, last, 1 - last) * (LANES - EDGE)
    lane = lane % LANES
    picks = []
    for pair in range(blocks // 2):
        at = lane - EDGE * (2 * pair + trace // LANES)
        pick = (at >= 0) & (at < EDGE) & (trace % LANES == at + begin)
        picks.append(jnp.where(pick, 1.0, 0.0).astype(jnp.bfloat16))
    return picks


def pick_part(picks, tiles_ref, start, stop):
    found = None
    for pair, pick in enumerate(picks):
        both = jnp.concatenate(
            [tiles_ref[2 * pair, start:stop, :], tiles_ref[2 * pair + 1, start:stop, :]], axis=1
        )
        one = jnp.dot(both, pick, preferred_element_type=jnp.float32)
        found = one if found is None else found + one
    return found


def pack_edges(picks, tiles_ref, packed_refs, ready):
    blocks, rows = tiles_ref.shape[:2]
    fold = folded_rows(rows)
    totals = [None, None]
    for part in range(FOLD):
        start, stop = part * fold, min(rows, (part + 1) * fold)
        ready(part)
        found = pick_part(picks, tiles_ref, start, stop)
        if stop - start < fold:
            found = jnp.concatenate(
                [found, jnp.zeros((fold - stop + start, 2 * LANES), jnp.float32)], axis=0
            )
        for way in range(2):
            piece = found[:, way * LANES : (way + 1) * LANES]
            if part:
                piece = pltpu.roll(piece, part * EDGE * blocks, 1)
            totals[way] = piece if totals[way] is None else totals[way] + piece
    for way in range(2):
        packed_refs[way][...] = totals[way].astype(jnp.bfloat16)


def unpack_edges(packed_refs, rows, blocks, start, stop, give):
    fold, width = packed_refs[0].shape[0], EDGE * blocks
    while start < stop:
        part = start // fold
        until = min(stop, (part + 1) * fold)
        pieces = []
        for way in range(2):
            piece = packed_refs[way][start - part * fold : until - part * fold, :]
            shift = (way - part) * width % LANES
            piece = piece.astype(jnp.float32)
            pieces.append(pltpu.roll(piece, shift, 1) if shift else piece)
        lane = lax.broadcasted_iota(jnp.int32, pieces[0].shape, 1)
        give(start, jnp.where(lane < width, pieces[0], pieces[1]).astype(jnp.bfloat16))
        start = until


def first_edges_kernel(even_ref, x_ref, out_a, out_b, picks_ref, held, sem):
    blocks, rows = held.shape[:2]
    fold = folded_rows(rows)

    def copy(part):
        span = pl.ds(part * fold, min(rows, (part + 1) * fold) - part * fold)
        return pltpu.make_async_copy(x_ref.at[:, span, :], held.at[:, span, :], sem.at[part])

    for part in range(FOLD):
        copy(part).start()
    picks = edge_picks(even_ref[0] == 1, blocks)
    for pair, pick in enumerate(picks):
        picks_ref[pair] = pick
    pack_edges(picks, held, (out_a, out_b), lambda part: copy(part).wait())


def first_edges(even, traces):
    blocks = traces.shape[0]
    packed = jax.ShapeDtypeStruct((folded_rows(traces.shape[1]), LANES), jnp.bfloat16)
    return pl.pallas_call(
        first_edges_kernel,
        in_specs=[SMEM, HBM],
        out_specs=[VMEM] * 4,
        out_shape=[
            packed,
            packed,
            jax.ShapeDtypeStruct((blocks // 2, 2 * LANES, 2 * LANES), jnp.bfloat16),
            jax.ShapeDtypeStruct(traces.shape, jnp.bfloat16),
        ],
        scratch_shapes=[pltpu.SemaphoreType.DMA((FOLD,))],
        cost_estimate=NO_COST,
        compiler_params=pltpu.CompilerParams(vmem_limit_bytes=50 * 2**20),
        name="first_edges",
    )(even, traces)


def second_edges_kernel(slot_ref, picks_ref, *refs):
    parts, (_, sorted_ref, out_a, out_b, sem) = refs[:-5], refs[-5:]
    blocks, slot_cap = sorted_ref.shape[0], parts[0].shape[0]
    for block in range(blocks):
        slot = slot_ref[block]
        for offset, part in enumerate(parts):

            @pl.when(slot // slot_cap == offset)
            def _():
                pltpu.make_async_copy(
                    part.at[slot % slot_cap], sorted_ref.at[block], sem.at[block]
                ).start()

    for block in range(blocks):
        pltpu.make_async_copy(parts[0].at[0], sorted_ref.at[block], sem.at[block]).wait()
    picks = [picks_ref[pair] for pair in range(blocks // 2)]
    pack_edges(picks, sorted_ref, (out_a, out_b), lambda part: None)


def second_edges(slots, picks, arrived, after, blocks):
    rows = arrived[0].shape[1]
    packed = jax.ShapeDtypeStruct((folded_rows(rows), LANES), jnp.bfloat16)
    return pl.pallas_call(
        second_edges_kernel,
        in_specs=[SMEM, VMEM] + [ANY] * (len(arrived) + 1),
        out_specs=[VMEM] * 3,
        scratch_shapes=[pltpu.SemaphoreType.DMA((blocks,))],
        out_shape=[jax.ShapeDtypeStruct((blocks, rows, LANES), jnp.bfloat16), packed, packed],
        cost_estimate=NO_COST,
        compiler_params=PARAMS,
        name="second_edges",
    )(slots, picks, *arrived, after)


def swap_edges(packed):
    count = lax.axis_size("shot")
    got = []
    for first, edges in enumerate(packed):
        pairs = []
        for low in range(first, count - 1, 2):
            pairs += [(low, low + 1), (low + 1, low)]
        got.append(lax.ppermute(edges, "shot", pairs))
    return got


def filter_window(pieces, merged, fans_ref, mats_ref, times_ref, rows, give):
    fan_pairs = mats_ref.shape[1]
    blocks = mats_ref.shape[0]
    tall = fans_ref.shape[1]
    count, width = segment_plan(rows)
    covered = 0
    for at, size, _ in list(pieces) + [(tall, 0, None)]:
        if at > covered:
            fans_ref[:, covered:at, :] = jnp.zeros(
                (fans_ref.shape[0], at - covered, fans_ref.shape[2]), jnp.bfloat16
            )
        covered = at + size
    def do_pair(pair, carry):
        for half in range(2):
            block = 2 * pair + half
            cols = slice(half * LANES, (half + 1) * LANES)
            for at, size, load in pieces:
                lhs = jnp.concatenate([load(block), merged[at : at + size, :]], axis=1)
                for fan_pair in range(fan_pairs):
                    both = jnp.dot(
                        lhs, mats_ref[block, fan_pair], preferred_element_type=jnp.float32
                    ).astype(jnp.bfloat16)
                    fans_ref[2 * fan_pair, at : at + size, cols] = both[:, :LANES]
                    fans_ref[2 * fan_pair + 1, at : at + size, cols] = both[:, LANES:]
        for step in range(count):
            start = min(step * width, rows - width)
            total = None
            for fan in range(2 * fan_pairs):
                part = jnp.dot(
                    times_ref[:width, fan * SPAN : (fan + 1) * SPAN],
                    fans_ref[fan, start : start + SPAN, :],
                    preferred_element_type=jnp.float32,
                )
                total = part if total is None else total + part
            give(pair, start, total)
        return carry

    lax.fori_loop(0, blocks // 2, do_pair, 0)


def first_kernel(start, stop, owners, key_ref, x_ref, edge_a, edge_b, mats_ref, times_ref, *refs):
    outs = refs[-4 - owners : -4]
    merged, fans_ref, done, sem = refs[-4:]
    blocks, rows = done.shape[:2]
    samples = x_ref.shape[1]
    slot_cap = outs[0].shape[0]
    window = start - REACH // 2
    begin, end = max(0, window), min(samples, stop + REACH // 2)

    def put(row, values):
        merged[row - window : row - window + values.shape[0], :] = values

    unpack_edges((edge_a, edge_b), samples, blocks, begin, end, put)

    def give(pair, at, values):
        values = values.astype(jnp.bfloat16)
        for half in range(2):
            done[2 * pair + half, at : at + values.shape[0], :] = values[
                :, half * LANES : (half + 1) * LANES
            ]
        if at + values.shape[0] == rows:
            for half in range(2):
                block = 2 * pair + half
                key = key_ref[block]
                for offset, out_ref in enumerate(outs):

                    @pl.when(key // slot_cap == offset)
                    def _():
                        pltpu.make_async_copy(
                            done.at[block], out_ref.at[key % slot_cap], sem.at[block]
                        ).start()

    pieces = [(begin - window, end - begin, lambda block: x_ref[block, begin:end, :])]
    filter_window(pieces, merged, fans_ref, mats_ref, times_ref, rows, give)
    for block in range(blocks):
        pltpu.make_async_copy(done.at[block], outs[0].at[0], sem.at[block]).wait()


def first_pass(keys, owners, traces, edges, mats, times, after, start, stop):
    blocks = traces.shape[0]
    fans = 2 * mats.shape[1]
    rows = stop - start
    tall = window_rows(rows)
    sent = jax.ShapeDtypeStruct((blocks // 2, rows, LANES), jnp.bfloat16)
    return pl.pallas_call(
        functools.partial(first_kernel, start, stop, owners),
        in_specs=[SMEM] + [VMEM] * 5 + [ANY] * len(after),
        out_specs=[ANY] * owners,
        scratch_shapes=[
            pltpu.VMEM((tall, LANES), jnp.bfloat16),
            pltpu.VMEM((fans, tall, 2 * LANES), jnp.bfloat16),
            pltpu.VMEM((blocks, rows, LANES), jnp.bfloat16),
            pltpu.SemaphoreType.DMA((blocks,)),
        ],
        out_shape=[sent] * owners,
        cost_estimate=NO_COST,
        compiler_params=PARAMS,
        name="first_pass",
    )(keys, traces, *edges, mats, times, *after)


def second_kernel(at, has_past, *refs):
    refs = list(refs)
    take = lambda: refs.pop(0)
    past = [take() for _ in range(3)] if has_past else None
    now = [take() for _ in range(3)]
    mats_ref, times_ref, _ = take(), take(), take()
    if has_past:
        take()
    out_ref, token_ref, merged, fans_ref, done, sem = refs
    token_ref[...] = jnp.zeros_like(token_ref)
    blocks, rows = done.shape[:2]
    lead = REACH if has_past else REACH // 2
    pieces = []

    def put(origin):
        def store(row, values):
            merged[row - origin : row - origin + values.shape[0], :] = values

        return store

    if has_past:
        held = past[0].shape[1]
        unpack_edges(past[1:], held, blocks, held - REACH, held, put(held - REACH))
        pieces.append((0, REACH, lambda block: past[0][block, held - REACH :, :]))
    size = now[0].shape[1]
    unpack_edges(now[1:], size, blocks, 0, size, put(-lead))
    pieces.append((lead, size, lambda block: now[0][block]))

    def copy(block):
        return pltpu.make_async_copy(
            done.at[block], out_ref.at[block, pl.ds(at, rows), :], sem.at[block]
        )

    def give(pair, start, values):
        for half in range(2):
            done[2 * pair + half, start : start + values.shape[0], :] = values[
                :, half * LANES : (half + 1) * LANES
            ]
        if start + values.shape[0] == rows:
            for half in range(2):
                copy(2 * pair + half).start()

    filter_window(pieces, merged, fans_ref, mats_ref, times_ref, rows, give)
    for block in range(blocks):
        copy(block).wait()


def second_pass(blocks, samples, past, now, mats, times, after, out, at, rows):
    fans = 2 * mats.shape[1]
    tall = window_rows(rows)
    operands = [*(past or ()), *now, mats, times, after]
    specs = [VMEM] * (len(operands) - 1) + [ANY]
    aliases = {}
    if out is not None:
        specs.append(ANY)
        operands.append(out)
        aliases = {len(operands) - 1: 0}
    return pl.pallas_call(
        functools.partial(second_kernel, at, past is not None),
        in_specs=specs,
        out_specs=[ANY, VMEM],
        scratch_shapes=[
            pltpu.VMEM((tall, LANES), jnp.bfloat16),
            pltpu.VMEM((fans, tall, 2 * LANES), jnp.bfloat16),
            pltpu.VMEM((blocks, rows, LANES), jnp.float32),
            pltpu.SemaphoreType.DMA((blocks,)),
        ],
        out_shape=[
            jax.ShapeDtypeStruct((blocks, samples, LANES), jnp.float32),
            jax.ShapeDtypeStruct((8, LANES), jnp.float32),
        ],
        input_output_aliases=aliases,
        cost_estimate=NO_COST,
        compiler_params=PARAMS,
        name="second_pass",
    )(*operands)


def per_device(
    traces, first_trace_taps, first_time_taps, second_trace_taps, second_time_taps, dest_row
):
    blocks, samples, _ = traces.shape
    owners = lax.axis_size("rcv")
    me = lax.axis_index("rcv")
    slot_cap = blocks // 2
    even = (1 - lax.axis_index("shot") % 2).astype(jnp.int32).reshape(1)

    target = dest_row[:, 0]
    ids = jnp.arange(blocks, dtype=jnp.int32)

    def ranks(owner):
        return jnp.sum(
            (
                (ids[:, None] > ids[None, :]) & (owner[..., :, None] == owner[..., None, :])
            ).astype(jnp.int32),
            axis=-1,
        )

    def send(values, offset):
        pairs = [(i, (i + offset) % owners) for i in range(owners)]
        return lax.ppermute(values, "rcv", pairs) if offset else values

    owner = target // blocks
    keys = (owner - me + owners) % owners * slot_cap + ranks(owner)

    bounds = chunk_bounds(samples)
    count = len(bounds) - 1
    *packed, picks, traces = first_edges(even, traces)
    edges = swap_edges(packed)
    late_target, _ = lax.optimization_barrier((target, packed[0]))
    column = jnp.stack([send(late_target, offset) for offset in range(owners)])
    place = jnp.arange(owners, dtype=jnp.int32)[:, None] * slot_cap + ranks(column // blocks)
    mine = column[None] == (me * blocks + ids)[:, None, None]
    slots = jnp.sum(jnp.where(mine, place[None], 0), axis=(1, 2))
    mats, times = weights(even, first_trace_taps, first_time_taps, blocks)

    def exchange(sent, before, token):
        arrived = []
        for offset, part in enumerate(sent):
            if offset and before is not None:
                part, before[offset] = lax.optimization_barrier((part, before[offset]))
            if offset and token is not None:
                part, _ = lax.optimization_barrier((part, token))
            arrived.append(send(part, offset))
        return arrived

    sent, after = [], [slots]
    for step in range(count):
        sent.append(
            first_pass(
                keys, owners, traces, edges, mats, times, after, bounds[step], bounds[step + 1]
            )
        )
        after = [sent[-1][0]]
    arrived = [exchange(sent[0], None, None)]

    mats, times = weights(even, second_trace_taps, second_time_taps, blocks, sent[0][0])
    out, past, token = None, None, None
    for step in range(count):
        if step + 1 < count:
            arrived.append(exchange(sent[step + 1], arrived[step], token))
        after = token if step else sent[min(2, count - 1)][0]
        gathered, *packed = second_edges(slots, picks, arrived[step], after, blocks)
        now = (gathered, *swap_edges(packed))
        at = max(0, bounds[step] - REACH // 2)
        stop = bounds[step + 1] - REACH // 2 if step + 1 < count else samples
        out, token = second_pass(
            blocks, samples, past, now, mats, times, sent[min(step + 3, count - 1)][0], out,
            at, stop - at,
        )
        past = now
    return out


def solution(mesh):
    in_specs = (P("rcv", None, "shot"), P(), P(), P(), P(), P("rcv", "shot"))
    out_specs = P("rcv", None, "shot")
    return jax.shard_map(
        per_device, mesh=mesh, in_specs=in_specs, out_specs=out_specs, check_vma=False
    )
```

```python
import functools

import jax
import jax.numpy as jnp
from jax import lax
from jax.experimental import pallas as pl
from jax.experimental.pallas import tpu as pltpu
from jax.sharding import PartitionSpec as P

LANES = 128
EDGE = 8
SPAN = 256
REACH = 64
WIDE = SPAN - REACH
FOLD = 4
PARAMS = pltpu.CompilerParams(vmem_limit_bytes=16 * 2**20)
NO_COST = pl.CostEstimate(flops=1, bytes_accessed=1, transcendentals=0)
VMEM = pl.BlockSpec(memory_space=pltpu.VMEM)
SMEM = pl.BlockSpec(memory_space=pltpu.SMEM)
ANY = pl.BlockSpec(memory_space=pl.ANY)
HBM = pl.BlockSpec(memory_space=pltpu.HBM)
CHUNKS = (384, 576, 576)


def chunk_bounds(samples):
    bounds = [0]
    for size in CHUNKS:
        if bounds[-1] + size + REACH <= samples:
            bounds.append(bounds[-1] + size)
    bounds.append(samples)
    return bounds


def segment_plan(rows):
    count = -(-rows // WIDE)
    width = min(WIDE, -(-rows // (16 * count)) * 16)
    return count, width


def window_rows(rows):
    return rows - segment_plan(rows)[1] + SPAN


def folded_rows(rows):
    return -(-rows // (16 * FOLD)) * 16


def place_taps(taps_ref, origin, step):
    width = taps_ref.shape[1]
    tap = lax.broadcasted_iota(jnp.int32, (width, SPAN), 0)
    at = lax.broadcasted_iota(jnp.int32, (width, SPAN), 1)
    spread = jnp.where(at == (origin + step * tap + SPAN) % SPAN, 1.0, 0.0).astype(jnp.bfloat16)
    return jnp.dot(taps_ref[...], spread, preferred_element_type=jnp.float32)


def fill_weights(even, trace_ref, time_ref, mats_ref, times_ref):
    fans = trace_ref.shape[0]
    blocks = mats_ref.shape[0]
    trace_rows = place_taps(trace_ref, trace_ref.shape[1] // 2, -1)
    time_rows = place_taps(time_ref, 0, 1)
    for fan in range(fans):
        row = jnp.broadcast_to(trace_rows[fan : fan + 1, :], (LANES, SPAN))
        own = pltpu.roll(row, 0, 1, stride=1, stride_axis=0)[:, :LANES]
        left = pltpu.roll(row[:EDGE], SPAN - EDGE, 1, stride=1, stride_axis=0)[:, :LANES]
        right = pltpu.roll(row[:EDGE], LANES, 1, stride=1, stride_axis=0)[:, :LANES]
        pieces = (jnp.where(even, right, left), jnp.where(even, left, right))
        pair, half = fan // 2, fan % 2
        cols = slice(half * LANES, (half + 1) * LANES)
        for block in range(blocks):
            before, after = EDGE * block, EDGE * (blocks - 1 - block)
            parts = []
            for piece in pieces:
                if before:
                    parts.append(jnp.zeros((before, LANES), jnp.float32))
                parts.append(piece)
                if after:
                    parts.append(jnp.zeros((after, LANES), jnp.float32))
            parts.append(jnp.zeros((LANES - 2 * EDGE * blocks, LANES), jnp.float32))
            mats_ref[block, pair, :LANES, cols] = own.astype(jnp.bfloat16)
            mats_ref[block, pair, LANES:, cols] = jnp.concatenate(parts, axis=0).astype(
                jnp.bfloat16
            )
        taps = jnp.broadcast_to(time_rows[fan : fan + 1, :], (WIDE, SPAN))
        times_ref[:, fan * SPAN : (fan + 1) * SPAN] = pltpu.roll(
            taps, 0, 1, stride=1, stride_axis=0
        ).astype(jnp.bfloat16)


def weights_kernel(even_ref, trace_ref, time_ref, mats_ref, times_ref):
    fill_weights(even_ref[0] == 1, trace_ref, time_ref, mats_ref, times_ref)


def ranks(targets, blocks):
    owners = [lax.div(target, blocks) for target in targets]
    order = []
    for block, owner in enumerate(owners):
        rank = jnp.int32(0)
        for other in owners[:block]:
            rank = rank + jnp.where(other == owner, 1, 0)
        order.append(rank)
    return owners, order


def late_kernel(even_ref, me_ref, trace_ref, time_ref, *refs):
    mats_ref, times_ref, slots_ref = refs[-3:]
    columns = refs[:-4]
    blocks, count, me = mats_ref.shape[0], len(columns), me_ref[0]
    fill_weights(even_ref[0] == 1, trace_ref, time_ref, mats_ref, times_ref)
    slot_cap = blocks // 2
    near, far = [jnp.int32(0)] * blocks, [jnp.int32(0)] * blocks
    for offset, column in enumerate(columns):
        targets = [column[block] for block in range(blocks)]
        order = ranks(targets, blocks)[1]
        source = lax.rem(me - offset + count, count)
        for target, rank in zip(targets, order):
            for block in range(blocks):
                found = target == me * blocks + block
                near[block] = jnp.where(found, offset * slot_cap + rank, near[block])
                far[block] = jnp.where(found, source * slot_cap + rank, far[block])
    for block in range(blocks):
        slots_ref[block] = near[block]
        slots_ref[blocks + block] = far[block]


def weight_shapes(blocks, fans):
    return [
        jax.ShapeDtypeStruct((blocks, fans // 2, 2 * LANES, 2 * LANES), jnp.bfloat16),
        jax.ShapeDtypeStruct((WIDE, fans * SPAN), jnp.bfloat16),
    ]


def weights(even, trace_taps, time_taps, blocks):
    return pl.pallas_call(
        weights_kernel,
        in_specs=[SMEM, VMEM, VMEM],
        out_specs=[VMEM, VMEM],
        out_shape=weight_shapes(blocks, trace_taps.shape[0]),
        cost_estimate=NO_COST,
        compiler_params=PARAMS,
        name="weights",
    )(even, trace_taps, time_taps)


def late_weights(even, me, trace_taps, time_taps, columns, after, blocks):
    return pl.pallas_call(
        late_kernel,
        in_specs=[SMEM, SMEM, VMEM, VMEM] + [SMEM] * len(columns) + [ANY],
        out_specs=[VMEM, VMEM, SMEM],
        out_shape=weight_shapes(blocks, trace_taps.shape[0])
        + [jax.ShapeDtypeStruct((2 * blocks,), jnp.int32)],
        cost_estimate=NO_COST,
        compiler_params=PARAMS,
        name="late_weights",
    )(even, me, trace_taps, time_taps, *columns, after)


def edge_picks(even, blocks):
    trace = lax.broadcasted_iota(jnp.int32, (2 * LANES, 2 * LANES), 0)
    lane = lax.broadcasted_iota(jnp.int32, (2 * LANES, 2 * LANES), 1)
    last = jnp.where(even, 1, 0)
    begin = jnp.where(lane < LANES, last, 1 - last) * (LANES - EDGE)
    lane = lane % LANES
    picks = []
    for pair in range(blocks // 2):
        at = lane - EDGE * (2 * pair + trace // LANES)
        pick = (at >= 0) & (at < EDGE) & (trace % LANES == at + begin)
        picks.append(jnp.where(pick, 1.0, 0.0).astype(jnp.bfloat16))
    return picks


def pick_part(picks, tiles_ref, start, stop):
    found = None
    for pair, pick in enumerate(picks):
        both = jnp.concatenate(
            [tiles_ref[2 * pair, start:stop, :], tiles_ref[2 * pair + 1, start:stop, :]], axis=1
        )
        one = jnp.dot(both, pick, preferred_element_type=jnp.float32)
        found = one if found is None else found + one
    return found


def pack_edges(picks, tiles_ref, packed_refs):
    blocks, rows = tiles_ref.shape[:2]
    fold = folded_rows(rows)
    totals = [None, None]
    for part in range(FOLD):
        start, stop = part * fold, min(rows, (part + 1) * fold)
        found = pick_part(picks, tiles_ref, start, stop)
        if stop - start < fold:
            found = jnp.concatenate(
                [found, jnp.zeros((fold - stop + start, 2 * LANES), jnp.float32)], axis=0
            )
        for way in range(2):
            piece = found[:, way * LANES : (way + 1) * LANES]
            if part:
                piece = pltpu.roll(piece, part * EDGE * blocks, 1)
            totals[way] = piece if totals[way] is None else totals[way] + piece
    for way in range(2):
        packed_refs[way][...] = totals[way].astype(jnp.bfloat16)


def unpack_edges(packed_refs, rows, blocks, start, stop, give):
    fold, width = packed_refs[0].shape[0], EDGE * blocks
    while start < stop:
        part = start // fold
        until = min(stop, (part + 1) * fold)
        pieces = []
        for way in range(2):
            piece = packed_refs[way][start - part * fold : until - part * fold, :]
            shift = (way - part) * width % LANES
            piece = piece.astype(jnp.float32)
            pieces.append(pltpu.roll(piece, shift, 1) if shift else piece)
        lane = lax.broadcasted_iota(jnp.int32, pieces[0].shape, 1)
        give(start, jnp.where(lane < width, pieces[0], pieces[1]).astype(jnp.bfloat16))
        start = until


def first_edges_kernel(even_ref, x_ref, out_a, out_b, picks_ref):
    blocks = x_ref.shape[0]
    picks = edge_picks(even_ref[0] == 1, blocks)
    for pair, pick in enumerate(picks):
        picks_ref[pair] = pick
    pack_edges(picks, x_ref, (out_a, out_b))


def first_edges(even, traces):
    blocks = traces.shape[0]
    packed = jax.ShapeDtypeStruct((folded_rows(traces.shape[1]), LANES), jnp.bfloat16)
    return pl.pallas_call(
        first_edges_kernel,
        in_specs=[SMEM, VMEM],
        out_specs=[VMEM] * 3,
        out_shape=[
            packed,
            packed,
            jax.ShapeDtypeStruct((blocks // 2, 2 * LANES, 2 * LANES), jnp.bfloat16),
        ],
        cost_estimate=NO_COST,
        compiler_params=PARAMS,
        name="first_edges",
    )(even, traces)


def second_edges_kernel(base, slot_ref, picks_ref, *refs):
    parts, (_, sorted_ref, out_a, out_b, sem) = refs[:-5], refs[-5:]
    blocks, slot_cap = sorted_ref.shape[0], parts[0].shape[0]
    for block in range(blocks):
        slot = slot_ref[base + block]
        for offset, part in enumerate(parts):

            @pl.when(slot // slot_cap == offset)
            def _():
                pltpu.make_async_copy(
                    part.at[slot % slot_cap], sorted_ref.at[block], sem.at[block]
                ).start()

    for block in range(blocks):
        pltpu.make_async_copy(parts[0].at[0], sorted_ref.at[block], sem.at[block]).wait()
    picks = [picks_ref[pair] for pair in range(blocks // 2)]
    pack_edges(picks, sorted_ref, (out_a, out_b))


def second_edges(slots, picks, arrived, after, blocks):
    rows = arrived[0].shape[1]
    packed = jax.ShapeDtypeStruct((folded_rows(rows), LANES), jnp.bfloat16)
    return pl.pallas_call(
        functools.partial(second_edges_kernel, blocks if len(arrived) == 1 else 0),
        in_specs=[SMEM, VMEM] + [ANY] * (len(arrived) + 1),
        out_specs=[VMEM] * 3,
        scratch_shapes=[pltpu.SemaphoreType.DMA((blocks,))],
        out_shape=[jax.ShapeDtypeStruct((blocks, rows, LANES), jnp.bfloat16), packed, packed],
        cost_estimate=NO_COST,
        compiler_params=PARAMS,
        name="second_edges",
    )(slots, picks, *arrived, after)


def swap_edges(packed):
    count = lax.axis_size("shot")
    got = []
    for first, edges in enumerate(packed):
        pairs = []
        for low in range(first, count - 1, 2):
            pairs += [(low, low + 1), (low + 1, low)]
        got.append(lax.ppermute(edges, "shot", pairs))
    return got


def filter_window(pieces, merged, fans_ref, mats_ref, times_ref, rows, give, finish):
    fan_pairs = mats_ref.shape[1]
    blocks = mats_ref.shape[0]
    tall = fans_ref.shape[1]
    count, width = segment_plan(rows)
    covered = 0
    for at, size, _ in list(pieces) + [(tall, 0, None)]:
        if at > covered:
            fans_ref[:, covered:at, :] = jnp.zeros(
                (fans_ref.shape[0], at - covered, fans_ref.shape[2]), jnp.bfloat16
            )
        covered = at + size
    def do_pair(pair, carry):
        for half in range(2):
            block = 2 * pair + half
            cols = slice(half * LANES, (half + 1) * LANES)
            for at, size, load in pieces:
                lhs = jnp.concatenate([load(block), merged[at : at + size, :]], axis=1)
                for fan_pair in range(fan_pairs):
                    both = jnp.dot(
                        lhs, mats_ref[block, fan_pair], preferred_element_type=jnp.float32
                    ).astype(jnp.bfloat16)
                    fans_ref[2 * fan_pair, at : at + size, cols] = both[:, :LANES]
                    fans_ref[2 * fan_pair + 1, at : at + size, cols] = both[:, LANES:]
        for step in range(count):
            start = min(step * width, rows - width)
            total = None
            for fan in range(2 * fan_pairs):
                part = jnp.dot(
                    times_ref[:width, fan * SPAN : (fan + 1) * SPAN],
                    fans_ref[fan, start : start + SPAN, :],
                    preferred_element_type=jnp.float32,
                )
                total = part if total is None else total + part
            give(pair, start, total)
        finish(pair)
        return carry

    lax.fori_loop(0, blocks // 2, do_pair, 0)


def first_kernel(
    start, sizes, samples, owners, me_ref, target_ref, x_ref, edge_a, edge_b, mats_ref, times_ref,
    *refs
):
    outs, (merged, fans_ref, done, sem) = list(refs[-4 - sum(n for _, n in sizes) : -4]), refs[-4:]
    blocks, rows = done.shape[:2]
    window = start - REACH // 2
    begin, end = max(0, window), min(samples, start + rows + REACH // 2)
    targets, order = ranks([target_ref[block] for block in range(blocks)], blocks)
    groups, at = [], 0
    for size, number in sizes:
        groups.append((at, size, outs[:number]))
        outs = outs[number:]
        at += size

    def put(row, values):
        merged[row - window : row - window + values.shape[0], :] = values

    unpack_edges((edge_a, edge_b), samples, blocks, begin, end, put)

    def give(pair, at, values):
        values = values.astype(jnp.bfloat16)
        for half in range(2):
            done[2 * pair + half, at : at + values.shape[0], :] = values[
                :, half * LANES : (half + 1) * LANES
            ]

    def pick(values, pair, half):
        value = values[half]
        for other in range(1, blocks // 2):
            value = jnp.where(pair == other, values[2 * other + half], value)
        return value

    def finish(pair):
        for half in range(2):
            block = 2 * pair + half
            owner, rank = pick(targets, pair, half), pick(order, pair, half)
            away = lax.rem(owner - me_ref[0] + owners, owners)
            for group, (at, size, arrays) in enumerate(groups):
                part = done.at[block, pl.ds(at, size), :]
                if len(arrays) == 1:
                    slot = owner * (blocks // 2) + rank
                    pltpu.make_async_copy(part, arrays[0].at[slot], sem.at[group, block]).start()
                    continue
                for offset, out_ref in enumerate(arrays):

                    @pl.when(away == offset)
                    def _():
                        pltpu.make_async_copy(
                            part, out_ref.at[rank], sem.at[group, block]
                        ).start()

    pieces = [
        (begin - window, end - begin, lambda block: x_ref[block, begin:end, :])
    ]
    filter_window(pieces, merged, fans_ref, mats_ref, times_ref, rows, give, finish)
    for group, (at, size, arrays) in enumerate(groups):
        for block in range(blocks):
            pltpu.make_async_copy(
                done.at[block, pl.ds(at, size), :], arrays[0].at[0], sem.at[group, block]
            ).wait()


def first_pass(me, target, owners, traces, samples, edges, mats, times, after, start, sizes):
    blocks = traces.shape[0]
    fans = 2 * mats.shape[1]
    rows = sum(size for size, _ in sizes)
    tall = window_rows(rows)
    shapes = []
    for size, number in sizes:
        slots = owners * (blocks // 2) // number
        shapes += [jax.ShapeDtypeStruct((slots, size, LANES), jnp.bfloat16)] * number
    flat = pl.pallas_call(
        functools.partial(first_kernel, start, sizes, samples, owners),
        in_specs=[SMEM, SMEM] + [VMEM] * 5 + [ANY] * len(after),
        out_specs=[ANY] * len(shapes),
        scratch_shapes=[
            pltpu.VMEM((tall, LANES), jnp.bfloat16),
            pltpu.VMEM((fans, tall, 2 * LANES), jnp.bfloat16),
            pltpu.VMEM((blocks, rows, LANES), jnp.bfloat16),
            pltpu.SemaphoreType.DMA((len(sizes), blocks)),
        ],
        out_shape=shapes,
        cost_estimate=NO_COST,
        compiler_params=PARAMS,
        name="first_pass",
    )(me, target, traces, *edges, mats, times, *after)
    chunks = []
    for _, number in sizes:
        chunks.append(flat[:number])
        flat = flat[number:]
    return chunks


def second_kernel(at, has_past, *refs):
    refs = list(refs)
    take = lambda: refs.pop(0)
    past = [take() for _ in range(3)] if has_past else None
    now = [take() for _ in range(3)]
    mats_ref, times_ref, _ = take(), take(), take()
    if has_past:
        take()
    out_ref, token_ref, merged, fans_ref, done, sem = refs
    token_ref[...] = jnp.zeros_like(token_ref)
    blocks, rows = done.shape[:2]
    lead = REACH if has_past else REACH // 2
    pieces = []

    def put(origin):
        def store(row, values):
            merged[row - origin : row - origin + values.shape[0], :] = values

        return store

    if has_past:
        held = past[0].shape[1]
        unpack_edges(past[1:], held, blocks, held - REACH, held, put(held - REACH))
        pieces.append((0, REACH, lambda block: past[0][block, held - REACH :, :]))
    size = now[0].shape[1]
    unpack_edges(now[1:], size, blocks, 0, size, put(-lead))
    pieces.append((lead, size, lambda block: now[0][block]))

    def copy(block):
        return pltpu.make_async_copy(
            done.at[block], out_ref.at[block, pl.ds(at, rows), :], sem.at[block]
        )

    def give(pair, start, values):
        for half in range(2):
            done[2 * pair + half, start : start + values.shape[0], :] = values[
                :, half * LANES : (half + 1) * LANES
            ]

    def finish(pair):
        for half in range(2):
            copy(2 * pair + half).start()

    filter_window(pieces, merged, fans_ref, mats_ref, times_ref, rows, give, finish)
    for block in range(blocks):
        copy(block).wait()


def second_pass(blocks, samples, past, now, mats, times, after, out, at, rows):
    fans = 2 * mats.shape[1]
    tall = window_rows(rows)
    operands = [*(past or ()), *now, mats, times, after]
    specs = [VMEM] * (len(operands) - 1) + [ANY]
    aliases = {}
    if out is not None:
        specs.append(ANY)
        operands.append(out)
        aliases = {len(operands) - 1: 0}
    return pl.pallas_call(
        functools.partial(second_kernel, at, past is not None),
        in_specs=specs,
        out_specs=[ANY, VMEM],
        scratch_shapes=[
            pltpu.VMEM((tall, LANES), jnp.bfloat16),
            pltpu.VMEM((fans, tall, 2 * LANES), jnp.bfloat16),
            pltpu.VMEM((blocks, rows, LANES), jnp.float32),
            pltpu.SemaphoreType.DMA((blocks,)),
        ],
        out_shape=[
            jax.ShapeDtypeStruct((blocks, samples, LANES), jnp.float32),
            jax.ShapeDtypeStruct((8, LANES), jnp.float32),
        ],
        input_output_aliases=aliases,
        cost_estimate=NO_COST,
        compiler_params=PARAMS,
        name="second_pass",
    )(*operands)


def per_device(
    traces, first_trace_taps, first_time_taps, second_trace_taps, second_time_taps, dest_row
):
    blocks, samples, _ = traces.shape
    owners = lax.axis_size("rcv")
    me = lax.axis_index("rcv").astype(jnp.int32).reshape(1)
    even = (1 - lax.axis_index("shot") % 2).astype(jnp.int32).reshape(1)
    target = dest_row.reshape(blocks)

    def send(values, offset):
        pairs = [(i, (i + offset) % owners) for i in range(owners)]
        return lax.ppermute(values, "rcv", pairs) if offset else values

    bounds = chunk_bounds(samples)
    count = len(bounds) - 1
    sizes = [
        (bounds[step + 1] - bounds[step], owners) for step in range(count)
    ]
    *packed, picks = first_edges(even, traces)
    edges = swap_edges(packed)
    mats, times = weights(even, first_trace_taps, first_time_taps, blocks)

    def first(after, start, sizes):
        return first_pass(
            me, target, owners, traces, samples, edges, mats, times, after, start, sizes
        )

    def exchange(sent, before, *after):
        if len(sent) == 1:
            part = sent[0]
            if before is not None:
                part, before[0], *_ = lax.optimization_barrier((part, before[0], *after))
            return [lax.all_to_all(part, "rcv", split_axis=0, concat_axis=0, tiled=True)]
        arrived = []
        for offset, part in enumerate(sent):
            if offset and before is not None:
                part, before[offset], *_ = lax.optimization_barrier(
                    (part, before[offset], *after)
                )
            arrived.append(send(part, offset))
        return arrived

    sent = first([], 0, sizes[:1])
    late_target, _ = lax.optimization_barrier((target, sent[0][0]))
    columns = [send(late_target, offset) for offset in range(owners)]
    arrived = [exchange(sent[0], None)]
    if count > 1:
        sent += first(columns[1:], bounds[1], sizes[1:])
    mats, times, slots = late_weights(
        even, me, second_trace_taps, second_time_taps, columns, sent[-1][0], blocks
    )

    out, past, now, token, rims = None, None, None, None, None

    def second(step, after):
        at = max(0, bounds[step] - REACH // 2)
        stop = bounds[step + 1] - REACH // 2 if step + 1 < count else samples
        return second_pass(
            blocks, samples, past, now, mats, times, after, out, at, stop - at
        )

    for step in range(count):
        if step + 1 < count:
            ahead = [*now[1:]] if now else []
            ahead += [token] if token is not None else []
            arrived.append(exchange(sent[step + 1], arrived[step], *ahead))
        gathered, *packed = second_edges(
            slots, picks, arrived[step], times if token is None else token, blocks
        )
        rims = packed[0]
        coming = (gathered, *swap_edges(packed))
        if step:
            out, token = second(step - 1, rims)
            past = now
        now = coming
    out, token = second(count - 1, slots)
    return out


def solution(mesh):
    in_specs = (P("rcv", None, "shot"), P(), P(), P(), P(), P("rcv", "shot"))
    out_specs = P("rcv", None, "shot")
    return jax.shard_map(
        per_device, mesh=mesh, in_specs=in_specs, out_specs=out_specs, check_vma=False
    )
```

```python
import functools

import jax
import jax.numpy as jnp
from jax import lax
from jax.experimental import pallas as pl
from jax.experimental.pallas import tpu as pltpu
from jax.sharding import PartitionSpec as P

LANES = 128
EDGE = 8
SPAN = 256
REACH = 64
WIDE = SPAN - REACH
FOLD = 4
PARAMS = pltpu.CompilerParams(vmem_limit_bytes=16 * 2**20)
NO_COST = pl.CostEstimate(flops=1, bytes_accessed=1, transcendentals=0)
VMEM = pl.BlockSpec(memory_space=pltpu.VMEM)
SMEM = pl.BlockSpec(memory_space=pltpu.SMEM)
ANY = pl.BlockSpec(memory_space=pl.ANY)
HBM = pl.BlockSpec(memory_space=pltpu.HBM)
CHUNKS = (384, 576, 576)
NOTE = 16


def chunk_bounds(samples):
    bounds = [0]
    for size in CHUNKS:
        if bounds[-1] + size + REACH <= samples:
            bounds.append(bounds[-1] + size)
    bounds.append(samples)
    return bounds


def segment_plan(rows):
    count = -(-rows // WIDE)
    width = min(WIDE, -(-rows // (16 * count)) * 16)
    return count, width


def window_rows(rows):
    return rows - segment_plan(rows)[1] + SPAN


def folded_rows(rows):
    return -(-rows // (16 * FOLD)) * 16


def place_taps(taps_ref, origin, step):
    width = taps_ref.shape[1]
    tap = lax.broadcasted_iota(jnp.int32, (width, SPAN), 0)
    at = lax.broadcasted_iota(jnp.int32, (width, SPAN), 1)
    spread = jnp.where(at == (origin + step * tap + SPAN) % SPAN, 1.0, 0.0).astype(jnp.bfloat16)
    return jnp.dot(taps_ref[...], spread, preferred_element_type=jnp.float32)


def fill_weights(even, trace_ref, time_ref, mats_ref, times_ref):
    fans = trace_ref.shape[0]
    blocks = mats_ref.shape[0]
    trace_rows = place_taps(trace_ref, trace_ref.shape[1] // 2, -1)
    time_rows = place_taps(time_ref, 0, 1)
    for fan in range(fans):
        row = jnp.broadcast_to(trace_rows[fan : fan + 1, :], (LANES, SPAN))
        own = pltpu.roll(row, 0, 1, stride=1, stride_axis=0)[:, :LANES]
        left = pltpu.roll(row[:EDGE], SPAN - EDGE, 1, stride=1, stride_axis=0)[:, :LANES]
        right = pltpu.roll(row[:EDGE], LANES, 1, stride=1, stride_axis=0)[:, :LANES]
        pieces = (jnp.where(even, right, left), jnp.where(even, left, right))
        pair, half = fan // 2, fan % 2
        cols = slice(half * LANES, (half + 1) * LANES)
        for block in range(blocks):
            before, after = EDGE * block, EDGE * (blocks - 1 - block)
            parts = []
            for piece in pieces:
                if before:
                    parts.append(jnp.zeros((before, LANES), jnp.float32))
                parts.append(piece)
                if after:
                    parts.append(jnp.zeros((after, LANES), jnp.float32))
            parts.append(jnp.zeros((LANES - 2 * EDGE * blocks, LANES), jnp.float32))
            mats_ref[block, pair, :LANES, cols] = own.astype(jnp.bfloat16)
            mats_ref[block, pair, LANES:, cols] = jnp.concatenate(parts, axis=0).astype(
                jnp.bfloat16
            )
        taps = jnp.broadcast_to(time_rows[fan : fan + 1, :], (WIDE, SPAN))
        times_ref[:, fan * SPAN : (fan + 1) * SPAN] = pltpu.roll(
            taps, 0, 1, stride=1, stride_axis=0
        ).astype(jnp.bfloat16)


def weights_kernel(even_ref, trace_ref, time_ref, _, mats_ref, times_ref):
    fill_weights(even_ref[0] == 1, trace_ref, time_ref, mats_ref, times_ref)


def ranks(targets, blocks):
    owners = [lax.div(target, blocks) for target in targets]
    order = []
    for block, owner in enumerate(owners):
        rank = jnp.int32(0)
        for other in owners[:block]:
            rank = rank + jnp.where(other == owner, 1, 0)
        order.append(rank)
    return owners, order


def late_kernel(even_ref, me_ref, target_ref, trace_ref, time_ref, *refs):
    parts, (_, mats_ref, times_ref, slots_ref, notes, sem) = refs[:-6], refs[-6:]
    blocks, me = mats_ref.shape[0], me_ref[0]
    slot_cap, held = parts[0].shape[0], parts[0].shape[1]

    def fetch(offset):
        return pltpu.make_async_copy(
            parts[offset].at[0, pl.ds(held - NOTE, NOTE), :], notes.at[offset], sem.at[offset]
        )

    for offset in range(1, len(parts)):
        fetch(offset).start()
    fill_weights(even_ref[0] == 1, trace_ref, time_ref, mats_ref, times_ref)
    slots = [jnp.int32(0)] * blocks
    lane = lax.broadcasted_iota(jnp.int32, (1, LANES), 1)
    for offset in range(len(parts)):
        if offset:
            fetch(offset).wait()
            note = notes[offset].astype(jnp.float32)[:1]
            targets = [
                jnp.sum(jnp.where(lane == block, note, 0.0)).astype(jnp.int32)
                for block in range(blocks)
            ]
        else:
            targets = [target_ref[block] for block in range(blocks)]
        for target, rank in zip(targets, ranks(targets, blocks)[1]):
            for block in range(blocks):
                slots[block] = jnp.where(
                    target == me * blocks + block, offset * slot_cap + rank, slots[block]
                )
    for block in range(blocks):
        slots_ref[block] = slots[block]


def weight_shapes(blocks, fans):
    return [
        jax.ShapeDtypeStruct((blocks, fans // 2, 2 * LANES, 2 * LANES), jnp.bfloat16),
        jax.ShapeDtypeStruct((WIDE, fans * SPAN), jnp.bfloat16),
    ]


def weights(even, trace_taps, time_taps, after, blocks):
    return pl.pallas_call(
        weights_kernel,
        in_specs=[SMEM, VMEM, VMEM, ANY],
        out_specs=[VMEM, VMEM],
        out_shape=weight_shapes(blocks, trace_taps.shape[0]),
        cost_estimate=NO_COST,
        compiler_params=PARAMS,
        name="weights",
    )(even, trace_taps, time_taps, after)


def late_weights(even, me, target, trace_taps, time_taps, arrived, after):
    blocks = target.shape[0]
    return pl.pallas_call(
        late_kernel,
        in_specs=[SMEM, SMEM, SMEM, VMEM, VMEM] + [ANY] * (len(arrived) + 1),
        out_specs=[VMEM, VMEM, SMEM],
        out_shape=weight_shapes(blocks, trace_taps.shape[0])
        + [jax.ShapeDtypeStruct((blocks,), jnp.int32)],
        scratch_shapes=[
            pltpu.VMEM((len(arrived), NOTE, LANES), jnp.bfloat16),
            pltpu.SemaphoreType.DMA((len(arrived),)),
        ],
        cost_estimate=NO_COST,
        compiler_params=PARAMS,
        name="late_weights",
    )(even, me, target, trace_taps, time_taps, *arrived, after)


def edge_picks(even, blocks):
    trace = lax.broadcasted_iota(jnp.int32, (2 * LANES, 2 * LANES), 0)
    lane = lax.broadcasted_iota(jnp.int32, (2 * LANES, 2 * LANES), 1)
    last = jnp.where(even, 1, 0)
    begin = jnp.where(lane < LANES, last, 1 - last) * (LANES - EDGE)
    lane = lane % LANES
    picks = []
    for pair in range(blocks // 2):
        at = lane - EDGE * (2 * pair + trace // LANES)
        pick = (at >= 0) & (at < EDGE) & (trace % LANES == at + begin)
        picks.append(jnp.where(pick, 1.0, 0.0).astype(jnp.bfloat16))
    return picks


def pick_part(picks, tiles_ref, start, stop):
    found = None
    for pair, pick in enumerate(picks):
        both = jnp.concatenate(
            [tiles_ref[2 * pair, start:stop, :], tiles_ref[2 * pair + 1, start:stop, :]], axis=1
        )
        one = jnp.dot(both, pick, preferred_element_type=jnp.float32)
        found = one if found is None else found + one
    return found


def pack_edges(picks, tiles_ref, packed_refs):
    blocks, rows = tiles_ref.shape[:2]
    fold = folded_rows(rows)
    totals = [None, None]
    for part in range(FOLD):
        start, stop = part * fold, min(rows, (part + 1) * fold)
        found = pick_part(picks, tiles_ref, start, stop)
        if stop - start < fold:
            found = jnp.concatenate(
                [found, jnp.zeros((fold - stop + start, 2 * LANES), jnp.float32)], axis=0
            )
        for way in range(2):
            piece = found[:, way * LANES : (way + 1) * LANES]
            if part:
                piece = pltpu.roll(piece, part * EDGE * blocks, 1)
            totals[way] = piece if totals[way] is None else totals[way] + piece
    for way in range(2):
        packed_refs[way][...] = totals[way].astype(jnp.bfloat16)


def unpack_edges(packed_refs, rows, blocks, start, stop, give):
    fold, width = packed_refs[0].shape[0], EDGE * blocks
    while start < stop:
        part = start // fold
        until = min(stop, (part + 1) * fold)
        pieces = []
        for way in range(2):
            piece = packed_refs[way][start - part * fold : until - part * fold, :]
            shift = (way - part) * width % LANES
            piece = piece.astype(jnp.float32)
            pieces.append(pltpu.roll(piece, shift, 1) if shift else piece)
        lane = lax.broadcasted_iota(jnp.int32, pieces[0].shape, 1)
        give(start, jnp.where(lane < width, pieces[0], pieces[1]).astype(jnp.bfloat16))
        start = until


def first_edges_kernel(even_ref, x_ref, out_a, out_b, picks_ref):
    blocks = x_ref.shape[0]
    picks = edge_picks(even_ref[0] == 1, blocks)
    for pair, pick in enumerate(picks):
        picks_ref[pair] = pick
    pack_edges(picks, x_ref, (out_a, out_b))


def first_edges(even, traces):
    blocks = traces.shape[0]
    packed = jax.ShapeDtypeStruct((folded_rows(traces.shape[1]), LANES), jnp.bfloat16)
    return pl.pallas_call(
        first_edges_kernel,
        in_specs=[SMEM, VMEM],
        out_specs=[VMEM] * 3,
        out_shape=[
            packed,
            packed,
            jax.ShapeDtypeStruct((blocks // 2, 2 * LANES, 2 * LANES), jnp.bfloat16),
        ],
        cost_estimate=NO_COST,
        compiler_params=PARAMS,
        name="first_edges",
    )(even, traces)


def second_edges_kernel(slot_ref, picks_ref, *refs):
    parts, (_, sorted_ref, out_a, out_b, sem) = refs[:-5], refs[-5:]
    blocks, rows = sorted_ref.shape[:2]
    slot_cap = parts[0].shape[0]
    for block in range(blocks):
        slot = slot_ref[block]
        for offset, part in enumerate(parts):

            @pl.when(slot // slot_cap == offset)
            def _():
                pltpu.make_async_copy(
                    part.at[slot % slot_cap, pl.ds(0, rows), :], sorted_ref.at[block], sem.at[block]
                ).start()

    for block in range(blocks):
        pltpu.make_async_copy(
            parts[0].at[0, pl.ds(0, rows), :], sorted_ref.at[block], sem.at[block]
        ).wait()
    picks = [picks_ref[pair] for pair in range(blocks // 2)]
    pack_edges(picks, sorted_ref, (out_a, out_b))


def second_edges(slots, picks, arrived, rows, after, blocks):
    packed = jax.ShapeDtypeStruct((folded_rows(rows), LANES), jnp.bfloat16)
    return pl.pallas_call(
        second_edges_kernel,
        in_specs=[SMEM, VMEM] + [ANY] * (len(arrived) + 1),
        out_specs=[VMEM] * 3,
        scratch_shapes=[pltpu.SemaphoreType.DMA((blocks,))],
        out_shape=[jax.ShapeDtypeStruct((blocks, rows, LANES), jnp.bfloat16), packed, packed],
        cost_estimate=NO_COST,
        compiler_params=PARAMS,
        name="second_edges",
    )(slots, picks, *arrived, after)


def swap_edges(packed):
    count = lax.axis_size("shot")
    got = []
    for first, edges in enumerate(packed):
        pairs = []
        for low in range(first, count - 1, 2):
            pairs += [(low, low + 1), (low + 1, low)]
        got.append(lax.ppermute(edges, "shot", pairs))
    return got


def filter_window(pieces, merged, fans_ref, mats_ref, times_ref, rows, give, finish):
    fan_pairs = mats_ref.shape[1]
    blocks = mats_ref.shape[0]
    tall = fans_ref.shape[1]
    count, width = segment_plan(rows)
    covered = 0
    for at, size, _ in list(pieces) + [(tall, 0, None)]:
        if at > covered:
            fans_ref[:, covered:at, :] = jnp.zeros(
                (fans_ref.shape[0], at - covered, fans_ref.shape[2]), jnp.bfloat16
            )
        covered = at + size
    def do_pair(pair, carry):
        for half in range(2):
            block = 2 * pair + half
            cols = slice(half * LANES, (half + 1) * LANES)
            for at, size, load in pieces:
                lhs = jnp.concatenate([load(block), merged[at : at + size, :]], axis=1)
                for fan_pair in range(fan_pairs):
                    both = jnp.dot(
                        lhs, mats_ref[block, fan_pair], preferred_element_type=jnp.float32
                    ).astype(jnp.bfloat16)
                    fans_ref[2 * fan_pair, at : at + size, cols] = both[:, :LANES]
                    fans_ref[2 * fan_pair + 1, at : at + size, cols] = both[:, LANES:]
        for step in range(count):
            start = min(step * width, rows - width)
            total = None
            for fan in range(2 * fan_pairs):
                part = jnp.dot(
                    times_ref[:width, fan * SPAN : (fan + 1) * SPAN],
                    fans_ref[fan, start : start + SPAN, :],
                    preferred_element_type=jnp.float32,
                )
                total = part if total is None else total + part
            give(pair, start, total)
        finish(pair)
        return carry

    lax.fori_loop(0, blocks // 2, do_pair, 0)


def first_kernel(
    start, sizes, noted, owners, me_ref, target_ref, x_ref, edge_a, edge_b, mats_ref, times_ref,
    *refs
):
    outs = refs[-6 - owners * len(sizes) : -6]
    merged, fans_ref, done, note, sem, note_sem = refs[-6:]
    blocks, rows = done.shape[:2]
    samples = x_ref.shape[1]
    window = start - REACH // 2
    begin, end = max(0, window), min(samples, start + rows + REACH // 2)
    homes, order = ranks([target_ref[block] for block in range(blocks)], blocks)
    groups, at = [], 0
    for group, size in enumerate(sizes):
        groups.append((at, size, outs[group * owners : (group + 1) * owners]))
        at += size

    def tell(offset):
        return pltpu.make_async_copy(
            note, groups[0][2][offset].at[0, pl.ds(sizes[0], NOTE), :], note_sem.at[offset]
        )

    if noted:
        lane = lax.broadcasted_iota(jnp.int32, note.shape, 1)
        row = jnp.zeros(note.shape, jnp.int32)
        for block in range(blocks):
            row = jnp.where(lane == block, target_ref[block], row)
        note[...] = row.astype(jnp.float32).astype(jnp.bfloat16)
        for offset in range(owners):
            tell(offset).start()

    def put(row, values):
        merged[row - window : row - window + values.shape[0], :] = values

    unpack_edges((edge_a, edge_b), samples, blocks, begin, end, put)

    def give(pair, at, values):
        values = values.astype(jnp.bfloat16)
        for half in range(2):
            done[2 * pair + half, at : at + values.shape[0], :] = values[
                :, half * LANES : (half + 1) * LANES
            ]

    def pick(values, pair, half):
        value = values[half]
        for other in range(1, blocks // 2):
            value = jnp.where(pair == other, values[2 * other + half], value)
        return value

    def finish(pair):
        for half in range(2):
            block = 2 * pair + half
            owner, rank = pick(homes, pair, half), pick(order, pair, half)
            away = lax.rem(owner - me_ref[0] + owners, owners)
            for group, (at, size, arrays) in enumerate(groups):
                part = done.at[block, pl.ds(at, size), :]
                for offset, out_ref in enumerate(arrays):

                    @pl.when(away == offset)
                    def _():
                        pltpu.make_async_copy(
                            part, out_ref.at[rank, pl.ds(0, size), :], sem.at[group, block]
                        ).start()

    pieces = [(begin - window, end - begin, lambda block: x_ref[block, begin:end, :])]
    filter_window(pieces, merged, fans_ref, mats_ref, times_ref, rows, give, finish)
    for group, (at, size, arrays) in enumerate(groups):
        for block in range(blocks):
            pltpu.make_async_copy(
                done.at[block, pl.ds(at, size), :],
                arrays[0].at[0, pl.ds(0, size), :],
                sem.at[group, block],
            ).wait()
    if noted:
        for offset in range(owners):
            tell(offset).wait()


def first_pass(me, target, owners, traces, edges, mats, times, after, start, sizes, noted):
    blocks = traces.shape[0]
    fans = 2 * mats.shape[1]
    rows = sum(sizes)
    tall = window_rows(rows)
    shapes = []
    for group, size in enumerate(sizes):
        size += NOTE if noted and not group else 0
        shapes += [jax.ShapeDtypeStruct((blocks // 2, size, LANES), jnp.bfloat16)] * owners
    flat = pl.pallas_call(
        functools.partial(first_kernel, start, sizes, noted, owners),
        in_specs=[SMEM, SMEM] + [VMEM] * 5 + [ANY] * len(after),
        out_specs=[ANY] * len(shapes),
        scratch_shapes=[
            pltpu.VMEM((tall, LANES), jnp.bfloat16),
            pltpu.VMEM((fans, tall, 2 * LANES), jnp.bfloat16),
            pltpu.VMEM((blocks, rows, LANES), jnp.bfloat16),
            pltpu.VMEM((NOTE, LANES), jnp.bfloat16),
            pltpu.SemaphoreType.DMA((len(sizes), blocks)),
            pltpu.SemaphoreType.DMA((owners,)),
        ],
        out_shape=shapes,
        cost_estimate=NO_COST,
        compiler_params=PARAMS,
        name="first_pass",
    )(me, target, traces, *edges, mats, times, *after)
    return [flat[group * owners : (group + 1) * owners] for group in range(len(sizes))]


def second_kernel(at, has_past, *refs):
    refs = list(refs)
    take = lambda: refs.pop(0)
    past = [take() for _ in range(3)] if has_past else None
    now = [take() for _ in range(3)]
    mats_ref, times_ref, _ = take(), take(), take()
    if has_past:
        take()
    out_ref, token_ref, merged, fans_ref, done, sem = refs
    token_ref[...] = jnp.zeros_like(token_ref)
    blocks, rows = done.shape[:2]
    lead = REACH if has_past else REACH // 2
    pieces = []

    def put(origin):
        def store(row, values):
            merged[row - origin : row - origin + values.shape[0], :] = values

        return store

    if has_past:
        held = past[0].shape[1]
        unpack_edges(past[1:], held, blocks, held - REACH, held, put(held - REACH))
        pieces.append((0, REACH, lambda block: past[0][block, held - REACH :, :]))
    size = now[0].shape[1]
    unpack_edges(now[1:], size, blocks, 0, size, put(-lead))
    pieces.append((lead, size, lambda block: now[0][block]))

    def copy(block):
        return pltpu.make_async_copy(
            done.at[block], out_ref.at[block, pl.ds(at, rows), :], sem.at[block]
        )

    def give(pair, start, values):
        for half in range(2):
            done[2 * pair + half, start : start + values.shape[0], :] = values[
                :, half * LANES : (half + 1) * LANES
            ]

    def finish(pair):
        for half in range(2):
            copy(2 * pair + half).start()

    filter_window(pieces, merged, fans_ref, mats_ref, times_ref, rows, give, finish)
    for block in range(blocks):
        copy(block).wait()


def second_pass(blocks, samples, past, now, mats, times, after, out, at, rows):
    fans = 2 * mats.shape[1]
    tall = window_rows(rows)
    operands = [*(past or ()), *now, mats, times, after]
    specs = [VMEM] * (len(operands) - 1) + [ANY]
    aliases = {}
    if out is not None:
        specs.append(ANY)
        operands.append(out)
        aliases = {len(operands) - 1: 0}
    return pl.pallas_call(
        functools.partial(second_kernel, at, past is not None),
        in_specs=specs,
        out_specs=[ANY, VMEM],
        scratch_shapes=[
            pltpu.VMEM((tall, LANES), jnp.bfloat16),
            pltpu.VMEM((fans, tall, 2 * LANES), jnp.bfloat16),
            pltpu.VMEM((blocks, rows, LANES), jnp.float32),
            pltpu.SemaphoreType.DMA((blocks,)),
        ],
        out_shape=[
            jax.ShapeDtypeStruct((blocks, samples, LANES), jnp.float32),
            jax.ShapeDtypeStruct((8, LANES), jnp.float32),
        ],
        input_output_aliases=aliases,
        cost_estimate=NO_COST,
        compiler_params=PARAMS,
        name="second_pass",
    )(*operands)


def per_device(
    traces, first_trace_taps, first_time_taps, second_trace_taps, second_time_taps, dest_row
):
    blocks, samples, _ = traces.shape
    owners = lax.axis_size("rcv")
    me = lax.axis_index("rcv").astype(jnp.int32).reshape(1)
    even = (1 - lax.axis_index("shot") % 2).astype(jnp.int32).reshape(1)
    target = dest_row.reshape(blocks)

    def send(values, offset):
        pairs = [(i, (i + offset) % owners) for i in range(owners)]
        return lax.ppermute(values, "rcv", pairs) if offset else values

    bounds = chunk_bounds(samples)
    count = len(bounds) - 1
    sizes = [bounds[step + 1] - bounds[step] for step in range(count)]
    *packed, picks = first_edges(even, traces)
    edges = swap_edges(packed)
    mats, times = weights(even, first_trace_taps, first_time_taps, traces, blocks)

    def first(after, start, sizes, noted):
        return first_pass(
            me, target, owners, traces, edges, mats, times, after, start, sizes, noted
        )

    def exchange(sent, before, *after):
        arrived = []
        for offset, part in enumerate(sent):
            if offset and before is not None:
                part, before[offset], *_ = lax.optimization_barrier(
                    (part, before[offset], *after)
                )
            arrived.append(send(part, offset))
        return arrived

    sent = first([], 0, sizes[:1], True)
    arrived = [exchange(sent[0], None)]
    if count > 1:
        sent += first([sent[0][0]], bounds[1], sizes[1:], False)
    second_mats, second_times, slots = late_weights(
        even, me, target, second_trace_taps, second_time_taps, arrived[0], sent[-1][0]
    )

    out, past, now, token, rims = None, None, None, None, None

    def second(step, after):
        at = max(0, bounds[step] - REACH // 2)
        stop = bounds[step + 1] - REACH // 2 if step + 1 < count else samples
        return second_pass(
            blocks, samples, past, now, second_mats, second_times, after, out, at, stop - at
        )

    for step in range(count):
        if step + 1 < count:
            ahead = [*now[1:]] if now else []
            ahead += [token] if token is not None else []
            arrived.append(exchange(sent[step + 1], arrived[step], *ahead))
        gathered, *packed = second_edges(
            slots, picks, arrived[step], sizes[step], slots if token is None else token, blocks
        )
        rims = packed[0]
        coming = (gathered, *swap_edges(packed))
        if step:
            out, token = second(step - 1, rims)
            past = now
        now = coming
    out, token = second(count - 1, slots)
    return out


def solution(mesh):
    in_specs = (P("rcv", None, "shot"), P(), P(), P(), P(), P("rcv", "shot"))
    out_specs = P("rcv", None, "shot")
    return jax.shard_map(
        per_device, mesh=mesh, in_specs=in_specs, out_specs=out_specs, check_vma=False
    )
```

```python
import functools

import jax
import jax.numpy as jnp
from jax import lax
from jax.experimental import pallas as pl
from jax.experimental.pallas import tpu as pltpu
from jax.sharding import PartitionSpec as P

LANES = 128
EDGE = 8
SPAN = 256
REACH = 64
WIDE = SPAN - REACH
FOLD = 4
PARAMS = pltpu.CompilerParams(vmem_limit_bytes=16 * 2**20)
NO_COST = pl.CostEstimate(flops=1, bytes_accessed=1, transcendentals=0)
VMEM = pl.BlockSpec(memory_space=pltpu.VMEM)
SMEM = pl.BlockSpec(memory_space=pltpu.SMEM)
ANY = pl.BlockSpec(memory_space=pl.ANY)
HBM = pl.BlockSpec(memory_space=pltpu.HBM)
CHUNKS = (384, 576, 576)
RIM_FOLD = 8
NOTE = 16


def chunk_bounds(samples):
    bounds = [0]
    for size in CHUNKS:
        if bounds[-1] + size + REACH <= samples:
            bounds.append(bounds[-1] + size)
    bounds.append(samples)
    return bounds


def segment_plan(rows):
    count = -(-rows // WIDE)
    width = min(WIDE, -(-rows // (16 * count)) * 16)
    return count, width


def window_rows(rows):
    return rows - segment_plan(rows)[1] + SPAN


def folded_rows(rows):
    return -(-rows // (16 * FOLD)) * 16


def rim_rows(rows):
    return -(-rows // (16 * RIM_FOLD)) * 16


def place_taps(taps_ref, origin, step):
    width = taps_ref.shape[1]
    tap = lax.broadcasted_iota(jnp.int32, (width, SPAN), 0)
    at = lax.broadcasted_iota(jnp.int32, (width, SPAN), 1)
    spread = jnp.where(at == (origin + step * tap + SPAN) % SPAN, 1.0, 0.0).astype(jnp.bfloat16)
    return jnp.dot(taps_ref[...], spread, preferred_element_type=jnp.float32)


def fill_weights(even, trace_ref, time_ref, mats_ref, times_ref):
    fans = trace_ref.shape[0]
    blocks = mats_ref.shape[0]
    trace_rows = place_taps(trace_ref, trace_ref.shape[1] // 2, -1)
    time_rows = place_taps(time_ref, 0, 1)
    for fan in range(fans):
        row = jnp.broadcast_to(trace_rows[fan : fan + 1, :], (LANES, SPAN))
        own = pltpu.roll(row, 0, 1, stride=1, stride_axis=0)[:, :LANES]
        left = pltpu.roll(row[:EDGE], SPAN - EDGE, 1, stride=1, stride_axis=0)[:, :LANES]
        right = pltpu.roll(row[:EDGE], LANES, 1, stride=1, stride_axis=0)[:, :LANES]
        pieces = (jnp.where(even, right, left), jnp.where(even, left, right))
        pair, half = fan // 2, fan % 2
        cols = slice(half * LANES, (half + 1) * LANES)
        for block in range(blocks):
            before, after = EDGE * block, EDGE * (blocks - 1 - block)
            parts = []
            for piece in pieces:
                if before:
                    parts.append(jnp.zeros((before, LANES), jnp.float32))
                parts.append(piece)
                if after:
                    parts.append(jnp.zeros((after, LANES), jnp.float32))
            parts.append(jnp.zeros((LANES - 2 * EDGE * blocks, LANES), jnp.float32))
            mats_ref[block, pair, :LANES, cols] = own.astype(jnp.bfloat16)
            mats_ref[block, pair, LANES:, cols] = jnp.concatenate(parts, axis=0).astype(
                jnp.bfloat16
            )
        taps = jnp.broadcast_to(time_rows[fan : fan + 1, :], (WIDE, SPAN))
        times_ref[:, fan * SPAN : (fan + 1) * SPAN] = pltpu.roll(
            taps, 0, 1, stride=1, stride_axis=0
        ).astype(jnp.bfloat16)


def weights_kernel(even_ref, trace_ref, time_ref, _, mats_ref, times_ref):
    fill_weights(even_ref[0] == 1, trace_ref, time_ref, mats_ref, times_ref)


def ranks(targets, blocks):
    owners = [lax.div(target, blocks) for target in targets]
    order = []
    for block, owner in enumerate(owners):
        rank = jnp.int32(0)
        for other in owners[:block]:
            rank = rank + jnp.where(other == owner, 1, 0)
        order.append(rank)
    return owners, order


def late_kernel(even_ref, me_ref, target_ref, trace_ref, time_ref, *refs):
    parts, (_, mats_ref, times_ref, slots_ref, notes, sem) = refs[:-6], refs[-6:]
    blocks, me = mats_ref.shape[0], me_ref[0]
    slot_cap, held = parts[0].shape[0], parts[0].shape[1]

    def fetch(offset):
        return pltpu.make_async_copy(
            parts[offset].at[0, pl.ds(held - NOTE, NOTE), :], notes.at[offset], sem.at[offset]
        )

    for offset in range(1, len(parts)):
        fetch(offset).start()
    fill_weights(even_ref[0] == 1, trace_ref, time_ref, mats_ref, times_ref)
    slots = [jnp.int32(0)] * blocks
    lane = lax.broadcasted_iota(jnp.int32, (1, LANES), 1)
    for offset in range(len(parts)):
        if offset:
            fetch(offset).wait()
            note = notes[offset].astype(jnp.float32)[:1]
            targets = [
                jnp.sum(jnp.where(lane == block, note, 0.0)).astype(jnp.int32)
                for block in range(blocks)
            ]
        else:
            targets = [target_ref[block] for block in range(blocks)]
        for target, rank in zip(targets, ranks(targets, blocks)[1]):
            for block in range(blocks):
                slots[block] = jnp.where(
                    target == me * blocks + block, offset * slot_cap + rank, slots[block]
                )
    for block in range(blocks):
        slots_ref[block] = slots[block]


def weight_shapes(blocks, fans):
    return [
        jax.ShapeDtypeStruct((blocks, fans // 2, 2 * LANES, 2 * LANES), jnp.bfloat16),
        jax.ShapeDtypeStruct((WIDE, fans * SPAN), jnp.bfloat16),
    ]


def weights(even, trace_taps, time_taps, after, blocks):
    return pl.pallas_call(
        weights_kernel,
        in_specs=[SMEM, VMEM, VMEM, ANY],
        out_specs=[VMEM, VMEM],
        out_shape=weight_shapes(blocks, trace_taps.shape[0]),
        cost_estimate=NO_COST,
        compiler_params=PARAMS,
        name="weights",
    )(even, trace_taps, time_taps, after)


def late_weights(even, me, target, trace_taps, time_taps, arrived, after):
    blocks = target.shape[0]
    return pl.pallas_call(
        late_kernel,
        in_specs=[SMEM, SMEM, SMEM, VMEM, VMEM] + [ANY] * (len(arrived) + 1),
        out_specs=[VMEM, VMEM, SMEM],
        out_shape=weight_shapes(blocks, trace_taps.shape[0])
        + [jax.ShapeDtypeStruct((blocks,), jnp.int32)],
        scratch_shapes=[
            pltpu.VMEM((len(arrived), NOTE, LANES), jnp.bfloat16),
            pltpu.SemaphoreType.DMA((len(arrived),)),
        ],
        cost_estimate=NO_COST,
        compiler_params=PARAMS,
        name="late_weights",
    )(even, me, target, trace_taps, time_taps, *arrived, after)


def edge_picks(even, blocks):
    trace = lax.broadcasted_iota(jnp.int32, (2 * LANES, 2 * LANES), 0)
    lane = lax.broadcasted_iota(jnp.int32, (2 * LANES, 2 * LANES), 1)
    last = jnp.where(even, 1, 0)
    begin = jnp.where(lane < LANES, last, 1 - last) * (LANES - EDGE)
    lane = lane % LANES
    picks = []
    for pair in range(blocks // 2):
        at = lane - EDGE * (2 * pair + trace // LANES)
        pick = (at >= 0) & (at < EDGE) & (trace % LANES == at + begin)
        picks.append(jnp.where(pick, 1.0, 0.0).astype(jnp.bfloat16))
    return picks


def pick_part(picks, tiles_ref, start, stop):
    found = None
    for pair, pick in enumerate(picks):
        both = jnp.concatenate(
            [tiles_ref[2 * pair, start:stop, :], tiles_ref[2 * pair + 1, start:stop, :]], axis=1
        )
        one = jnp.dot(both, pick, preferred_element_type=jnp.float32)
        found = one if found is None else found + one
    return found


def pack_edges(picks, tiles_ref, packed_refs):
    blocks, rows = tiles_ref.shape[:2]
    fold = folded_rows(rows)
    totals = [None, None]
    for part in range(FOLD):
        start, stop = part * fold, min(rows, (part + 1) * fold)
        found = pick_part(picks, tiles_ref, start, stop)
        if stop - start < fold:
            found = jnp.concatenate(
                [found, jnp.zeros((fold - stop + start, 2 * LANES), jnp.float32)], axis=0
            )
        for way in range(2):
            piece = found[:, way * LANES : (way + 1) * LANES]
            if part:
                piece = pltpu.roll(piece, part * EDGE * blocks, 1)
            totals[way] = piece if totals[way] is None else totals[way] + piece
    for way in range(2):
        packed_refs[way][:fold, :] = totals[way].astype(jnp.bfloat16)


def unpack_edges(packed_refs, rows, blocks, start, stop, give):
    fold, width = folded_rows(rows), EDGE * blocks
    while start < stop:
        part = start // fold
        until = min(stop, (part + 1) * fold)
        pieces = []
        for way in range(2):
            piece = packed_refs[way][start - part * fold : until - part * fold, :]
            shift = (way - part) * width % LANES
            piece = piece.astype(jnp.float32)
            pieces.append(pltpu.roll(piece, shift, 1) if shift else piece)
        lane = lax.broadcasted_iota(jnp.int32, pieces[0].shape, 1)
        give(start, jnp.where(lane < width, pieces[0], pieces[1]).astype(jnp.bfloat16))
        start = until


def first_edges_kernel(even_ref, x_ref, out_a, out_b, picks_ref):
    blocks = x_ref.shape[0]
    picks = edge_picks(even_ref[0] == 1, blocks)
    for pair, pick in enumerate(picks):
        picks_ref[pair] = pick
    pack_edges(picks, x_ref, (out_a, out_b))


def first_edges(even, traces):
    blocks = traces.shape[0]
    packed = jax.ShapeDtypeStruct((folded_rows(traces.shape[1]), LANES), jnp.bfloat16)
    return pl.pallas_call(
        first_edges_kernel,
        in_specs=[SMEM, VMEM],
        out_specs=[VMEM] * 3,
        out_shape=[
            packed,
            packed,
            jax.ShapeDtypeStruct((blocks // 2, 2 * LANES, 2 * LANES), jnp.bfloat16),
        ],
        cost_estimate=NO_COST,
        compiler_params=PARAMS,
        name="first_edges",
    )(even, traces)


def gather_rows(slot_ref, parts, held_ref, sem, start):
    blocks, rows = held_ref.shape[:2]
    slot_cap = parts[0].shape[0]

    def begin():
        for block in range(blocks):
            slot = slot_ref[block]
            for offset, part in enumerate(parts):

                @pl.when(slot // slot_cap == offset)
                def _():
                    pltpu.make_async_copy(
                        part.at[slot % slot_cap, pl.ds(start, rows), :],
                        held_ref.at[block],
                        sem.at[block],
                    ).start()

    def wait():
        for block in range(blocks):
            pltpu.make_async_copy(
                parts[0].at[0, pl.ds(start, rows), :], held_ref.at[block], sem.at[block]
            ).wait()

    return begin, wait


def second_edges_kernel(even_ref, slot_ref, picks_ref, *refs):
    parts, (_, sorted_ref, out_a, out_b, rims_ref, sem, rim_sem) = refs[:-7], refs[-7:]
    blocks, rows = sorted_ref.shape[:2]
    begin, wait = gather_rows(slot_ref, parts, sorted_ref, sem, 0)
    begin()
    fold = folded_rows(rows)
    rimmed = out_a.shape[0] > fold
    if rimmed:
        rim_begin, rim_wait = gather_rows(slot_ref, parts, rims_ref, rim_sem, rows)
        rim_begin()
    wait()
    picks = [picks_ref[pair] for pair in range(blocks // 2)]
    pack_edges(picks, sorted_ref, (out_a, out_b))
    if rimmed:
        rim_wait()
        size = rims_ref.shape[1]
        even = even_ref[0] == 1
        for block in range(blocks):
            first = rims_ref[block].astype(jnp.float32)
            last = pltpu.roll(first, LANES - EDGE, 1)
            span = slice(fold + block * size, fold + (block + 1) * size)
            out_a[span, :] = jnp.where(even, last, first).astype(jnp.bfloat16)
            out_b[span, :] = jnp.where(even, first, last).astype(jnp.bfloat16)


def second_edges(even, slots, picks, arrived, rows, rims, after, blocks):
    packed = jax.ShapeDtypeStruct((folded_rows(rows) + blocks * rims, LANES), jnp.bfloat16)
    return pl.pallas_call(
        second_edges_kernel,
        in_specs=[SMEM, SMEM, VMEM] + [ANY] * (len(arrived) + 1),
        out_specs=[VMEM] * 3,
        scratch_shapes=[
            pltpu.VMEM((blocks, rims or 16, LANES), jnp.bfloat16),
            pltpu.SemaphoreType.DMA((blocks,)),
            pltpu.SemaphoreType.DMA((blocks,)),
        ],
        out_shape=[jax.ShapeDtypeStruct((blocks, rows, LANES), jnp.bfloat16), packed, packed],
        cost_estimate=NO_COST,
        compiler_params=PARAMS,
        name="second_edges",
    )(even, slots, picks, *arrived, after)


def swap_edges(packed):
    count = lax.axis_size("shot")
    got = []
    for first, edges in enumerate(packed):
        pairs = []
        for low in range(first, count - 1, 2):
            pairs += [(low, low + 1), (low + 1, low)]
        got.append(lax.ppermute(edges, "shot", pairs))
    return got


def filter_window(pieces, merged, fans_ref, mats_ref, times_ref, rows, give, finish):
    fan_pairs = mats_ref.shape[1]
    blocks = mats_ref.shape[0]
    tall = fans_ref.shape[1]
    count, width = segment_plan(rows)
    covered = 0
    for at, size, _ in list(pieces) + [(tall, 0, None)]:
        if at > covered:
            fans_ref[:, covered:at, :] = jnp.zeros(
                (fans_ref.shape[0], at - covered, fans_ref.shape[2]), jnp.bfloat16
            )
        covered = at + size
    def do_pair(pair, carry):
        for half in range(2):
            block = 2 * pair + half
            cols = slice(half * LANES, (half + 1) * LANES)
            for at, size, load in pieces:
                lhs = jnp.concatenate([load(block), merged[at : at + size, :]], axis=1)
                for fan_pair in range(fan_pairs):
                    both = jnp.dot(
                        lhs, mats_ref[block, fan_pair], preferred_element_type=jnp.float32
                    ).astype(jnp.bfloat16)
                    fans_ref[2 * fan_pair, at : at + size, cols] = both[:, :LANES]
                    fans_ref[2 * fan_pair + 1, at : at + size, cols] = both[:, LANES:]
        for step in range(count):
            start = min(step * width, rows - width)
            total = None
            for fan in range(2 * fan_pairs):
                part = jnp.dot(
                    times_ref[:width, fan * SPAN : (fan + 1) * SPAN],
                    fans_ref[fan, start : start + SPAN, :],
                    preferred_element_type=jnp.float32,
                )
                total = part if total is None else total + part
            give(pair, start, total)
        finish(pair)
        return carry

    lax.fori_loop(0, blocks // 2, do_pair, 0)


def first_kernel(
    start, sizes, noted, owners, me_ref, target_ref, x_ref, edge_a, edge_b, mats_ref, times_ref,
    *refs
):
    outs = refs[-8 - owners * len(sizes) : -8]
    merged, fans_ref, done, note, rims, sem, note_sem, rim_sem = refs[-8:]
    blocks, rows = done.shape[:2]
    samples = x_ref.shape[1]
    window = start - REACH // 2
    begin, end = max(0, window), min(samples, start + rows + REACH // 2)
    homes, order = ranks([target_ref[block] for block in range(blocks)], blocks)
    groups, at = [], 0
    for group, size in enumerate(sizes):
        groups.append((at, size, outs[group * owners : (group + 1) * owners]))
        at += size

    def tell(offset):
        return pltpu.make_async_copy(
            note, groups[0][2][offset].at[0, pl.ds(sizes[0], NOTE), :], note_sem.at[offset]
        )

    if noted:
        lane = lax.broadcasted_iota(jnp.int32, note.shape, 1)
        row = jnp.zeros(note.shape, jnp.int32)
        for block in range(blocks):
            row = jnp.where(lane == block, target_ref[block], row)
        note[...] = row.astype(jnp.float32).astype(jnp.bfloat16)
        for offset in range(owners):
            tell(offset).start()

    def put(row, values):
        merged[row - window : row - window + values.shape[0], :] = values

    unpack_edges((edge_a, edge_b), samples, blocks, begin, end, put)

    def give(pair, at, values):
        values = values.astype(jnp.bfloat16)
        for half in range(2):
            done[2 * pair + half, at : at + values.shape[0], :] = values[
                :, half * LANES : (half + 1) * LANES
            ]

    def pick(values, pair, half):
        value = values[half]
        for other in range(1, blocks // 2):
            value = jnp.where(pair == other, values[2 * other + half], value)
        return value

    def pack_rim(block):
        at, size, _ = groups[-1]
        trace = lax.broadcasted_iota(jnp.int32, (LANES, LANES), 0)
        lane = lax.broadcasted_iota(jnp.int32, (LANES, LANES), 1)
        wanted = jnp.where(lane < EDGE, lane, lane + LANES - 2 * EDGE)
        chosen = jnp.where((lane < 2 * EDGE) & (trace == wanted), 1.0, 0.0).astype(jnp.bfloat16)
        found = jnp.dot(done[block, at : at + size, :], chosen, preferred_element_type=jnp.float32)
        fold, total = rims.shape[1], None
        for part in range(-(-size // fold)):
            piece = found[part * fold : (part + 1) * fold]
            if piece.shape[0] < fold:
                rest = jnp.zeros((fold - piece.shape[0], LANES), jnp.float32)
                piece = jnp.concatenate([piece, rest], axis=0)
            if part:
                piece = pltpu.roll(piece, 2 * EDGE * part, 1)
            total = piece if total is None else total + piece
        rims[block] = total.astype(jnp.bfloat16)

    rim_group = None if noted else len(groups) - 2

    def finish(pair):
        for half in range(2):
            block = 2 * pair + half
            if not noted:
                pack_rim(block)
            owner, rank = pick(homes, pair, half), pick(order, pair, half)
            away = lax.rem(owner - me_ref[0] + owners, owners)
            for group, (at, size, arrays) in enumerate(groups):
                part = done.at[block, pl.ds(at, size), :]
                for offset, out_ref in enumerate(arrays):

                    @pl.when(away == offset)
                    def _():
                        pltpu.make_async_copy(
                            part, out_ref.at[rank, pl.ds(0, size), :], sem.at[group, block]
                        ).start()
                        if group == rim_group:
                            pltpu.make_async_copy(
                                rims.at[block],
                                out_ref.at[rank, pl.ds(size, rims.shape[1]), :],
                                rim_sem.at[block],
                            ).start()

    pieces = [(begin - window, end - begin, lambda block: x_ref[block, begin:end, :])]
    filter_window(pieces, merged, fans_ref, mats_ref, times_ref, rows, give, finish)
    for group, (at, size, arrays) in enumerate(groups):
        for block in range(blocks):
            pltpu.make_async_copy(
                done.at[block, pl.ds(at, size), :],
                arrays[0].at[0, pl.ds(0, size), :],
                sem.at[group, block],
            ).wait()
    if noted:
        for offset in range(owners):
            tell(offset).wait()
    else:
        _, size, arrays = groups[rim_group]
        for block in range(blocks):
            pltpu.make_async_copy(
                rims.at[block],
                arrays[0].at[0, pl.ds(size, rims.shape[1]), :],
                rim_sem.at[block],
            ).wait()


def first_pass(me, target, owners, traces, edges, mats, times, after, start, sizes, noted):
    blocks = traces.shape[0]
    fans = 2 * mats.shape[1]
    rows = sum(sizes)
    tall = window_rows(rows)
    shapes = []
    for group, size in enumerate(sizes):
        size += NOTE if noted else rim_rows(sizes[-1]) if group == len(sizes) - 2 else 0
        shapes += [jax.ShapeDtypeStruct((blocks // 2, size, LANES), jnp.bfloat16)] * owners
    flat = pl.pallas_call(
        functools.partial(first_kernel, start, sizes, noted, owners),
        in_specs=[SMEM, SMEM] + [VMEM] * 5 + [ANY] * len(after),
        out_specs=[ANY] * len(shapes),
        scratch_shapes=[
            pltpu.VMEM((tall, LANES), jnp.bfloat16),
            pltpu.VMEM((fans, tall, 2 * LANES), jnp.bfloat16),
            pltpu.VMEM((blocks, rows, LANES), jnp.bfloat16),
            pltpu.VMEM((NOTE, LANES), jnp.bfloat16),
            pltpu.VMEM((blocks, rim_rows(sizes[-1]), LANES), jnp.bfloat16),
            pltpu.SemaphoreType.DMA((len(sizes), blocks)),
            pltpu.SemaphoreType.DMA((owners,)),
            pltpu.SemaphoreType.DMA((blocks,)),
        ],
        out_shape=shapes,
        cost_estimate=NO_COST,
        compiler_params=PARAMS,
        name="first_pass",
    )(me, target, traces, *edges, mats, times, *after)
    return [flat[group * owners : (group + 1) * owners] for group in range(len(sizes))]


def second_kernel(at, has_past, *refs):
    refs = list(refs)
    take = lambda: refs.pop(0)
    past = [take() for _ in range(3)] if has_past else None
    now = [take() for _ in range(3)]
    mats_ref, times_ref, _ = take(), take(), take()
    if has_past:
        take()
    out_ref, token_ref, merged, fans_ref, done, sem = refs
    token_ref[...] = jnp.zeros_like(token_ref)
    blocks, rows = done.shape[:2]
    lead = REACH if has_past else REACH // 2
    pieces = []

    def put(origin):
        def store(row, values):
            merged[row - origin : row - origin + values.shape[0], :] = values

        return store

    if has_past:
        held = past[0].shape[1]
        unpack_edges(past[1:], held, blocks, held - REACH, held, put(held - REACH))
        pieces.append((0, REACH, lambda block: past[0][block, held - REACH :, :]))
    size = now[0].shape[1]
    unpack_edges(now[1:], size, blocks, 0, size, put(-lead))
    pieces.append((lead, size, lambda block: now[0][block]))

    def copy(block):
        return pltpu.make_async_copy(
            done.at[block], out_ref.at[block, pl.ds(at, rows), :], sem.at[block]
        )

    def give(pair, start, values):
        for half in range(2):
            done[2 * pair + half, start : start + values.shape[0], :] = values[
                :, half * LANES : (half + 1) * LANES
            ]

    def finish(pair):
        for half in range(2):
            copy(2 * pair + half).start()

    filter_window(pieces, merged, fans_ref, mats_ref, times_ref, rows, give, finish)
    for block in range(blocks):
        copy(block).wait()


def second_pass(blocks, samples, past, now, mats, times, after, out, at, rows):
    fans = 2 * mats.shape[1]
    tall = window_rows(rows)
    operands = [*(past or ()), *now, mats, times, after]
    specs = [VMEM] * (len(operands) - 1) + [ANY]
    aliases = {}
    if out is not None:
        specs.append(ANY)
        operands.append(out)
        aliases = {len(operands) - 1: 0}
    return pl.pallas_call(
        functools.partial(second_kernel, at, past is not None),
        in_specs=specs,
        out_specs=[ANY, VMEM],
        scratch_shapes=[
            pltpu.VMEM((tall, LANES), jnp.bfloat16),
            pltpu.VMEM((fans, tall, 2 * LANES), jnp.bfloat16),
            pltpu.VMEM((blocks, rows, LANES), jnp.float32),
            pltpu.SemaphoreType.DMA((blocks,)),
        ],
        out_shape=[
            jax.ShapeDtypeStruct((blocks, samples, LANES), jnp.float32),
            jax.ShapeDtypeStruct((8, LANES), jnp.float32),
        ],
        input_output_aliases=aliases,
        cost_estimate=NO_COST,
        compiler_params=PARAMS,
        name="second_pass",
    )(*operands)


def last_kernel(
    at, slot_ref, past_ref, edge_a, edge_b, mats_ref, times_ref, _, *refs
):
    parts, (out_ref, merged, fans_ref, held, done, in_sem, sem) = refs[:-7], refs[-7:]
    blocks, rows = done.shape[:2]
    before, size = past_ref.shape[1], held.shape[1]
    begin, wait = gather_rows(slot_ref, parts, held, in_sem, 0)
    begin()
    origin = before - REACH

    def put(row, values):
        merged[row - origin : row - origin + values.shape[0], :] = values

    unpack_edges((edge_a, edge_b), before, blocks, origin, before, put)
    fold, base = rim_rows(size), folded_rows(before)
    for part in range(-(-size // fold)):
        count = min(fold, size - part * fold)
        lane = lax.broadcasted_iota(jnp.int32, (count, LANES), 1)
        total = jnp.zeros((count, LANES), jnp.float32)
        for way, edge in enumerate((edge_a, edge_b)):
            for block in range(blocks):
                to = EDGE * (way * blocks + block)
                top = base + block * fold
                piece = edge[top : top + count, :].astype(jnp.float32)
                shift = (to - 2 * EDGE * part) % LANES
                piece = pltpu.roll(piece, shift, 1) if shift else piece
                total = jnp.where((lane >= to) & (lane < to + EDGE), piece, total)
        row = REACH + part * fold
        merged[row : row + count, :] = total.astype(jnp.bfloat16)
    wait()

    def copy(block):
        return pltpu.make_async_copy(
            done.at[block], out_ref.at[block, pl.ds(at, rows), :], sem.at[block]
        )

    def give(pair, start, values):
        for half in range(2):
            done[2 * pair + half, start : start + values.shape[0], :] = values[
                :, half * LANES : (half + 1) * LANES
            ]

    def finish(pair):
        for half in range(2):
            copy(2 * pair + half).start()

    pieces = [
        (0, REACH, lambda block: past_ref[block, origin:, :]),
        (REACH, size, lambda block: held[block]),
    ]
    filter_window(pieces, merged, fans_ref, mats_ref, times_ref, rows, give, finish)
    for block in range(blocks):
        copy(block).wait()


def last_pass(slots, past, parts, size, mats, times, out, at, rows):
    blocks, samples, _ = out.shape
    fans = 2 * mats.shape[1]
    tall = window_rows(rows)
    return pl.pallas_call(
        functools.partial(last_kernel, at),
        in_specs=[SMEM] + [VMEM] * 5 + [ANY] * (1 + len(parts)),
        out_specs=ANY,
        scratch_shapes=[
            pltpu.VMEM((tall, LANES), jnp.bfloat16),
            pltpu.VMEM((fans, tall, 2 * LANES), jnp.bfloat16),
            pltpu.VMEM((blocks, size, LANES), jnp.bfloat16),
            pltpu.VMEM((blocks, rows, LANES), jnp.float32),
            pltpu.SemaphoreType.DMA((blocks,)),
            pltpu.SemaphoreType.DMA((blocks,)),
        ],
        out_shape=jax.ShapeDtypeStruct(out.shape, jnp.float32),
        input_output_aliases={6: 0},
        cost_estimate=NO_COST,
        compiler_params=PARAMS,
        name="last_pass",
    )(slots, *past, mats, times, out, *parts)


def per_device(
    traces, first_trace_taps, first_time_taps, second_trace_taps, second_time_taps, dest_row
):
    blocks, samples, _ = traces.shape
    owners = lax.axis_size("rcv")
    me = lax.axis_index("rcv").astype(jnp.int32).reshape(1)
    even = (1 - lax.axis_index("shot") % 2).astype(jnp.int32).reshape(1)
    target = dest_row.reshape(blocks)

    def send(values, offset):
        pairs = [(i, (i + offset) % owners) for i in range(owners)]
        return lax.ppermute(values, "rcv", pairs) if offset else values

    bounds = chunk_bounds(samples)
    count = len(bounds) - 1
    sizes = [bounds[step + 1] - bounds[step] for step in range(count)]
    *packed, picks = first_edges(even, traces)
    edges = swap_edges(packed)
    mats, times = weights(even, first_trace_taps, first_time_taps, traces, blocks)

    def first(after, start, sizes, noted):
        return first_pass(
            me, target, owners, traces, edges, mats, times, after, start, sizes, noted
        )

    def exchange(sent, before, *after):
        arrived = []
        for offset, part in enumerate(sent):
            if offset and before is not None:
                part, before[offset], *_ = lax.optimization_barrier(
                    (part, before[offset], *after)
                )
            arrived.append(send(part, offset))
        return arrived

    sent = first([], 0, sizes[:1], True)
    arrived = [exchange(sent[0], None)]
    sent += first([sent[0][0]], bounds[1], sizes[1:], False)
    second_mats, second_times, slots = late_weights(
        even, me, target, second_trace_taps, second_time_taps, arrived[0], sent[-1][0]
    )

    out, past, now, token, rims = None, None, None, None, None

    def second(step, after):
        at = max(0, bounds[step] - REACH // 2)
        stop = bounds[step + 1] - REACH // 2 if step + 1 < count else samples
        return second_pass(
            blocks, samples, past, now, second_mats, second_times, after, out, at, stop - at
        )

    for step in range(count - 1):
        ahead = [*now[1:]] if now else []
        ahead += [token] if token is not None else []
        arrived.append(exchange(sent[step + 1], arrived[step], *ahead))
        gathered, *packed = second_edges(
            even,
            slots,
            picks,
            arrived[step],
            sizes[step],
            rim_rows(sizes[-1]) if step == count - 2 else 0,
            slots if token is None else token,
            blocks,
        )
        rims = packed[0]
        coming = (gathered, *swap_edges(packed))
        if step:
            out, token = second(step - 1, rims)
            past = now
        now = coming
    out, token = second(count - 2, slots)
    at = bounds[count - 1] - REACH // 2
    return last_pass(
        slots, now, arrived[-1], sizes[-1], second_mats, second_times, out, at, samples - at
    )


def solution(mesh):
    in_specs = (P("rcv", None, "shot"), P(), P(), P(), P(), P("rcv", "shot"))
    out_specs = P("rcv", None, "shot")
    return jax.shard_map(
        per_device, mesh=mesh, in_specs=in_specs, out_specs=out_specs, check_vma=False
    )
```

```python
import functools

import jax
import jax.numpy as jnp
from jax import lax
from jax.experimental import pallas as pl
from jax.experimental.pallas import tpu as pltpu
from jax.sharding import PartitionSpec as P

LANES = 128
EDGE = 8
SPAN = 256
REACH = 64
WIDE = SPAN - REACH
FOLD = 4
PARAMS = pltpu.CompilerParams(vmem_limit_bytes=16 * 2**20)
NO_COST = pl.CostEstimate(flops=1, bytes_accessed=1, transcendentals=0)
VMEM = pl.BlockSpec(memory_space=pltpu.VMEM)
SMEM = pl.BlockSpec(memory_space=pltpu.SMEM)
ANY = pl.BlockSpec(memory_space=pl.ANY)
HBM = pl.BlockSpec(memory_space=pltpu.HBM)
CHUNKS = (384, 576, 512)
RIM_FOLD = 8
NOTE = 16


def chunk_bounds(samples):
    bounds = [0]
    for size in CHUNKS:
        if bounds[-1] + size + REACH <= samples:
            bounds.append(bounds[-1] + size)
    bounds.append(samples)
    return bounds


def segment_plan(rows):
    count = -(-rows // WIDE)
    width = min(WIDE, -(-rows // (16 * count)) * 16)
    return count, width


def window_rows(rows):
    return rows - segment_plan(rows)[1] + SPAN


def folded_rows(rows):
    return -(-rows // (16 * FOLD)) * 16


def rim_rows(rows):
    return -(-rows // (16 * RIM_FOLD)) * 16


def place_taps(taps_ref, origin, step):
    width = taps_ref.shape[1]
    tap = lax.broadcasted_iota(jnp.int32, (width, SPAN), 0)
    at = lax.broadcasted_iota(jnp.int32, (width, SPAN), 1)
    spread = jnp.where(at == (origin + step * tap + SPAN) % SPAN, 1.0, 0.0).astype(jnp.bfloat16)
    return jnp.dot(taps_ref[...], spread, preferred_element_type=jnp.float32)


def fill_weights(even, trace_ref, time_ref, own_ref, halo_ref, times_ref):
    fans = trace_ref.shape[0]
    blocks = halo_ref.shape[0]
    trace_rows = place_taps(trace_ref, trace_ref.shape[1] // 2, -1)
    time_rows = place_taps(time_ref, 0, 1)
    for fan in range(fans):
        row = jnp.broadcast_to(trace_rows[fan : fan + 1, :], (LANES, SPAN))
        own = pltpu.roll(row, 0, 1, stride=1, stride_axis=0)[:, :LANES]
        left = pltpu.roll(row[:EDGE], SPAN - EDGE, 1, stride=1, stride_axis=0)[:, :LANES]
        right = pltpu.roll(row[:EDGE], LANES, 1, stride=1, stride_axis=0)[:, :LANES]
        pieces = (jnp.where(even, right, left), jnp.where(even, left, right))
        pair, half = fan // 2, fan % 2
        cols = slice(half * LANES, (half + 1) * LANES)
        own_ref[pair, :, cols] = own.astype(jnp.bfloat16)
        for block in range(blocks):
            before, after = EDGE * block, EDGE * (blocks - 1 - block)
            parts = []
            for piece in pieces:
                if before:
                    parts.append(jnp.zeros((before, LANES), jnp.float32))
                parts.append(piece)
                if after:
                    parts.append(jnp.zeros((after, LANES), jnp.float32))
            parts.append(jnp.zeros((LANES - 2 * EDGE * blocks, LANES), jnp.float32))
            halo_ref[block, pair, :, cols] = jnp.concatenate(parts, axis=0).astype(jnp.bfloat16)
        taps = jnp.broadcast_to(time_rows[fan : fan + 1, :], (WIDE, SPAN))
        times_ref[:, fan * SPAN : (fan + 1) * SPAN] = pltpu.roll(
            taps, 0, 1, stride=1, stride_axis=0
        ).astype(jnp.bfloat16)


def weights_kernel(even_ref, trace_ref, time_ref, _, *refs):
    fill_weights(even_ref[0] == 1, trace_ref, time_ref, *refs)


def ranks(targets, blocks):
    owners = [lax.div(target, blocks) for target in targets]
    order = []
    for block, owner in enumerate(owners):
        rank = jnp.int32(0)
        for other in owners[:block]:
            rank = rank + jnp.where(other == owner, 1, 0)
        order.append(rank)
    return owners, order


def late_kernel(even_ref, me_ref, target_ref, trace_ref, time_ref, *refs):
    parts, (_, own_ref, halo_ref, times_ref, slots_ref, notes, sem) = refs[:-7], refs[-7:]
    blocks, me = halo_ref.shape[0], me_ref[0]
    slot_cap, held = parts[0].shape[0], parts[0].shape[1]

    def fetch(offset):
        return pltpu.make_async_copy(
            parts[offset].at[0, pl.ds(held - NOTE, NOTE), :], notes.at[offset], sem.at[offset]
        )

    for offset in range(1, len(parts)):
        fetch(offset).start()
    fill_weights(even_ref[0] == 1, trace_ref, time_ref, own_ref, halo_ref, times_ref)
    slots = [jnp.int32(0)] * blocks
    lane = lax.broadcasted_iota(jnp.int32, (1, LANES), 1)
    for offset in range(len(parts)):
        if offset:
            fetch(offset).wait()
            note = notes[offset].astype(jnp.float32)[:1]
            targets = [
                jnp.sum(jnp.where(lane == block, note, 0.0)).astype(jnp.int32)
                for block in range(blocks)
            ]
        else:
            targets = [target_ref[block] for block in range(blocks)]
        for target, rank in zip(targets, ranks(targets, blocks)[1]):
            for block in range(blocks):
                slots[block] = jnp.where(
                    target == me * blocks + block, offset * slot_cap + rank, slots[block]
                )
    for block in range(blocks):
        slots_ref[block] = slots[block]


def weight_shapes(blocks, fans):
    return [
        jax.ShapeDtypeStruct((fans // 2, LANES, 2 * LANES), jnp.bfloat16),
        jax.ShapeDtypeStruct((blocks, fans // 2, LANES, 2 * LANES), jnp.bfloat16),
        jax.ShapeDtypeStruct((WIDE, fans * SPAN), jnp.bfloat16),
    ]


def weights(even, trace_taps, time_taps, after, blocks):
    return pl.pallas_call(
        weights_kernel,
        in_specs=[SMEM, VMEM, VMEM, ANY],
        out_specs=[VMEM] * 3,
        out_shape=weight_shapes(blocks, trace_taps.shape[0]),
        cost_estimate=NO_COST,
        compiler_params=PARAMS,
        name="weights",
    )(even, trace_taps, time_taps, after)


def late_weights(even, me, target, trace_taps, time_taps, arrived, after):
    blocks = target.shape[0]
    return pl.pallas_call(
        late_kernel,
        in_specs=[SMEM, SMEM, SMEM, VMEM, VMEM] + [ANY] * (len(arrived) + 1),
        out_specs=[VMEM] * 3 + [SMEM],
        out_shape=weight_shapes(blocks, trace_taps.shape[0])
        + [jax.ShapeDtypeStruct((blocks,), jnp.int32)],
        scratch_shapes=[
            pltpu.VMEM((len(arrived), NOTE, LANES), jnp.bfloat16),
            pltpu.SemaphoreType.DMA((len(arrived),)),
        ],
        cost_estimate=NO_COST,
        compiler_params=PARAMS,
        name="late_weights",
    )(even, me, target, trace_taps, time_taps, *arrived, after)


def edge_picks(even, blocks):
    trace = lax.broadcasted_iota(jnp.int32, (2 * LANES, 2 * LANES), 0)
    lane = lax.broadcasted_iota(jnp.int32, (2 * LANES, 2 * LANES), 1)
    last = jnp.where(even, 1, 0)
    begin = jnp.where(lane < LANES, last, 1 - last) * (LANES - EDGE)
    lane = lane % LANES
    picks = []
    for pair in range(blocks // 2):
        at = lane - EDGE * (2 * pair + trace // LANES)
        pick = (at >= 0) & (at < EDGE) & (trace % LANES == at + begin)
        picks.append(jnp.where(pick, 1.0, 0.0).astype(jnp.bfloat16))
    return picks


def pick_part(picks, tiles_ref, start, stop):
    found = None
    for pair, pick in enumerate(picks):
        both = jnp.concatenate(
            [tiles_ref[2 * pair, start:stop, :], tiles_ref[2 * pair + 1, start:stop, :]], axis=1
        )
        one = jnp.dot(both, pick, preferred_element_type=jnp.float32)
        found = one if found is None else found + one
    return found


def pack_edges(picks, tiles_ref, packed_refs):
    blocks, rows = tiles_ref.shape[:2]
    fold = folded_rows(rows)
    totals = [None, None]
    for part in range(FOLD):
        start, stop = part * fold, min(rows, (part + 1) * fold)
        found = pick_part(picks, tiles_ref, start, stop)
        if stop - start < fold:
            found = jnp.concatenate(
                [found, jnp.zeros((fold - stop + start, 2 * LANES), jnp.float32)], axis=0
            )
        for way in range(2):
            piece = found[:, way * LANES : (way + 1) * LANES]
            if part:
                piece = pltpu.roll(piece, part * EDGE * blocks, 1)
            totals[way] = piece if totals[way] is None else totals[way] + piece
    for way in range(2):
        packed_refs[way][:fold, :] = totals[way].astype(jnp.bfloat16)


def unpack_edges(packed_refs, rows, blocks, start, stop, give):
    fold, width = folded_rows(rows), EDGE * blocks
    while start < stop:
        part = start // fold
        until = min(stop, (part + 1) * fold)
        pieces = []
        for way in range(2):
            piece = packed_refs[way][start - part * fold : until - part * fold, :]
            shift = (way - part) * width % LANES
            piece = piece.astype(jnp.float32)
            pieces.append(pltpu.roll(piece, shift, 1) if shift else piece)
        lane = lax.broadcasted_iota(jnp.int32, pieces[0].shape, 1)
        give(start, jnp.where(lane < width, pieces[0], pieces[1]).astype(jnp.bfloat16))
        start = until


def first_edges_kernel(even_ref, x_ref, out_a, out_b, picks_ref):
    blocks = x_ref.shape[0]
    picks = edge_picks(even_ref[0] == 1, blocks)
    for pair, pick in enumerate(picks):
        picks_ref[pair] = pick
    pack_edges(picks, x_ref, (out_a, out_b))


def first_edges(even, traces):
    blocks = traces.shape[0]
    packed = jax.ShapeDtypeStruct((folded_rows(traces.shape[1]), LANES), jnp.bfloat16)
    return pl.pallas_call(
        first_edges_kernel,
        in_specs=[SMEM, VMEM],
        out_specs=[VMEM] * 3,
        out_shape=[
            packed,
            packed,
            jax.ShapeDtypeStruct((blocks // 2, 2 * LANES, 2 * LANES), jnp.bfloat16),
        ],
        cost_estimate=NO_COST,
        compiler_params=PARAMS,
        name="first_edges",
    )(even, traces)


def gather_rows(slot_ref, parts, held_ref, sem, start):
    blocks, rows = held_ref.shape[:2]
    slot_cap = parts[0].shape[0]

    def begin():
        for block in range(blocks):
            slot = slot_ref[block]
            for offset, part in enumerate(parts):

                @pl.when(slot // slot_cap == offset)
                def _():
                    pltpu.make_async_copy(
                        part.at[slot % slot_cap, pl.ds(start, rows), :],
                        held_ref.at[block],
                        sem.at[block],
                    ).start()

    def wait():
        for block in range(blocks):
            pltpu.make_async_copy(
                parts[0].at[0, pl.ds(start, rows), :], held_ref.at[block], sem.at[block]
            ).wait()

    return begin, wait


def second_edges_kernel(even_ref, slot_ref, picks_ref, *refs):
    parts, (_, sorted_ref, out_a, out_b, rims_ref, sem, rim_sem) = refs[:-7], refs[-7:]
    blocks, rows = sorted_ref.shape[:2]
    begin, wait = gather_rows(slot_ref, parts, sorted_ref, sem, 0)
    begin()
    fold = folded_rows(rows)
    rimmed = out_a.shape[0] > fold
    if rimmed:
        rim_begin, rim_wait = gather_rows(slot_ref, parts, rims_ref, rim_sem, rows)
        rim_begin()
    wait()
    picks = [picks_ref[pair] for pair in range(blocks // 2)]
    pack_edges(picks, sorted_ref, (out_a, out_b))
    if rimmed:
        rim_wait()
        size = rims_ref.shape[1]
        even = even_ref[0] == 1
        for block in range(blocks):
            first = rims_ref[block].astype(jnp.float32)
            last = pltpu.roll(first, LANES - EDGE, 1)
            span = slice(fold + block * size, fold + (block + 1) * size)
            out_a[span, :] = jnp.where(even, last, first).astype(jnp.bfloat16)
            out_b[span, :] = jnp.where(even, first, last).astype(jnp.bfloat16)


def second_edges(even, slots, picks, arrived, rows, rims, after, blocks):
    packed = jax.ShapeDtypeStruct((folded_rows(rows) + blocks * rims, LANES), jnp.bfloat16)
    return pl.pallas_call(
        second_edges_kernel,
        in_specs=[SMEM, SMEM, VMEM] + [ANY] * (len(arrived) + 1),
        out_specs=[VMEM] * 3,
        scratch_shapes=[
            pltpu.VMEM((blocks, rims or 16, LANES), jnp.bfloat16),
            pltpu.SemaphoreType.DMA((blocks,)),
            pltpu.SemaphoreType.DMA((blocks,)),
        ],
        out_shape=[jax.ShapeDtypeStruct((blocks, rows, LANES), jnp.bfloat16), packed, packed],
        cost_estimate=NO_COST,
        compiler_params=PARAMS,
        name="second_edges",
    )(even, slots, picks, *arrived, after)


def swap_edges(packed):
    count = lax.axis_size("shot")
    got = []
    for first, edges in enumerate(packed):
        pairs = []
        for low in range(first, count - 1, 2):
            pairs += [(low, low + 1), (low + 1, low)]
        got.append(lax.ppermute(edges, "shot", pairs))
    return got


def filter_window(pieces, merged, fans_ref, mats, times_ref, rows, give, finish):
    own_ref, halo_ref = mats
    blocks, fan_pairs = halo_ref.shape[:2]
    tall = fans_ref.shape[1]
    count, width = segment_plan(rows)
    covered = 0
    for at, size, _ in list(pieces) + [(tall, 0, None)]:
        if at > covered:
            fans_ref[:, covered:at, :] = jnp.zeros(
                (fans_ref.shape[0], at - covered, fans_ref.shape[2]), jnp.bfloat16
            )
        covered = at + size
    def do_pair(pair, carry):
        for half in range(2):
            block = 2 * pair + half
            cols = slice(half * LANES, (half + 1) * LANES)
            for at, size, load in pieces:
                lhs = jnp.concatenate([load(block), merged[at : at + size, :]], axis=1)
                for fan_pair in range(fan_pairs):
                    rhs = jnp.concatenate([own_ref[fan_pair], halo_ref[block, fan_pair]], axis=0)
                    both = jnp.dot(lhs, rhs, preferred_element_type=jnp.float32).astype(
                        jnp.bfloat16
                    )
                    fans_ref[2 * fan_pair, at : at + size, cols] = both[:, :LANES]
                    fans_ref[2 * fan_pair + 1, at : at + size, cols] = both[:, LANES:]
        for step in range(count):
            start = min(step * width, rows - width)
            total = None
            for fan in range(2 * fan_pairs):
                part = jnp.dot(
                    times_ref[:width, fan * SPAN : (fan + 1) * SPAN],
                    fans_ref[fan, start : start + SPAN, :],
                    preferred_element_type=jnp.float32,
                )
                total = part if total is None else total + part
            give(pair, start, total)
        finish(pair)
        return carry

    lax.fori_loop(0, blocks // 2, do_pair, 0)


def first_kernel(
    start, sizes, noted, owners, me_ref, target_ref, x_ref, edge_a, edge_b, own_ref, halo_ref,
    times_ref, *refs
):
    outs = refs[-8 - owners * len(sizes) : -8]
    merged, fans_ref, done, note, rims, sem, note_sem, rim_sem = refs[-8:]
    blocks, rows = done.shape[:2]
    samples = x_ref.shape[1]
    window = start - REACH // 2
    begin, end = max(0, window), min(samples, start + rows + REACH // 2)
    homes, order = ranks([target_ref[block] for block in range(blocks)], blocks)
    groups, at = [], 0
    for group, size in enumerate(sizes):
        groups.append((at, size, outs[group * owners : (group + 1) * owners]))
        at += size

    def tell(offset):
        return pltpu.make_async_copy(
            note, groups[0][2][offset].at[0, pl.ds(sizes[0], NOTE), :], note_sem.at[offset]
        )

    if noted:
        lane = lax.broadcasted_iota(jnp.int32, note.shape, 1)
        row = jnp.zeros(note.shape, jnp.int32)
        for block in range(blocks):
            row = jnp.where(lane == block, target_ref[block], row)
        note[...] = row.astype(jnp.float32).astype(jnp.bfloat16)
        for offset in range(owners):
            tell(offset).start()

    def put(row, values):
        merged[row - window : row - window + values.shape[0], :] = values

    unpack_edges((edge_a, edge_b), samples, blocks, begin, end, put)

    def give(pair, at, values):
        values = values.astype(jnp.bfloat16)
        for half in range(2):
            done[2 * pair + half, at : at + values.shape[0], :] = values[
                :, half * LANES : (half + 1) * LANES
            ]

    def pick(values, pair, half):
        value = values[half]
        for other in range(1, blocks // 2):
            value = jnp.where(pair == other, values[2 * other + half], value)
        return value

    def pack_rim(block):
        at, size, _ = groups[-1]
        trace = lax.broadcasted_iota(jnp.int32, (LANES, LANES), 0)
        lane = lax.broadcasted_iota(jnp.int32, (LANES, LANES), 1)
        wanted = jnp.where(lane < EDGE, lane, lane + LANES - 2 * EDGE)
        chosen = jnp.where((lane < 2 * EDGE) & (trace == wanted), 1.0, 0.0).astype(jnp.bfloat16)
        found = jnp.dot(done[block, at : at + size, :], chosen, preferred_element_type=jnp.float32)
        fold, total = rims.shape[1], None
        for part in range(-(-size // fold)):
            piece = found[part * fold : (part + 1) * fold]
            if piece.shape[0] < fold:
                rest = jnp.zeros((fold - piece.shape[0], LANES), jnp.float32)
                piece = jnp.concatenate([piece, rest], axis=0)
            if part:
                piece = pltpu.roll(piece, 2 * EDGE * part, 1)
            total = piece if total is None else total + piece
        rims[block] = total.astype(jnp.bfloat16)

    rim_group = None if noted else len(groups) - 2

    def finish(pair):
        for half in range(2):
            block = 2 * pair + half
            if not noted:
                pack_rim(block)
            owner, rank = pick(homes, pair, half), pick(order, pair, half)
            away = lax.rem(owner - me_ref[0] + owners, owners)
            for group, (at, size, arrays) in enumerate(groups):
                part = done.at[block, pl.ds(at, size), :]
                for offset, out_ref in enumerate(arrays):

                    @pl.when(away == offset)
                    def _():
                        pltpu.make_async_copy(
                            part, out_ref.at[rank, pl.ds(0, size), :], sem.at[group, block]
                        ).start()
                        if group == rim_group:
                            pltpu.make_async_copy(
                                rims.at[block],
                                out_ref.at[rank, pl.ds(size, rims.shape[1]), :],
                                rim_sem.at[block],
                            ).start()

    pieces = [(begin - window, end - begin, lambda block: x_ref[block, begin:end, :])]
    filter_window(pieces, merged, fans_ref, (own_ref, halo_ref), times_ref, rows, give, finish)
    for group, (at, size, arrays) in enumerate(groups):
        for block in range(blocks):
            pltpu.make_async_copy(
                done.at[block, pl.ds(at, size), :],
                arrays[0].at[0, pl.ds(0, size), :],
                sem.at[group, block],
            ).wait()
    if noted:
        for offset in range(owners):
            tell(offset).wait()
    else:
        _, size, arrays = groups[rim_group]
        for block in range(blocks):
            pltpu.make_async_copy(
                rims.at[block],
                arrays[0].at[0, pl.ds(size, rims.shape[1]), :],
                rim_sem.at[block],
            ).wait()


def first_pass(me, target, owners, traces, edges, mats, times, after, start, sizes, noted):
    blocks = traces.shape[0]
    fans = 2 * mats[1].shape[1]
    rows = sum(sizes)
    tall = window_rows(rows)
    shapes = []
    for group, size in enumerate(sizes):
        size += NOTE if noted else rim_rows(sizes[-1]) if group == len(sizes) - 2 else 0
        shapes += [jax.ShapeDtypeStruct((blocks // 2, size, LANES), jnp.bfloat16)] * owners
    flat = pl.pallas_call(
        functools.partial(first_kernel, start, sizes, noted, owners),
        in_specs=[SMEM, SMEM] + [VMEM] * 6 + [ANY] * len(after),
        out_specs=[ANY] * len(shapes),
        scratch_shapes=[
            pltpu.VMEM((tall, LANES), jnp.bfloat16),
            pltpu.VMEM((fans, tall, 2 * LANES), jnp.bfloat16),
            pltpu.VMEM((blocks, rows, LANES), jnp.bfloat16),
            pltpu.VMEM((NOTE, LANES), jnp.bfloat16),
            pltpu.VMEM((blocks, rim_rows(sizes[-1]), LANES), jnp.bfloat16),
            pltpu.SemaphoreType.DMA((len(sizes), blocks)),
            pltpu.SemaphoreType.DMA((owners,)),
            pltpu.SemaphoreType.DMA((blocks,)),
        ],
        out_shape=shapes,
        cost_estimate=NO_COST,
        compiler_params=PARAMS,
        name="first_pass",
    )(me, target, traces, *edges, *mats, times, *after)
    return [flat[group * owners : (group + 1) * owners] for group in range(len(sizes))]


def second_kernel(at, has_past, *refs):
    refs = list(refs)
    take = lambda: refs.pop(0)
    past = [take() for _ in range(3)] if has_past else None
    now = [take() for _ in range(3)]
    own_ref, halo_ref, times_ref, _ = take(), take(), take(), take()
    if has_past:
        take()
    out_ref, token_ref, merged, fans_ref, done, sem = refs
    token_ref[...] = jnp.zeros_like(token_ref)
    blocks, rows = done.shape[:2]
    lead = REACH if has_past else REACH // 2
    pieces = []

    def put(origin):
        def store(row, values):
            merged[row - origin : row - origin + values.shape[0], :] = values

        return store

    if has_past:
        held = past[0].shape[1]
        unpack_edges(past[1:], held, blocks, held - REACH, held, put(held - REACH))
        pieces.append((0, REACH, lambda block: past[0][block, held - REACH :, :]))
    size = now[0].shape[1]
    unpack_edges(now[1:], size, blocks, 0, size, put(-lead))
    pieces.append((lead, size, lambda block: now[0][block]))

    def copy(block):
        return pltpu.make_async_copy(
            done.at[block], out_ref.at[block, pl.ds(at, rows), :], sem.at[block]
        )

    def give(pair, start, values):
        for half in range(2):
            done[2 * pair + half, start : start + values.shape[0], :] = values[
                :, half * LANES : (half + 1) * LANES
            ]

    def finish(pair):
        for half in range(2):
            copy(2 * pair + half).start()

    filter_window(pieces, merged, fans_ref, (own_ref, halo_ref), times_ref, rows, give, finish)
    for block in range(blocks):
        copy(block).wait()


def second_pass(blocks, samples, past, now, mats, times, after, out, at, rows):
    fans = 2 * mats[1].shape[1]
    tall = window_rows(rows)
    operands = [*(past or ()), *now, *mats, times, after]
    specs = [VMEM] * (len(operands) - 1) + [ANY]
    aliases = {}
    if out is not None:
        specs.append(ANY)
        operands.append(out)
        aliases = {len(operands) - 1: 0}
    return pl.pallas_call(
        functools.partial(second_kernel, at, past is not None),
        in_specs=specs,
        out_specs=[ANY, VMEM],
        scratch_shapes=[
            pltpu.VMEM((tall, LANES), jnp.bfloat16),
            pltpu.VMEM((fans, tall, 2 * LANES), jnp.bfloat16),
            pltpu.VMEM((blocks, rows, LANES), jnp.float32),
            pltpu.SemaphoreType.DMA((blocks,)),
        ],
        out_shape=[
            jax.ShapeDtypeStruct((blocks, samples, LANES), jnp.float32),
            jax.ShapeDtypeStruct((8, LANES), jnp.float32),
        ],
        input_output_aliases=aliases,
        cost_estimate=NO_COST,
        compiler_params=PARAMS,
        name="second_pass",
    )(*operands)


def last_kernel(
    at, slot_ref, past_ref, edge_a, edge_b, own_ref, halo_ref, times_ref, _, *refs
):
    parts, (out_ref, merged, fans_ref, held, done, in_sem, sem) = refs[:-7], refs[-7:]
    blocks, rows = done.shape[:2]
    before, size = past_ref.shape[1], held.shape[1]
    begin, wait = gather_rows(slot_ref, parts, held, in_sem, 0)
    begin()
    origin = before - REACH

    def put(row, values):
        merged[row - origin : row - origin + values.shape[0], :] = values

    unpack_edges((edge_a, edge_b), before, blocks, origin, before, put)
    fold, base = rim_rows(size), folded_rows(before)
    for part in range(-(-size // fold)):
        count = min(fold, size - part * fold)
        lane = lax.broadcasted_iota(jnp.int32, (count, LANES), 1)
        total = jnp.zeros((count, LANES), jnp.float32)
        for way, edge in enumerate((edge_a, edge_b)):
            for block in range(blocks):
                to = EDGE * (way * blocks + block)
                top = base + block * fold
                piece = edge[top : top + count, :].astype(jnp.float32)
                shift = (to - 2 * EDGE * part) % LANES
                piece = pltpu.roll(piece, shift, 1) if shift else piece
                total = jnp.where((lane >= to) & (lane < to + EDGE), piece, total)
        row = REACH + part * fold
        merged[row : row + count, :] = total.astype(jnp.bfloat16)
    wait()

    def copy(block):
        return pltpu.make_async_copy(
            done.at[block], out_ref.at[block, pl.ds(at, rows), :], sem.at[block]
        )

    def give(pair, start, values):
        for half in range(2):
            done[2 * pair + half, start : start + values.shape[0], :] = values[
                :, half * LANES : (half + 1) * LANES
            ]

    def finish(pair):
        for half in range(2):
            copy(2 * pair + half).start()

    pieces = [
        (0, REACH, lambda block: past_ref[block, origin:, :]),
        (REACH, size, lambda block: held[block]),
    ]
    filter_window(pieces, merged, fans_ref, (own_ref, halo_ref), times_ref, rows, give, finish)
    for block in range(blocks):
        copy(block).wait()


def last_pass(slots, past, parts, size, mats, times, out, at, rows):
    blocks, samples, _ = out.shape
    fans = 2 * mats[1].shape[1]
    tall = window_rows(rows)
    return pl.pallas_call(
        functools.partial(last_kernel, at),
        in_specs=[SMEM] + [VMEM] * 6 + [ANY] * (1 + len(parts)),
        out_specs=ANY,
        scratch_shapes=[
            pltpu.VMEM((tall, LANES), jnp.bfloat16),
            pltpu.VMEM((fans, tall, 2 * LANES), jnp.bfloat16),
            pltpu.VMEM((blocks, size, LANES), jnp.bfloat16),
            pltpu.VMEM((blocks, rows, LANES), jnp.float32),
            pltpu.SemaphoreType.DMA((blocks,)),
            pltpu.SemaphoreType.DMA((blocks,)),
        ],
        out_shape=jax.ShapeDtypeStruct(out.shape, jnp.float32),
        input_output_aliases={7: 0},
        cost_estimate=NO_COST,
        compiler_params=PARAMS,
        name="last_pass",
    )(slots, *past, *mats, times, out, *parts)


def per_device(
    traces, first_trace_taps, first_time_taps, second_trace_taps, second_time_taps, dest_row
):
    blocks, samples, _ = traces.shape
    owners = lax.axis_size("rcv")
    me = lax.axis_index("rcv").astype(jnp.int32).reshape(1)
    even = (1 - lax.axis_index("shot") % 2).astype(jnp.int32).reshape(1)
    target = dest_row.reshape(blocks)

    def send(values, offset):
        pairs = [(i, (i + offset) % owners) for i in range(owners)]
        return lax.ppermute(values, "rcv", pairs) if offset else values

    bounds = chunk_bounds(samples)
    count = len(bounds) - 1
    sizes = [bounds[step + 1] - bounds[step] for step in range(count)]
    *packed, picks = first_edges(even, traces)
    edges = swap_edges(packed)
    *mats, times = weights(even, first_trace_taps, first_time_taps, traces, blocks)

    def first(after, start, sizes, noted):
        return first_pass(
            me, target, owners, traces, edges, mats, times, after, start, sizes, noted
        )

    def exchange(sent, before, *after):
        arrived = []
        for offset, part in enumerate(sent):
            if offset and before is not None:
                part, before[offset], *_ = lax.optimization_barrier(
                    (part, before[offset], *after)
                )
            arrived.append(send(part, offset))
        return arrived

    sent = first([], 0, sizes[:1], True)
    arrived = [exchange(sent[0], None)]
    sent += first([sent[0][0]], bounds[1], sizes[1:], False)
    *second_mats, second_times, slots = late_weights(
        even, me, target, second_trace_taps, second_time_taps, arrived[0], sent[-1][0]
    )

    out, past, now, token, rims = None, None, None, None, None

    def second(step, after):
        at = max(0, bounds[step] - REACH // 2)
        stop = bounds[step + 1] - REACH // 2 if step + 1 < count else samples
        return second_pass(
            blocks, samples, past, now, second_mats, second_times, after, out, at, stop - at
        )

    for step in range(count - 1):
        ahead = [*now[1:]] if now else []
        ahead += [token] if token is not None else []
        arrived.append(exchange(sent[step + 1], arrived[step], *ahead))
        gathered, *packed = second_edges(
            even,
            slots,
            picks,
            arrived[step],
            sizes[step],
            rim_rows(sizes[-1]) if step == count - 2 else 0,
            slots if token is None else token,
            blocks,
        )
        rims = packed[0]
        coming = (gathered, *swap_edges(packed))
        if step:
            out, token = second(step - 1, rims)
            past = now
        now = coming
    out, token = second(count - 2, slots)
    at = bounds[count - 1] - REACH // 2
    return last_pass(
        slots, now, arrived[-1], sizes[-1], second_mats, second_times, out, at, samples - at
    )


def solution(mesh):
    in_specs = (P("rcv", None, "shot"), P(), P(), P(), P(), P("rcv", "shot"))
    out_specs = P("rcv", None, "shot")
    return jax.shard_map(
        per_device, mesh=mesh, in_specs=in_specs, out_specs=out_specs, check_vma=False
    )
```

```python
import functools

import jax
import jax.numpy as jnp
from jax import lax
from jax.experimental import pallas as pl
from jax.experimental.pallas import tpu as pltpu
from jax.sharding import PartitionSpec as P

LANES = 128
EDGE = 8
SPAN = 256
REACH = 64
WIDE = SPAN - REACH
FOLD = 4
PARAMS = pltpu.CompilerParams(vmem_limit_bytes=16 * 2**20)
NO_COST = pl.CostEstimate(flops=1, bytes_accessed=1, transcendentals=0)
VMEM = pl.BlockSpec(memory_space=pltpu.VMEM)
SMEM = pl.BlockSpec(memory_space=pltpu.SMEM)
ANY = pl.BlockSpec(memory_space=pl.ANY)
HBM = pl.BlockSpec(memory_space=pltpu.HBM)
CHUNKS = (384, 576, 576)
RIM_FOLD = 8
NOTE = 16


def chunk_bounds(samples):
    bounds = [0]
    for size in CHUNKS:
        if bounds[-1] + size + REACH <= samples:
            bounds.append(bounds[-1] + size)
    bounds.append(samples)
    return bounds


def segment_plan(rows):
    count = -(-rows // WIDE)
    width = min(WIDE, -(-rows // (16 * count)) * 16)
    return count, width


def window_rows(rows):
    return rows - segment_plan(rows)[1] + SPAN


def folded_rows(rows):
    return -(-rows // (16 * FOLD)) * 16


def rim_rows(rows):
    return -(-rows // (16 * RIM_FOLD)) * 16


def place_taps(taps_ref, origin, step):
    width = taps_ref.shape[1]
    tap = lax.broadcasted_iota(jnp.int32, (width, SPAN), 0)
    at = lax.broadcasted_iota(jnp.int32, (width, SPAN), 1)
    spread = jnp.where(at == (origin + step * tap + SPAN) % SPAN, 1.0, 0.0).astype(jnp.bfloat16)
    return jnp.dot(taps_ref[...], spread, preferred_element_type=jnp.float32)


def fill_weights(even, trace_ref, time_ref, mats_ref, times_ref):
    fans = trace_ref.shape[0]
    blocks = mats_ref.shape[0]
    trace_rows = place_taps(trace_ref, trace_ref.shape[1] // 2, -1)
    time_rows = place_taps(time_ref, 0, 1)
    for fan in range(fans):
        row = jnp.broadcast_to(trace_rows[fan : fan + 1, :], (LANES, SPAN))
        own = pltpu.roll(row, 0, 1, stride=1, stride_axis=0)[:, :LANES]
        left = pltpu.roll(row[:EDGE], SPAN - EDGE, 1, stride=1, stride_axis=0)[:, :LANES]
        right = pltpu.roll(row[:EDGE], LANES, 1, stride=1, stride_axis=0)[:, :LANES]
        pieces = (jnp.where(even, right, left), jnp.where(even, left, right))
        pair, half = fan // 2, fan % 2
        cols = slice(half * LANES, (half + 1) * LANES)
        for block in range(blocks):
            before, after = EDGE * block, EDGE * (blocks - 1 - block)
            parts = []
            for piece in pieces:
                if before:
                    parts.append(jnp.zeros((before, LANES), jnp.float32))
                parts.append(piece)
                if after:
                    parts.append(jnp.zeros((after, LANES), jnp.float32))
            parts.append(jnp.zeros((LANES - 2 * EDGE * blocks, LANES), jnp.float32))
            mats_ref[block, pair, :LANES, cols] = own.astype(jnp.bfloat16)
            mats_ref[block, pair, LANES:, cols] = jnp.concatenate(parts, axis=0).astype(
                jnp.bfloat16
            )
        taps = jnp.broadcast_to(time_rows[fan : fan + 1, :], (WIDE, SPAN))
        times_ref[:, fan * SPAN : (fan + 1) * SPAN] = pltpu.roll(
            taps, 0, 1, stride=1, stride_axis=0
        ).astype(jnp.bfloat16)


def weights_kernel(even_ref, trace_ref, time_ref, _, mats_ref, times_ref):
    fill_weights(even_ref[0] == 1, trace_ref, time_ref, mats_ref, times_ref)


def ranks(targets, blocks):
    owners = [lax.div(target, blocks) for target in targets]
    order = []
    for block, owner in enumerate(owners):
        rank = jnp.int32(0)
        for other in owners[:block]:
            rank = rank + jnp.where(other == owner, 1, 0)
        order.append(rank)
    return owners, order


def late_kernel(even_ref, me_ref, target_ref, trace_ref, time_ref, *refs):
    parts, (_, mats_ref, times_ref, slots_ref, notes, sem) = refs[:-6], refs[-6:]
    blocks, me = mats_ref.shape[0], me_ref[0]
    slot_cap, held = parts[0].shape[0], parts[0].shape[1]

    def fetch(offset):
        return pltpu.make_async_copy(
            parts[offset].at[0, pl.ds(held - NOTE, NOTE), :], notes.at[offset], sem.at[offset]
        )

    for offset in range(1, len(parts)):
        fetch(offset).start()
    fill_weights(even_ref[0] == 1, trace_ref, time_ref, mats_ref, times_ref)
    slots = [jnp.int32(0)] * blocks
    lane = lax.broadcasted_iota(jnp.int32, (1, LANES), 1)
    for offset in range(len(parts)):
        if offset:
            fetch(offset).wait()
            note = notes[offset].astype(jnp.float32)[:1]
            targets = [
                jnp.sum(jnp.where(lane == block, note, 0.0)).astype(jnp.int32)
                for block in range(blocks)
            ]
        else:
            targets = [target_ref[block] for block in range(blocks)]
        for target, rank in zip(targets, ranks(targets, blocks)[1]):
            for block in range(blocks):
                slots[block] = jnp.where(
                    target == me * blocks + block, offset * slot_cap + rank, slots[block]
                )
    for block in range(blocks):
        slots_ref[block] = slots[block]


def weight_shapes(blocks, fans):
    return [
        jax.ShapeDtypeStruct((blocks, fans // 2, 2 * LANES, 2 * LANES), jnp.bfloat16),
        jax.ShapeDtypeStruct((WIDE, fans * SPAN), jnp.bfloat16),
    ]


def weights(even, trace_taps, time_taps, after, blocks):
    return pl.pallas_call(
        weights_kernel,
        in_specs=[SMEM, VMEM, VMEM, ANY],
        out_specs=[VMEM, VMEM],
        out_shape=weight_shapes(blocks, trace_taps.shape[0]),
        cost_estimate=NO_COST,
        compiler_params=PARAMS,
        name="weights",
    )(even, trace_taps, time_taps, after)


def late_weights(even, me, target, trace_taps, time_taps, arrived, after):
    blocks = target.shape[0]
    return pl.pallas_call(
        late_kernel,
        in_specs=[SMEM, SMEM, SMEM, VMEM, VMEM] + [ANY] * (len(arrived) + 1),
        out_specs=[VMEM, VMEM, SMEM],
        out_shape=weight_shapes(blocks, trace_taps.shape[0])
        + [jax.ShapeDtypeStruct((blocks,), jnp.int32)],
        scratch_shapes=[
            pltpu.VMEM((len(arrived), NOTE, LANES), jnp.bfloat16),
            pltpu.SemaphoreType.DMA((len(arrived),)),
        ],
        cost_estimate=NO_COST,
        compiler_params=PARAMS,
        name="late_weights",
    )(even, me, target, trace_taps, time_taps, *arrived, after)


def edge_picks(even, blocks):
    trace = lax.broadcasted_iota(jnp.int32, (2 * LANES, 2 * LANES), 0)
    lane = lax.broadcasted_iota(jnp.int32, (2 * LANES, 2 * LANES), 1)
    last = jnp.where(even, 1, 0)
    begin = jnp.where(lane < LANES, last, 1 - last) * (LANES - EDGE)
    lane = lane % LANES
    picks = []
    for pair in range(blocks // 2):
        at = lane - EDGE * (2 * pair + trace // LANES)
        pick = (at >= 0) & (at < EDGE) & (trace % LANES == at + begin)
        picks.append(jnp.where(pick, 1.0, 0.0).astype(jnp.bfloat16))
    return picks


def pick_part(picks, tiles_ref, start, stop):
    found = None
    for pair, pick in enumerate(picks):
        both = jnp.concatenate(
            [tiles_ref[2 * pair, start:stop, :], tiles_ref[2 * pair + 1, start:stop, :]], axis=1
        )
        one = jnp.dot(both, pick, preferred_element_type=jnp.float32)
        found = one if found is None else found + one
    return found


def pack_edges(picks, tiles_ref, packed_refs):
    blocks, rows = tiles_ref.shape[:2]
    fold = folded_rows(rows)
    totals = [None, None]
    for part in range(FOLD):
        start, stop = part * fold, min(rows, (part + 1) * fold)
        found = pick_part(picks, tiles_ref, start, stop)
        if stop - start < fold:
            found = jnp.concatenate(
                [found, jnp.zeros((fold - stop + start, 2 * LANES), jnp.float32)], axis=0
            )
        for way in range(2):
            piece = found[:, way * LANES : (way + 1) * LANES]
            if part:
                piece = pltpu.roll(piece, part * EDGE * blocks, 1)
            totals[way] = piece if totals[way] is None else totals[way] + piece
    for way in range(2):
        packed_refs[way][:fold, :] = totals[way].astype(jnp.bfloat16)


def unpack_edges(packed_refs, rows, blocks, start, stop, give):
    fold, width = folded_rows(rows), EDGE * blocks
    while start < stop:
        part = start // fold
        until = min(stop, (part + 1) * fold)
        pieces = []
        for way in range(2):
            piece = packed_refs[way][start - part * fold : until - part * fold, :]
            shift = (way - part) * width % LANES
            piece = piece.astype(jnp.float32)
            pieces.append(pltpu.roll(piece, shift, 1) if shift else piece)
        lane = lax.broadcasted_iota(jnp.int32, pieces[0].shape, 1)
        give(start, jnp.where(lane < width, pieces[0], pieces[1]).astype(jnp.bfloat16))
        start = until


def first_edges_kernel(even_ref, x_ref, out_a, out_b, picks_ref):
    blocks = x_ref.shape[0]
    picks = edge_picks(even_ref[0] == 1, blocks)
    for pair, pick in enumerate(picks):
        picks_ref[pair] = pick
    pack_edges(picks, x_ref, (out_a, out_b))


def first_edges(even, traces):
    blocks = traces.shape[0]
    packed = jax.ShapeDtypeStruct((folded_rows(traces.shape[1]), LANES), jnp.bfloat16)
    return pl.pallas_call(
        first_edges_kernel,
        in_specs=[SMEM, VMEM],
        out_specs=[VMEM] * 3,
        out_shape=[
            packed,
            packed,
            jax.ShapeDtypeStruct((blocks // 2, 2 * LANES, 2 * LANES), jnp.bfloat16),
        ],
        cost_estimate=NO_COST,
        compiler_params=PARAMS,
        name="first_edges",
    )(even, traces)


def gather_rows(slot_ref, parts, held_ref, sem, start):
    blocks, rows = held_ref.shape[:2]
    slot_cap = parts[0].shape[0]

    def begin():
        for block in range(blocks):
            slot = slot_ref[block]
            for offset, part in enumerate(parts):

                @pl.when(slot // slot_cap == offset)
                def _():
                    pltpu.make_async_copy(
                        part.at[slot % slot_cap, pl.ds(start, rows), :],
                        held_ref.at[block],
                        sem.at[block],
                    ).start()

    def wait():
        for block in range(blocks):
            pltpu.make_async_copy(
                parts[0].at[0, pl.ds(start, rows), :], held_ref.at[block], sem.at[block]
            ).wait()

    return begin, wait


def second_edges_kernel(even_ref, slot_ref, picks_ref, *refs):
    parts, (_, sorted_ref, out_a, out_b, rims_ref, sem, rim_sem) = refs[:-7], refs[-7:]
    blocks, rows = sorted_ref.shape[:2]
    begin, wait = gather_rows(slot_ref, parts, sorted_ref, sem, 0)
    begin()
    fold = folded_rows(rows)
    rimmed = out_a.shape[0] > fold
    if rimmed:
        rim_begin, rim_wait = gather_rows(slot_ref, parts, rims_ref, rim_sem, rows)
        rim_begin()
    wait()
    picks = [picks_ref[pair] for pair in range(blocks // 2)]
    pack_edges(picks, sorted_ref, (out_a, out_b))
    if rimmed:
        rim_wait()
        size = rims_ref.shape[1]
        even = even_ref[0] == 1
        lane = lax.broadcasted_iota(jnp.int32, (size, LANES), 1)
        low = lane % (2 * EDGE) < EDGE
        for pair in range(blocks // 2):
            one, two = (rims_ref[2 * pair + half].astype(jnp.float32) for half in range(2))
            first = jnp.where(low, one, pltpu.roll(two, EDGE, 1))
            last = jnp.where(low, pltpu.roll(one, LANES - EDGE, 1), two)
            span = slice(fold + pair * size, fold + (pair + 1) * size)
            out_a[span, :] = jnp.where(even, last, first).astype(jnp.bfloat16)
            out_b[span, :] = jnp.where(even, first, last).astype(jnp.bfloat16)


def second_edges(even, slots, picks, arrived, rows, rims, after, blocks):
    packed = jax.ShapeDtypeStruct((folded_rows(rows) + blocks // 2 * rims, LANES), jnp.bfloat16)
    return pl.pallas_call(
        second_edges_kernel,
        in_specs=[SMEM, SMEM, VMEM] + [ANY] * (len(arrived) + 1),
        out_specs=[VMEM] * 3,
        scratch_shapes=[
            pltpu.VMEM((blocks, rims or 16, LANES), jnp.bfloat16),
            pltpu.SemaphoreType.DMA((blocks,)),
            pltpu.SemaphoreType.DMA((blocks,)),
        ],
        out_shape=[jax.ShapeDtypeStruct((blocks, rows, LANES), jnp.bfloat16), packed, packed],
        cost_estimate=NO_COST,
        compiler_params=PARAMS,
        name="second_edges",
    )(even, slots, picks, *arrived, after)


def swap_edges(packed):
    count = lax.axis_size("shot")
    got = []
    for first, edges in enumerate(packed):
        pairs = []
        for low in range(first, count - 1, 2):
            pairs += [(low, low + 1), (low + 1, low)]
        got.append(lax.ppermute(edges, "shot", pairs))
    return got


def filter_window(pieces, merged, fans_ref, mats_ref, times_ref, rows, give, finish):
    fan_pairs = mats_ref.shape[1]
    blocks = mats_ref.shape[0]
    tall = fans_ref.shape[1]
    count, width = segment_plan(rows)
    covered = 0
    for at, size, _ in list(pieces) + [(tall, 0, None)]:
        if at > covered:
            fans_ref[:, covered:at, :] = jnp.zeros(
                (fans_ref.shape[0], at - covered, fans_ref.shape[2]), jnp.bfloat16
            )
        covered = at + size
    def do_pair(pair, carry):
        for half in range(2):
            block = 2 * pair + half
            cols = slice(half * LANES, (half + 1) * LANES)
            for at, size, load in pieces:
                lhs = jnp.concatenate([load(block), merged[at : at + size, :]], axis=1)
                for fan_pair in range(fan_pairs):
                    both = jnp.dot(
                        lhs, mats_ref[block, fan_pair], preferred_element_type=jnp.float32
                    ).astype(jnp.bfloat16)
                    fans_ref[2 * fan_pair, at : at + size, cols] = both[:, :LANES]
                    fans_ref[2 * fan_pair + 1, at : at + size, cols] = both[:, LANES:]
        for step in range(count):
            start = min(step * width, rows - width)
            total = None
            for fan in range(2 * fan_pairs):
                part = jnp.dot(
                    times_ref[:width, fan * SPAN : (fan + 1) * SPAN],
                    fans_ref[fan, start : start + SPAN, :],
                    preferred_element_type=jnp.float32,
                )
                total = part if total is None else total + part
            give(pair, start, total)
        finish(pair)
        return carry

    lax.fori_loop(0, blocks // 2, do_pair, 0)


def first_kernel(
    start, sizes, noted, owners, me_ref, target_ref, x_ref, edge_a, edge_b, mats_ref, times_ref,
    *refs
):
    outs = refs[-8 - owners * len(sizes) : -8]
    merged, fans_ref, done, note, rims, sem, note_sem, rim_sem = refs[-8:]
    blocks, rows = done.shape[:2]
    samples = x_ref.shape[1]
    window = start - REACH // 2
    begin, end = max(0, window), min(samples, start + rows + REACH // 2)
    homes, order = ranks([target_ref[block] for block in range(blocks)], blocks)
    groups, at = [], 0
    for group, size in enumerate(sizes):
        groups.append((at, size, outs[group * owners : (group + 1) * owners]))
        at += size

    def tell(offset):
        return pltpu.make_async_copy(
            note, groups[0][2][offset].at[0, pl.ds(sizes[0], NOTE), :], note_sem.at[offset]
        )

    if noted:
        lane = lax.broadcasted_iota(jnp.int32, note.shape, 1)
        row = jnp.zeros(note.shape, jnp.int32)
        for block in range(blocks):
            row = jnp.where(lane == block, target_ref[block], row)
        note[...] = row.astype(jnp.float32).astype(jnp.bfloat16)
        for offset in range(owners):
            tell(offset).start()

    def put(row, values):
        merged[row - window : row - window + values.shape[0], :] = values

    unpack_edges((edge_a, edge_b), samples, blocks, begin, end, put)

    def give(pair, at, values):
        values = values.astype(jnp.bfloat16)
        for half in range(2):
            done[2 * pair + half, at : at + values.shape[0], :] = values[
                :, half * LANES : (half + 1) * LANES
            ]

    def pick(values, pair, half):
        value = values[half]
        for other in range(1, blocks // 2):
            value = jnp.where(pair == other, values[2 * other + half], value)
        return value

    def pack_rim(block):
        at, size, _ = groups[-1]
        trace = lax.broadcasted_iota(jnp.int32, (LANES, LANES), 0)
        lane = lax.broadcasted_iota(jnp.int32, (LANES, LANES), 1)
        wanted = jnp.where(lane < EDGE, lane, lane + LANES - 2 * EDGE)
        chosen = jnp.where((lane < 2 * EDGE) & (trace == wanted), 1.0, 0.0).astype(jnp.bfloat16)
        found = jnp.dot(done[block, at : at + size, :], chosen, preferred_element_type=jnp.float32)
        fold, total = rims.shape[1], None
        for part in range(-(-size // fold)):
            piece = found[part * fold : (part + 1) * fold]
            if piece.shape[0] < fold:
                rest = jnp.zeros((fold - piece.shape[0], LANES), jnp.float32)
                piece = jnp.concatenate([piece, rest], axis=0)
            if part:
                piece = pltpu.roll(piece, 2 * EDGE * part, 1)
            total = piece if total is None else total + piece
        rims[block] = total.astype(jnp.bfloat16)

    rim_group = None if noted else len(groups) - 2

    def finish(pair):
        for half in range(2):
            block = 2 * pair + half
            if not noted:
                pack_rim(block)
            owner, rank = pick(homes, pair, half), pick(order, pair, half)
            away = lax.rem(owner - me_ref[0] + owners, owners)
            for group, (at, size, arrays) in enumerate(groups):
                part = done.at[block, pl.ds(at, size), :]
                for offset, out_ref in enumerate(arrays):

                    @pl.when(away == offset)
                    def _():
                        pltpu.make_async_copy(
                            part, out_ref.at[rank, pl.ds(0, size), :], sem.at[group, block]
                        ).start()
                        if group == rim_group:
                            pltpu.make_async_copy(
                                rims.at[block],
                                out_ref.at[rank, pl.ds(size, rims.shape[1]), :],
                                rim_sem.at[block],
                            ).start()

    pieces = [(begin - window, end - begin, lambda block: x_ref[block, begin:end, :])]
    filter_window(pieces, merged, fans_ref, mats_ref, times_ref, rows, give, finish)
    for group, (at, size, arrays) in enumerate(groups):
        for block in range(blocks):
            pltpu.make_async_copy(
                done.at[block, pl.ds(at, size), :],
                arrays[0].at[0, pl.ds(0, size), :],
                sem.at[group, block],
            ).wait()
    if noted:
        for offset in range(owners):
            tell(offset).wait()
    else:
        _, size, arrays = groups[rim_group]
        for block in range(blocks):
            pltpu.make_async_copy(
                rims.at[block],
                arrays[0].at[0, pl.ds(size, rims.shape[1]), :],
                rim_sem.at[block],
            ).wait()


def first_pass(me, target, owners, traces, edges, mats, times, after, start, sizes, noted):
    blocks = traces.shape[0]
    fans = 2 * mats.shape[1]
    rows = sum(sizes)
    tall = window_rows(rows)
    shapes = []
    for group, size in enumerate(sizes):
        size += NOTE if noted else rim_rows(sizes[-1]) if group == len(sizes) - 2 else 0
        shapes += [jax.ShapeDtypeStruct((blocks // 2, size, LANES), jnp.bfloat16)] * owners
    flat = pl.pallas_call(
        functools.partial(first_kernel, start, sizes, noted, owners),
        in_specs=[SMEM, SMEM] + [VMEM] * 5 + [ANY] * len(after),
        out_specs=[ANY] * len(shapes),
        scratch_shapes=[
            pltpu.VMEM((tall, LANES), jnp.bfloat16),
            pltpu.VMEM((fans, tall, 2 * LANES), jnp.bfloat16),
            pltpu.VMEM((blocks, rows, LANES), jnp.bfloat16),
            pltpu.VMEM((NOTE, LANES), jnp.bfloat16),
            pltpu.VMEM((blocks, rim_rows(sizes[-1]), LANES), jnp.bfloat16),
            pltpu.SemaphoreType.DMA((len(sizes), blocks)),
            pltpu.SemaphoreType.DMA((owners,)),
            pltpu.SemaphoreType.DMA((blocks,)),
        ],
        out_shape=shapes,
        cost_estimate=NO_COST,
        compiler_params=PARAMS,
        name="first_pass",
    )(me, target, traces, *edges, mats, times, *after)
    return [flat[group * owners : (group + 1) * owners] for group in range(len(sizes))]


def second_kernel(at, has_past, *refs):
    refs = list(refs)
    take = lambda: refs.pop(0)
    past = [take() for _ in range(3)] if has_past else None
    now = [take() for _ in range(3)]
    mats_ref, times_ref, _ = take(), take(), take()
    if has_past:
        take()
    out_ref, token_ref, merged, fans_ref, done, sem = refs
    token_ref[...] = jnp.zeros_like(token_ref)
    blocks, rows = done.shape[:2]
    lead = REACH if has_past else REACH // 2
    pieces = []

    def put(origin):
        def store(row, values):
            merged[row - origin : row - origin + values.shape[0], :] = values

        return store

    if has_past:
        held = past[0].shape[1]
        unpack_edges(past[1:], held, blocks, held - REACH, held, put(held - REACH))
        pieces.append((0, REACH, lambda block: past[0][block, held - REACH :, :]))
    size = now[0].shape[1]
    unpack_edges(now[1:], size, blocks, 0, size, put(-lead))
    pieces.append((lead, size, lambda block: now[0][block]))

    def copy(block):
        return pltpu.make_async_copy(
            done.at[block], out_ref.at[block, pl.ds(at, rows), :], sem.at[block]
        )

    def give(pair, start, values):
        for half in range(2):
            done[2 * pair + half, start : start + values.shape[0], :] = values[
                :, half * LANES : (half + 1) * LANES
            ]

    def finish(pair):
        for half in range(2):
            copy(2 * pair + half).start()

    filter_window(pieces, merged, fans_ref, mats_ref, times_ref, rows, give, finish)
    for block in range(blocks):
        copy(block).wait()


def second_pass(blocks, samples, past, now, mats, times, after, out, at, rows):
    fans = 2 * mats.shape[1]
    tall = window_rows(rows)
    operands = [*(past or ()), *now, mats, times, after]
    specs = [VMEM] * (len(operands) - 1) + [ANY]
    aliases = {}
    if out is not None:
        specs.append(ANY)
        operands.append(out)
        aliases = {len(operands) - 1: 0}
    return pl.pallas_call(
        functools.partial(second_kernel, at, past is not None),
        in_specs=specs,
        out_specs=[ANY, VMEM],
        scratch_shapes=[
            pltpu.VMEM((tall, LANES), jnp.bfloat16),
            pltpu.VMEM((fans, tall, 2 * LANES), jnp.bfloat16),
            pltpu.VMEM((blocks, rows, LANES), jnp.float32),
            pltpu.SemaphoreType.DMA((blocks,)),
        ],
        out_shape=[
            jax.ShapeDtypeStruct((blocks, samples, LANES), jnp.float32),
            jax.ShapeDtypeStruct((8, LANES), jnp.float32),
        ],
        input_output_aliases=aliases,
        cost_estimate=NO_COST,
        compiler_params=PARAMS,
        name="second_pass",
    )(*operands)


def last_kernel(
    at, slot_ref, past_ref, edge_a, edge_b, mats_ref, times_ref, _, *refs
):
    parts, (out_ref, merged, fans_ref, held, done, in_sem, sem) = refs[:-7], refs[-7:]
    blocks, rows = done.shape[:2]
    before, size = past_ref.shape[1], held.shape[1]
    begin, wait = gather_rows(slot_ref, parts, held, in_sem, 0)
    begin()
    origin = before - REACH

    def put(row, values):
        merged[row - origin : row - origin + values.shape[0], :] = values

    unpack_edges((edge_a, edge_b), before, blocks, origin, before, put)
    fold, base = rim_rows(size), folded_rows(before)
    for part in range(-(-size // fold)):
        count = min(fold, size - part * fold)
        lane = lax.broadcasted_iota(jnp.int32, (count, LANES), 1)
        total = jnp.zeros((count, LANES), jnp.float32)
        for way, edge in enumerate((edge_a, edge_b)):
            for block in range(blocks):
                to = EDGE * (way * blocks + block)
                top = base + block // 2 * fold
                piece = edge[top : top + count, :].astype(jnp.float32)
                shift = (to - EDGE * (2 * part + block % 2)) % LANES
                piece = pltpu.roll(piece, shift, 1) if shift else piece
                total = jnp.where((lane >= to) & (lane < to + EDGE), piece, total)
        row = REACH + part * fold
        merged[row : row + count, :] = total.astype(jnp.bfloat16)
    wait()

    def copy(block):
        return pltpu.make_async_copy(
            done.at[block], out_ref.at[block, pl.ds(at, rows), :], sem.at[block]
        )

    def give(pair, start, values):
        for half in range(2):
            done[2 * pair + half, start : start + values.shape[0], :] = values[
                :, half * LANES : (half + 1) * LANES
            ]

    def finish(pair):
        for half in range(2):
            copy(2 * pair + half).start()

    pieces = [
        (0, REACH, lambda block: past_ref[block, origin:, :]),
        (REACH, size, lambda block: held[block]),
    ]
    filter_window(pieces, merged, fans_ref, mats_ref, times_ref, rows, give, finish)
    for block in range(blocks):
        copy(block).wait()


def last_pass(slots, past, parts, size, mats, times, out, at, rows):
    blocks, samples, _ = out.shape
    fans = 2 * mats.shape[1]
    tall = window_rows(rows)
    return pl.pallas_call(
        functools.partial(last_kernel, at),
        in_specs=[SMEM] + [VMEM] * 5 + [ANY] * (1 + len(parts)),
        out_specs=ANY,
        scratch_shapes=[
            pltpu.VMEM((tall, LANES), jnp.bfloat16),
            pltpu.VMEM((fans, tall, 2 * LANES), jnp.bfloat16),
            pltpu.VMEM((blocks, size, LANES), jnp.bfloat16),
            pltpu.VMEM((blocks, rows, LANES), jnp.float32),
            pltpu.SemaphoreType.DMA((blocks,)),
            pltpu.SemaphoreType.DMA((blocks,)),
        ],
        out_shape=jax.ShapeDtypeStruct(out.shape, jnp.float32),
        input_output_aliases={6: 0},
        cost_estimate=NO_COST,
        compiler_params=PARAMS,
        name="last_pass",
    )(slots, *past, mats, times, out, *parts)


def per_device(
    traces, first_trace_taps, first_time_taps, second_trace_taps, second_time_taps, dest_row
):
    blocks, samples, _ = traces.shape
    owners = lax.axis_size("rcv")
    me = lax.axis_index("rcv").astype(jnp.int32).reshape(1)
    even = (1 - lax.axis_index("shot") % 2).astype(jnp.int32).reshape(1)
    target = dest_row.reshape(blocks)

    def send(values, offset):
        pairs = [(i, (i + offset) % owners) for i in range(owners)]
        return lax.ppermute(values, "rcv", pairs) if offset else values

    bounds = chunk_bounds(samples)
    count = len(bounds) - 1
    sizes = [bounds[step + 1] - bounds[step] for step in range(count)]
    *packed, picks = first_edges(even, traces)
    edges = swap_edges(packed)
    mats, times = weights(even, first_trace_taps, first_time_taps, traces, blocks)

    def first(after, start, sizes, noted):
        return first_pass(
            me, target, owners, traces, edges, mats, times, after, start, sizes, noted
        )

    def exchange(sent, before, *after):
        arrived = []
        for offset, part in enumerate(sent):
            if offset and before is not None:
                part, before[offset], *_ = lax.optimization_barrier(
                    (part, before[offset], *after)
                )
            arrived.append(send(part, offset))
        return arrived

    sent = first([], 0, sizes[:1], True)
    arrived = [exchange(sent[0], None)]
    sent += first([sent[0][0]], bounds[1], sizes[1:], False)
    second_mats, second_times, slots = late_weights(
        even, me, target, second_trace_taps, second_time_taps, arrived[0], sent[-1][0]
    )

    out, past, now, token, rims = None, None, None, None, None

    def second(step, after):
        at = max(0, bounds[step] - REACH // 2)
        stop = bounds[step + 1] - REACH // 2 if step + 1 < count else samples
        return second_pass(
            blocks, samples, past, now, second_mats, second_times, after, out, at, stop - at
        )

    for step in range(count - 1):
        ahead = [*now[1:]] if now else []
        ahead += [token] if token is not None else []
        arrived.append(exchange(sent[step + 1], arrived[step], *ahead))
        gathered, *packed = second_edges(
            even,
            slots,
            picks,
            arrived[step],
            sizes[step],
            rim_rows(sizes[-1]) if step == count - 2 else 0,
            slots if token is None else token,
            blocks,
        )
        rims = packed[0]
        coming = (gathered, *swap_edges(packed))
        if step:
            out, token = second(step - 1, rims)
            past = now
        now = coming
    out, token = second(count - 2, slots)
    at = bounds[count - 1] - REACH // 2
    return last_pass(
        slots, now, arrived[-1], sizes[-1], second_mats, second_times, out, at, samples - at
    )


def solution(mesh):
    in_specs = (P("rcv", None, "shot"), P(), P(), P(), P(), P("rcv", "shot"))
    out_specs = P("rcv", None, "shot")
    return jax.shard_map(
        per_device, mesh=mesh, in_specs=in_specs, out_specs=out_specs, check_vma=False
    )
```

```python
import functools

import jax
import jax.numpy as jnp
from jax import lax
from jax.experimental import pallas as pl
from jax.experimental.pallas import tpu as pltpu
from jax.sharding import PartitionSpec as P

LANES = 128
EDGE = 8
SPAN = 256
REACH = 64
WIDE = SPAN - REACH
FOLD = 4
PARAMS = pltpu.CompilerParams(vmem_limit_bytes=16 * 2**20)
NO_COST = pl.CostEstimate(flops=1, bytes_accessed=1, transcendentals=0)
VMEM = pl.BlockSpec(memory_space=pltpu.VMEM)
SMEM = pl.BlockSpec(memory_space=pltpu.SMEM)
ANY = pl.BlockSpec(memory_space=pl.ANY)
HBM = pl.BlockSpec(memory_space=pltpu.HBM)
CHUNKS = (384, 576, 576)
RIM_FOLD = 8
NOTE = 16


def chunk_bounds(samples):
    bounds = [0]
    for size in CHUNKS:
        if bounds[-1] + size + REACH <= samples:
            bounds.append(bounds[-1] + size)
    bounds.append(samples)
    return bounds


def segment_plan(rows):
    count = -(-rows // WIDE)
    width = min(WIDE, -(-rows // (16 * count)) * 16)
    return count, width


def window_rows(rows):
    return rows - segment_plan(rows)[1] + SPAN


def folded_rows(rows):
    return -(-rows // (16 * FOLD)) * 16


def rim_rows(rows):
    return -(-rows // (16 * RIM_FOLD)) * 16


def place_taps(taps_ref, origin, step):
    width = taps_ref.shape[1]
    tap = lax.broadcasted_iota(jnp.int32, (width, SPAN), 0)
    at = lax.broadcasted_iota(jnp.int32, (width, SPAN), 1)
    spread = jnp.where(at == (origin + step * tap + SPAN) % SPAN, 1.0, 0.0).astype(jnp.bfloat16)
    return jnp.dot(taps_ref[...], spread, preferred_element_type=jnp.float32)


def fill_weights(even, trace_ref, time_ref, mats_ref, times_ref):
    fans = trace_ref.shape[0]
    blocks = mats_ref.shape[0]
    trace_rows = place_taps(trace_ref, trace_ref.shape[1] // 2, -1)
    time_rows = place_taps(time_ref, 0, 1)
    for fan in range(fans):
        row = jnp.broadcast_to(trace_rows[fan : fan + 1, :], (LANES, SPAN))
        own = pltpu.roll(row, 0, 1, stride=1, stride_axis=0)[:, :LANES]
        left = pltpu.roll(row[:EDGE], SPAN - EDGE, 1, stride=1, stride_axis=0)[:, :LANES]
        right = pltpu.roll(row[:EDGE], LANES, 1, stride=1, stride_axis=0)[:, :LANES]
        pieces = (jnp.where(even, right, left), jnp.where(even, left, right))
        pair, half = fan // 2, fan % 2
        cols = slice(half * LANES, (half + 1) * LANES)
        for block in range(blocks):
            before, after = EDGE * block, EDGE * (blocks - 1 - block)
            parts = []
            for piece in pieces:
                if before:
                    parts.append(jnp.zeros((before, LANES), jnp.float32))
                parts.append(piece)
                if after:
                    parts.append(jnp.zeros((after, LANES), jnp.float32))
            parts.append(jnp.zeros((LANES - 2 * EDGE * blocks, LANES), jnp.float32))
            mats_ref[block, pair, :LANES, cols] = own.astype(jnp.bfloat16)
            mats_ref[block, pair, LANES:, cols] = jnp.concatenate(parts, axis=0).astype(
                jnp.bfloat16
            )
        taps = jnp.broadcast_to(time_rows[fan : fan + 1, :], (WIDE, SPAN))
        times_ref[:, fan * SPAN : (fan + 1) * SPAN] = pltpu.roll(
            taps, 0, 1, stride=1, stride_axis=0
        ).astype(jnp.bfloat16)


def weights_kernel(even_ref, trace_ref, time_ref, _, mats_ref, times_ref):
    fill_weights(even_ref[0] == 1, trace_ref, time_ref, mats_ref, times_ref)


def ranks(targets, blocks):
    owners = [lax.div(target, blocks) for target in targets]
    order = []
    for block, owner in enumerate(owners):
        rank = jnp.int32(0)
        for other in owners[:block]:
            rank = rank + jnp.where(other == owner, 1, 0)
        order.append(rank)
    return owners, order


def late_kernel(even_ref, me_ref, target_ref, trace_ref, time_ref, *refs):
    parts, (_, mats_ref, times_ref, slots_ref, notes, sem) = refs[:-6], refs[-6:]
    blocks, me = mats_ref.shape[0], me_ref[0]
    slot_cap, held = parts[0].shape[0], parts[0].shape[1]

    def fetch(offset):
        return pltpu.make_async_copy(
            parts[offset].at[0, pl.ds(held - NOTE, NOTE), :], notes.at[offset], sem.at[offset]
        )

    for offset in range(1, len(parts)):
        fetch(offset).start()
    fill_weights(even_ref[0] == 1, trace_ref, time_ref, mats_ref, times_ref)
    slots = [jnp.int32(0)] * blocks
    lane = lax.broadcasted_iota(jnp.int32, (1, LANES), 1)
    for offset in range(len(parts)):
        if offset:
            fetch(offset).wait()
            note = notes[offset].astype(jnp.float32)[:1]
            targets = [
                jnp.sum(jnp.where(lane == block, note, 0.0)).astype(jnp.int32)
                for block in range(blocks)
            ]
        else:
            targets = [target_ref[block] for block in range(blocks)]
        for target, rank in zip(targets, ranks(targets, blocks)[1]):
            for block in range(blocks):
                slots[block] = jnp.where(
                    target == me * blocks + block, offset * slot_cap + rank, slots[block]
                )
    for block in range(blocks):
        slots_ref[block] = slots[block]


def weight_shapes(blocks, fans):
    return [
        jax.ShapeDtypeStruct((blocks, fans // 2, 2 * LANES, 2 * LANES), jnp.bfloat16),
        jax.ShapeDtypeStruct((WIDE, fans * SPAN), jnp.bfloat16),
    ]


def weights(even, trace_taps, time_taps, after, blocks):
    return pl.pallas_call(
        weights_kernel,
        in_specs=[SMEM, VMEM, VMEM, ANY],
        out_specs=[VMEM, VMEM],
        out_shape=weight_shapes(blocks, trace_taps.shape[0]),
        cost_estimate=NO_COST,
        compiler_params=PARAMS,
        name="weights",
    )(even, trace_taps, time_taps, after)


def late_weights(even, me, target, trace_taps, time_taps, arrived, after):
    blocks = target.shape[0]
    return pl.pallas_call(
        late_kernel,
        in_specs=[SMEM, SMEM, SMEM, VMEM, VMEM] + [ANY] * (len(arrived) + 1),
        out_specs=[VMEM, VMEM, SMEM],
        out_shape=weight_shapes(blocks, trace_taps.shape[0])
        + [jax.ShapeDtypeStruct((blocks,), jnp.int32)],
        scratch_shapes=[
            pltpu.VMEM((len(arrived), NOTE, LANES), jnp.bfloat16),
            pltpu.SemaphoreType.DMA((len(arrived),)),
        ],
        cost_estimate=NO_COST,
        compiler_params=PARAMS,
        name="late_weights",
    )(even, me, target, trace_taps, time_taps, *arrived, after)


def edge_picks(even, blocks):
    trace = lax.broadcasted_iota(jnp.int32, (2 * LANES, 2 * LANES), 0)
    lane = lax.broadcasted_iota(jnp.int32, (2 * LANES, 2 * LANES), 1)
    last = jnp.where(even, 1, 0)
    begin = jnp.where(lane < LANES, last, 1 - last) * (LANES - EDGE)
    lane = lane % LANES
    picks = []
    for pair in range(blocks // 2):
        at = lane - EDGE * (2 * pair + trace // LANES)
        pick = (at >= 0) & (at < EDGE) & (trace % LANES == at + begin)
        picks.append(jnp.where(pick, 1.0, 0.0).astype(jnp.bfloat16))
    return picks


def pick_part(picks, tiles_ref, start, stop):
    found = None
    for pair, pick in enumerate(picks):
        both = jnp.concatenate(
            [tiles_ref[2 * pair, start:stop, :], tiles_ref[2 * pair + 1, start:stop, :]], axis=1
        )
        one = jnp.dot(both, pick, preferred_element_type=jnp.float32)
        found = one if found is None else found + one
    return found


def pack_edges(picks, tiles_ref, packed_refs):
    blocks, rows = tiles_ref.shape[:2]
    fold = folded_rows(rows)
    totals = [None, None]
    for part in range(FOLD):
        start, stop = part * fold, min(rows, (part + 1) * fold)
        found = pick_part(picks, tiles_ref, start, stop)
        if stop - start < fold:
            found = jnp.concatenate(
                [found, jnp.zeros((fold - stop + start, 2 * LANES), jnp.float32)], axis=0
            )
        for way in range(2):
            piece = found[:, way * LANES : (way + 1) * LANES]
            if part:
                piece = pltpu.roll(piece, part * EDGE * blocks, 1)
            totals[way] = piece if totals[way] is None else totals[way] + piece
    for way in range(2):
        packed_refs[way][:fold, :] = totals[way].astype(jnp.bfloat16)


def unpack_edges(packed_refs, rows, blocks, start, stop, give):
    fold, width = folded_rows(rows), EDGE * blocks
    while start < stop:
        part = start // fold
        until = min(stop, (part + 1) * fold)
        pieces = []
        for way in range(2):
            piece = packed_refs[way][start - part * fold : until - part * fold, :]
            shift = (way - part) * width % LANES
            piece = piece.astype(jnp.float32)
            pieces.append(pltpu.roll(piece, shift, 1) if shift else piece)
        lane = lax.broadcasted_iota(jnp.int32, pieces[0].shape, 1)
        give(start, jnp.where(lane < width, pieces[0], pieces[1]).astype(jnp.bfloat16))
        start = until


def first_edges_kernel(even_ref, x_ref, out_a, out_b, picks_ref):
    blocks = x_ref.shape[0]
    picks = edge_picks(even_ref[0] == 1, blocks)
    for pair, pick in enumerate(picks):
        picks_ref[pair] = pick
    pack_edges(picks, x_ref, (out_a, out_b))


def first_edges(even, traces):
    blocks = traces.shape[0]
    packed = jax.ShapeDtypeStruct((folded_rows(traces.shape[1]), LANES), jnp.bfloat16)
    return pl.pallas_call(
        first_edges_kernel,
        in_specs=[SMEM, VMEM],
        out_specs=[VMEM] * 3,
        out_shape=[
            packed,
            packed,
            jax.ShapeDtypeStruct((blocks // 2, 2 * LANES, 2 * LANES), jnp.bfloat16),
        ],
        cost_estimate=NO_COST,
        compiler_params=PARAMS,
        name="first_edges",
    )(even, traces)


def gather_rows(slot_ref, parts, held_ref, sem, start):
    blocks, rows = held_ref.shape[:2]
    slot_cap = parts[0].shape[0]

    def begin():
        for block in range(blocks):
            slot = slot_ref[block]
            for offset, part in enumerate(parts):

                @pl.when(slot // slot_cap == offset)
                def _():
                    pltpu.make_async_copy(
                        part.at[slot % slot_cap, pl.ds(start, rows), :],
                        held_ref.at[block],
                        sem.at[block],
                    ).start()

    def wait():
        for block in range(blocks):
            pltpu.make_async_copy(
                parts[0].at[0, pl.ds(start, rows), :], held_ref.at[block], sem.at[block]
            ).wait()

    return begin, wait


def second_edges_kernel(even_ref, slot_ref, picks_ref, *refs):
    parts, (_, sorted_ref, out_a, out_b, rims_ref, sem, rim_sem) = refs[:-7], refs[-7:]
    blocks, rows = sorted_ref.shape[:2]
    begin, wait = gather_rows(slot_ref, parts, sorted_ref, sem, 0)
    begin()
    fold = folded_rows(rows)
    rimmed = out_a.shape[0] > fold
    if rimmed:
        rim_begin, rim_wait = gather_rows(slot_ref, parts, rims_ref, rim_sem, rows)
        rim_begin()
    wait()
    picks = [picks_ref[pair] for pair in range(blocks // 2)]
    pack_edges(picks, sorted_ref, (out_a, out_b))
    if rimmed:
        rim_wait()
        size = rims_ref.shape[1]
        even = even_ref[0] == 1
        lane = lax.broadcasted_iota(jnp.int32, (size, LANES), 1)
        low = lane % (2 * EDGE) < EDGE
        for pair in range(blocks // 2):
            one, two = (rims_ref[2 * pair + half].astype(jnp.float32) for half in range(2))
            first = jnp.where(low, one, pltpu.roll(two, EDGE, 1))
            last = jnp.where(low, pltpu.roll(one, LANES - EDGE, 1), two)
            span = slice(fold + pair * size, fold + (pair + 1) * size)
            out_a[span, :] = jnp.where(even, last, first).astype(jnp.bfloat16)
            out_b[span, :] = jnp.where(even, first, last).astype(jnp.bfloat16)


def second_edges(even, slots, picks, arrived, rows, rims, after, blocks):
    packed = jax.ShapeDtypeStruct((folded_rows(rows) + blocks // 2 * rims, LANES), jnp.bfloat16)
    return pl.pallas_call(
        second_edges_kernel,
        in_specs=[SMEM, SMEM, VMEM] + [ANY] * (len(arrived) + 1),
        out_specs=[VMEM] * 3,
        scratch_shapes=[
            pltpu.VMEM((blocks, rims or 16, LANES), jnp.bfloat16),
            pltpu.SemaphoreType.DMA((blocks,)),
            pltpu.SemaphoreType.DMA((blocks,)),
        ],
        out_shape=[jax.ShapeDtypeStruct((blocks, rows, LANES), jnp.bfloat16), packed, packed],
        cost_estimate=NO_COST,
        compiler_params=PARAMS,
        name="second_edges",
    )(even, slots, picks, *arrived, after)


def swap_edges(packed):
    count = lax.axis_size("shot")
    got = []
    for first, edges in enumerate(packed):
        pairs = []
        for low in range(first, count - 1, 2):
            pairs += [(low, low + 1), (low + 1, low)]
        got.append(lax.ppermute(edges, "shot", pairs))
    return got


def filter_window(pieces, merged, fans_ref, mats_ref, times_ref, rows, give, finish):
    fan_pairs = mats_ref.shape[1]
    blocks = mats_ref.shape[0]
    tall = fans_ref.shape[1]
    count, width = segment_plan(rows)
    covered = 0
    for at, size, _ in list(pieces) + [(tall, 0, None)]:
        if at > covered:
            fans_ref[:, covered:at, :] = jnp.zeros(
                (fans_ref.shape[0], at - covered, fans_ref.shape[2]), jnp.bfloat16
            )
        covered = at + size
    def do_pair(pair, carry):
        for half in range(2):
            block = 2 * pair + half
            cols = slice(half * LANES, (half + 1) * LANES)
            for at, size, load in pieces:
                lhs = jnp.concatenate([load(block), merged[at : at + size, :]], axis=1)
                for fan_pair in range(fan_pairs):
                    both = jnp.dot(
                        lhs, mats_ref[block, fan_pair], preferred_element_type=jnp.float32
                    ).astype(jnp.bfloat16)
                    fans_ref[2 * fan_pair, at : at + size, cols] = both[:, :LANES]
                    fans_ref[2 * fan_pair + 1, at : at + size, cols] = both[:, LANES:]
        for step in range(count):
            start = min(step * width, rows - width)
            total = None
            for fan in range(2 * fan_pairs):
                part = jnp.dot(
                    times_ref[:width, fan * SPAN : (fan + 1) * SPAN],
                    fans_ref[fan, start : start + SPAN, :],
                    preferred_element_type=jnp.float32,
                )
                total = part if total is None else total + part
            give(pair, start, total)
        finish(pair)
        return carry

    lax.fori_loop(0, blocks // 2, do_pair, 0)


def first_kernel(
    start, sizes, noted, owners, me_ref, target_ref, x_ref, edge_a, edge_b, mats_ref, times_ref,
    *refs
):
    outs = refs[-8 - owners * len(sizes) : -8]
    merged, fans_ref, done, note, rims, sem, note_sem, rim_sem = refs[-8:]
    blocks, rows = done.shape[:2]
    samples = x_ref.shape[1]
    window = start - REACH // 2
    begin, end = max(0, window), min(samples, start + rows + REACH // 2)
    homes, order = ranks([target_ref[block] for block in range(blocks)], blocks)
    groups, at = [], 0
    for group, size in enumerate(sizes):
        groups.append((at, size, outs[group * owners : (group + 1) * owners]))
        at += size

    def tell(offset):
        return pltpu.make_async_copy(
            note, groups[0][2][offset].at[0, pl.ds(sizes[0], NOTE), :], note_sem.at[offset]
        )

    if noted:
        lane = lax.broadcasted_iota(jnp.int32, note.shape, 1)
        row = jnp.zeros(note.shape, jnp.int32)
        for block in range(blocks):
            row = jnp.where(lane == block, target_ref[block], row)
        note[...] = row.astype(jnp.float32).astype(jnp.bfloat16)
        for offset in range(owners):
            tell(offset).start()

    def put(row, values):
        merged[row - window : row - window + values.shape[0], :] = values

    unpack_edges((edge_a, edge_b), samples, blocks, begin, end, put)

    def give(pair, at, values):
        values = values.astype(jnp.bfloat16)
        for half in range(2):
            done[2 * pair + half, at : at + values.shape[0], :] = values[
                :, half * LANES : (half + 1) * LANES
            ]

    def pick(values, pair, half):
        value = values[half]
        for other in range(1, blocks // 2):
            value = jnp.where(pair == other, values[2 * other + half], value)
        return value

    def pack_rim(block):
        at, size, _ = groups[-1]
        trace = lax.broadcasted_iota(jnp.int32, (LANES, LANES), 0)
        lane = lax.broadcasted_iota(jnp.int32, (LANES, LANES), 1)
        wanted = jnp.where(lane < EDGE, lane, lane + LANES - 2 * EDGE)
        chosen = jnp.where((lane < 2 * EDGE) & (trace == wanted), 1.0, 0.0).astype(jnp.bfloat16)
        found = jnp.dot(done[block, at : at + size, :], chosen, preferred_element_type=jnp.float32)
        fold, total = rims.shape[1], None
        for part in range(-(-size // fold)):
            piece = found[part * fold : (part + 1) * fold]
            if piece.shape[0] < fold:
                rest = jnp.zeros((fold - piece.shape[0], LANES), jnp.float32)
                piece = jnp.concatenate([piece, rest], axis=0)
            if part:
                piece = pltpu.roll(piece, 2 * EDGE * part, 1)
            total = piece if total is None else total + piece
        rims[block] = total.astype(jnp.bfloat16)

    rim_group = None if noted else len(groups) - 2

    def finish(pair):
        for half in range(2):
            block = 2 * pair + half
            if not noted:
                pack_rim(block)
            owner, rank = pick(homes, pair, half), pick(order, pair, half)
            away = lax.rem(owner - me_ref[0] + owners, owners)
            for group, (at, size, arrays) in enumerate(groups):
                part = done.at[block, pl.ds(at, size), :]
                for offset, out_ref in enumerate(arrays):

                    @pl.when(away == offset)
                    def _():
                        pltpu.make_async_copy(
                            part, out_ref.at[rank, pl.ds(0, size), :], sem.at[group, block]
                        ).start()
                        if group == rim_group:
                            pltpu.make_async_copy(
                                rims.at[block],
                                out_ref.at[rank, pl.ds(size, rims.shape[1]), :],
                                rim_sem.at[block],
                            ).start()

    pieces = [(begin - window, end - begin, lambda block: x_ref[block, begin:end, :])]
    filter_window(pieces, merged, fans_ref, mats_ref, times_ref, rows, give, finish)
    for group, (at, size, arrays) in enumerate(groups):
        for block in range(blocks):
            pltpu.make_async_copy(
                done.at[block, pl.ds(at, size), :],
                arrays[0].at[0, pl.ds(0, size), :],
                sem.at[group, block],
            ).wait()
    if noted:
        for offset in range(owners):
            tell(offset).wait()
    else:
        _, size, arrays = groups[rim_group]
        for block in range(blocks):
            pltpu.make_async_copy(
                rims.at[block],
                arrays[0].at[0, pl.ds(size, rims.shape[1]), :],
                rim_sem.at[block],
            ).wait()


def first_pass(me, target, owners, traces, edges, mats, times, after, start, sizes, noted):
    blocks = traces.shape[0]
    fans = 2 * mats.shape[1]
    rows = sum(sizes)
    tall = window_rows(rows)
    shapes = []
    for group, size in enumerate(sizes):
        size += NOTE if noted else rim_rows(sizes[-1]) if group == len(sizes) - 2 else 0
        shapes += [jax.ShapeDtypeStruct((blocks // 2, size, LANES), jnp.bfloat16)] * owners
    flat = pl.pallas_call(
        functools.partial(first_kernel, start, sizes, noted, owners),
        in_specs=[SMEM, SMEM] + [VMEM] * 5 + [ANY] * len(after),
        out_specs=[ANY] * len(shapes),
        scratch_shapes=[
            pltpu.VMEM((tall, LANES), jnp.bfloat16),
            pltpu.VMEM((fans, tall, 2 * LANES), jnp.bfloat16),
            pltpu.VMEM((blocks, rows, LANES), jnp.bfloat16),
            pltpu.VMEM((NOTE, LANES), jnp.bfloat16),
            pltpu.VMEM((blocks, rim_rows(sizes[-1]), LANES), jnp.bfloat16),
            pltpu.SemaphoreType.DMA((len(sizes), blocks)),
            pltpu.SemaphoreType.DMA((owners,)),
            pltpu.SemaphoreType.DMA((blocks,)),
        ],
        out_shape=shapes,
        cost_estimate=NO_COST,
        compiler_params=PARAMS,
        name="first_pass",
    )(me, target, traces, *edges, mats, times, *after)
    return [flat[group * owners : (group + 1) * owners] for group in range(len(sizes))]


def second_kernel(at, has_past, *refs):
    refs = list(refs)
    take = lambda: refs.pop(0)
    past = [take() for _ in range(3)] if has_past else None
    now = [take() for _ in range(3)]
    mats_ref, times_ref, _ = take(), take(), take()
    if has_past:
        take()
    out_ref, token_ref, merged, fans_ref, done, sem = refs
    token_ref[...] = jnp.zeros_like(token_ref)
    blocks, rows = done.shape[:2]
    lead = REACH if has_past else REACH // 2
    pieces = []

    def put(origin):
        def store(row, values):
            merged[row - origin : row - origin + values.shape[0], :] = values

        return store

    if has_past:
        held = past[0].shape[1]
        unpack_edges(past[1:], held, blocks, held - REACH, held, put(held - REACH))
        pieces.append((0, REACH, lambda block: past[0][block, held - REACH :, :]))
    size = now[0].shape[1]
    unpack_edges(now[1:], size, blocks, 0, size, put(-lead))
    pieces.append((lead, size, lambda block: now[0][block]))

    def copy(block):
        return pltpu.make_async_copy(
            done.at[block], out_ref.at[block, pl.ds(at, rows), :], sem.at[block]
        )

    def give(pair, start, values):
        for half in range(2):
            done[2 * pair + half, start : start + values.shape[0], :] = values[
                :, half * LANES : (half + 1) * LANES
            ]

    def finish(pair):
        for half in range(2):
            copy(2 * pair + half).start()

    filter_window(pieces, merged, fans_ref, mats_ref, times_ref, rows, give, finish)
    for block in range(blocks):
        copy(block).wait()


def second_pass(blocks, samples, past, now, mats, times, after, out, at, rows):
    fans = 2 * mats.shape[1]
    tall = window_rows(rows)
    operands = [*(past or ()), *now, mats, times, after]
    specs = [VMEM] * (len(operands) - 1) + [ANY]
    aliases = {}
    if out is not None:
        specs.append(ANY)
        operands.append(out)
        aliases = {len(operands) - 1: 0}
    return pl.pallas_call(
        functools.partial(second_kernel, at, past is not None),
        in_specs=specs,
        out_specs=[ANY, VMEM],
        scratch_shapes=[
            pltpu.VMEM((tall, LANES), jnp.bfloat16),
            pltpu.VMEM((fans, tall, 2 * LANES), jnp.bfloat16),
            pltpu.VMEM((blocks, rows, LANES), jnp.float32),
            pltpu.SemaphoreType.DMA((blocks,)),
        ],
        out_shape=[
            jax.ShapeDtypeStruct((blocks, samples, LANES), jnp.float32),
            jax.ShapeDtypeStruct((8, LANES), jnp.float32),
        ],
        input_output_aliases=aliases,
        cost_estimate=NO_COST,
        compiler_params=PARAMS,
        name="second_pass",
    )(*operands)


def last_kernel(
    at, slot_ref, past_ref, edge_a, edge_b, mats_ref, times_ref, _, *refs
):
    parts, (out_ref, merged, fans_ref, held, done, in_sem, sem) = refs[:-7], refs[-7:]
    blocks, rows = done.shape[:2]
    before, size = past_ref.shape[1], held.shape[1]
    begin, wait = gather_rows(slot_ref, parts, held, in_sem, 0)
    begin()
    origin = before - REACH

    def put(row, values):
        merged[row - origin : row - origin + values.shape[0], :] = values

    unpack_edges((edge_a, edge_b), before, blocks, origin, before, put)
    fold, base = rim_rows(size), folded_rows(before)
    for part in range(-(-size // fold)):
        count = min(fold, size - part * fold)
        lane = lax.broadcasted_iota(jnp.int32, (count, LANES), 1)
        total = jnp.zeros((count, LANES), jnp.float32)
        for way, edge in enumerate((edge_a, edge_b)):
            for block in range(blocks):
                to = EDGE * (way * blocks + block)
                top = base + block // 2 * fold
                piece = edge[top : top + count, :].astype(jnp.float32)
                shift = (to - EDGE * (2 * part + block % 2)) % LANES
                piece = pltpu.roll(piece, shift, 1) if shift else piece
                total = jnp.where((lane >= to) & (lane < to + EDGE), piece, total)
        row = REACH + part * fold
        merged[row : row + count, :] = total.astype(jnp.bfloat16)
    wait()

    def copy(block):
        return pltpu.make_async_copy(
            done.at[block], out_ref.at[block, pl.ds(at, rows), :], sem.at[block]
        )

    def give(pair, start, values):
        for half in range(2):
            done[2 * pair + half, start : start + values.shape[0], :] = values[
                :, half * LANES : (half + 1) * LANES
            ]

    def finish(pair):
        for half in range(2):
            copy(2 * pair + half).start()

    pieces = [
        (0, REACH, lambda block: past_ref[block, origin:, :]),
        (REACH, size, lambda block: held[block]),
    ]
    filter_window(pieces, merged, fans_ref, mats_ref, times_ref, rows, give, finish)
    for block in range(blocks):
        copy(block).wait()


def last_pass(slots, past, parts, size, mats, times, out, at, rows):
    blocks, samples, _ = out.shape
    fans = 2 * mats.shape[1]
    tall = window_rows(rows)
    return pl.pallas_call(
        functools.partial(last_kernel, at),
        in_specs=[SMEM] + [VMEM] * 5 + [ANY] * (1 + len(parts)),
        out_specs=ANY,
        scratch_shapes=[
            pltpu.VMEM((tall, LANES), jnp.bfloat16),
            pltpu.VMEM((fans, tall, 2 * LANES), jnp.bfloat16),
            pltpu.VMEM((blocks, size, LANES), jnp.bfloat16),
            pltpu.VMEM((blocks, rows, LANES), jnp.float32),
            pltpu.SemaphoreType.DMA((blocks,)),
            pltpu.SemaphoreType.DMA((blocks,)),
        ],
        out_shape=jax.ShapeDtypeStruct(out.shape, jnp.float32),
        input_output_aliases={6: 0},
        cost_estimate=NO_COST,
        compiler_params=PARAMS,
        name="last_pass",
    )(slots, *past, mats, times, out, *parts)


def per_device(
    traces, first_trace_taps, first_time_taps, second_trace_taps, second_time_taps, dest_row
):
    blocks, samples, _ = traces.shape
    owners = lax.axis_size("rcv")
    me = lax.axis_index("rcv").astype(jnp.int32).reshape(1)
    even = (1 - lax.axis_index("shot") % 2).astype(jnp.int32).reshape(1)
    target = dest_row.reshape(blocks)

    def send(values, offset):
        pairs = [(i, (i + offset) % owners) for i in range(owners)]
        return lax.ppermute(values, "rcv", pairs) if offset else values

    bounds = chunk_bounds(samples)
    count = len(bounds) - 1
    sizes = [bounds[step + 1] - bounds[step] for step in range(count)]
    *packed, picks = first_edges(even, traces)
    edges = swap_edges(packed)
    mats, times = weights(even, first_trace_taps, first_time_taps, traces, blocks)

    def first(after, start, sizes, noted):
        return first_pass(
            me, target, owners, traces, edges, mats, times, after, start, sizes, noted
        )

    def exchange(sent, before, *after):
        arrived = []
        for offset, part in enumerate(sent):
            if offset and before is not None:
                part, before[offset], *_ = lax.optimization_barrier(
                    (part, before[offset], *after)
                )
            arrived.append(send(part, offset))
        return arrived

    sent = first([], 0, sizes[:1], True)
    arrived = [exchange(sent[0], None)]
    sent += first([sent[0][0]], bounds[1], sizes[1:], False)
    second_mats, second_times, slots = late_weights(
        even, me, target, second_trace_taps, second_time_taps, arrived[0], sent[-1][0]
    )

    out, past, now, token, rims = None, None, None, None, None

    def second(step, after):
        at = max(0, bounds[step] - REACH // 2)
        stop = bounds[step + 1] - REACH // 2 if step + 1 < count else samples
        return second_pass(
            blocks, samples, past, now, second_mats, second_times, after, out, at, stop - at
        )

    for step in range(count - 1):
        ahead = [*now[1:]] if now else []
        ahead += [token] if token is not None else []
        arrived.append(exchange(sent[step + 1], arrived[step], *ahead))
        early = 0 < step == count - 2
        if early:
            out, token = second(step - 1, slots)
            past = now
        gathered, *packed = second_edges(
            even,
            slots,
            picks,
            arrived[step],
            sizes[step],
            rim_rows(sizes[-1]) if step == count - 2 else 0,
            slots if token is None else token,
            blocks,
        )
        rims = packed[0]
        coming = (gathered, *swap_edges(packed))
        if step and not early:
            out, token = second(step - 1, rims)
            past = now
        now = coming
    out, token = second(count - 2, slots)
    at = bounds[count - 1] - REACH // 2
    return last_pass(
        slots, now, arrived[-1], sizes[-1], second_mats, second_times, out, at, samples - at
    )


def solution(mesh):
    in_specs = (P("rcv", None, "shot"), P(), P(), P(), P(), P("rcv", "shot"))
    out_specs = P("rcv", None, "shot")
    return jax.shard_map(
        per_device, mesh=mesh, in_specs=in_specs, out_specs=out_specs, check_vma=False
    )
```

```python
import functools

import jax
import jax.numpy as jnp
from jax import lax
from jax.experimental import pallas as pl
from jax.experimental.pallas import tpu as pltpu
from jax.sharding import PartitionSpec as P

LANES = 128
EDGE = 8
SPAN = 256
REACH = 64
WIDE = SPAN - REACH
FOLD = 4
PARAMS = pltpu.CompilerParams(vmem_limit_bytes=16 * 2**20)
NO_COST = pl.CostEstimate(flops=1, bytes_accessed=1, transcendentals=0)
VMEM = pl.BlockSpec(memory_space=pltpu.VMEM)
SMEM = pl.BlockSpec(memory_space=pltpu.SMEM)
ANY = pl.BlockSpec(memory_space=pl.ANY)
HBM = pl.BlockSpec(memory_space=pltpu.HBM)
CHUNKS = (384, 640, 512)
RIM_FOLD = 8
NOTE = 16


def chunk_bounds(samples):
    bounds = [0]
    for size in CHUNKS:
        if bounds[-1] + size + REACH <= samples:
            bounds.append(bounds[-1] + size)
    bounds.append(samples)
    return bounds


def segment_plan(rows):
    count = -(-rows // WIDE)
    width = min(WIDE, -(-rows // (16 * count)) * 16)
    return count, width


def window_rows(rows):
    return rows - segment_plan(rows)[1] + SPAN


def folded_rows(rows):
    return -(-rows // (16 * FOLD)) * 16


def rim_rows(rows):
    return -(-rows // (16 * RIM_FOLD)) * 16


def place_taps(taps_ref, origin, step):
    width = taps_ref.shape[1]
    tap = lax.broadcasted_iota(jnp.int32, (width, SPAN), 0)
    at = lax.broadcasted_iota(jnp.int32, (width, SPAN), 1)
    spread = jnp.where(at == (origin + step * tap + SPAN) % SPAN, 1.0, 0.0).astype(jnp.bfloat16)
    return jnp.dot(taps_ref[...], spread, preferred_element_type=jnp.float32)


def fill_weights(even, trace_ref, time_ref, mats_ref, times_ref):
    fans = trace_ref.shape[0]
    blocks = mats_ref.shape[0]
    trace_rows = place_taps(trace_ref, trace_ref.shape[1] // 2, -1)
    time_rows = place_taps(time_ref, 0, 1)
    for fan in range(fans):
        row = jnp.broadcast_to(trace_rows[fan : fan + 1, :], (LANES, SPAN))
        own = pltpu.roll(row, 0, 1, stride=1, stride_axis=0)[:, :LANES]
        left = pltpu.roll(row[:EDGE], SPAN - EDGE, 1, stride=1, stride_axis=0)[:, :LANES]
        right = pltpu.roll(row[:EDGE], LANES, 1, stride=1, stride_axis=0)[:, :LANES]
        pieces = (jnp.where(even, right, left), jnp.where(even, left, right))
        pair, half = fan // 2, fan % 2
        cols = slice(half * LANES, (half + 1) * LANES)
        for block in range(blocks):
            before, after = EDGE * block, EDGE * (blocks - 1 - block)
            parts = []
            for piece in pieces:
                if before:
                    parts.append(jnp.zeros((before, LANES), jnp.float32))
                parts.append(piece)
                if after:
                    parts.append(jnp.zeros((after, LANES), jnp.float32))
            parts.append(jnp.zeros((LANES - 2 * EDGE * blocks, LANES), jnp.float32))
            mats_ref[block, pair, :LANES, cols] = own.astype(jnp.bfloat16)
            mats_ref[block, pair, LANES:, cols] = jnp.concatenate(parts, axis=0).astype(
                jnp.bfloat16
            )
        taps = jnp.broadcast_to(time_rows[fan : fan + 1, :], (WIDE, SPAN))
        times_ref[:, fan * SPAN : (fan + 1) * SPAN] = pltpu.roll(
            taps, 0, 1, stride=1, stride_axis=0
        ).astype(jnp.bfloat16)


def weights_kernel(even_ref, trace_ref, time_ref, _, mats_ref, times_ref):
    fill_weights(even_ref[0] == 1, trace_ref, time_ref, mats_ref, times_ref)


def ranks(targets, blocks):
    owners = [lax.div(target, blocks) for target in targets]
    order = []
    for block, owner in enumerate(owners):
        rank = jnp.int32(0)
        for other in owners[:block]:
            rank = rank + jnp.where(other == owner, 1, 0)
        order.append(rank)
    return owners, order


def late_kernel(even_ref, me_ref, target_ref, trace_ref, time_ref, *refs):
    parts, (_, mats_ref, times_ref, slots_ref, notes, sem) = refs[:-6], refs[-6:]
    blocks, me = mats_ref.shape[0], me_ref[0]
    slot_cap, held = parts[0].shape[0], parts[0].shape[1]

    def fetch(offset):
        return pltpu.make_async_copy(
            parts[offset].at[0, pl.ds(held - NOTE, NOTE), :], notes.at[offset], sem.at[offset]
        )

    for offset in range(1, len(parts)):
        fetch(offset).start()
    fill_weights(even_ref[0] == 1, trace_ref, time_ref, mats_ref, times_ref)
    slots = [jnp.int32(0)] * blocks
    lane = lax.broadcasted_iota(jnp.int32, (1, LANES), 1)
    for offset in range(len(parts)):
        if offset:
            fetch(offset).wait()
            note = notes[offset].astype(jnp.float32)[:1]
            targets = [
                jnp.sum(jnp.where(lane == block, note, 0.0)).astype(jnp.int32)
                for block in range(blocks)
            ]
        else:
            targets = [target_ref[block] for block in range(blocks)]
        for target, rank in zip(targets, ranks(targets, blocks)[1]):
            for block in range(blocks):
                slots[block] = jnp.where(
                    target == me * blocks + block, offset * slot_cap + rank, slots[block]
                )
    for block in range(blocks):
        slots_ref[block] = slots[block]


def weight_shapes(blocks, fans):
    return [
        jax.ShapeDtypeStruct((blocks, fans // 2, 2 * LANES, 2 * LANES), jnp.bfloat16),
        jax.ShapeDtypeStruct((WIDE, fans * SPAN), jnp.bfloat16),
    ]


def weights(even, trace_taps, time_taps, after, blocks):
    return pl.pallas_call(
        weights_kernel,
        in_specs=[SMEM, VMEM, VMEM, ANY],
        out_specs=[VMEM, VMEM],
        out_shape=weight_shapes(blocks, trace_taps.shape[0]),
        cost_estimate=NO_COST,
        compiler_params=PARAMS,
        name="weights",
    )(even, trace_taps, time_taps, after)


def late_weights(even, me, target, trace_taps, time_taps, arrived, after):
    blocks = target.shape[0]
    return pl.pallas_call(
        late_kernel,
        in_specs=[SMEM, SMEM, SMEM, VMEM, VMEM] + [ANY] * (len(arrived) + 1),
        out_specs=[VMEM, VMEM, SMEM],
        out_shape=weight_shapes(blocks, trace_taps.shape[0])
        + [jax.ShapeDtypeStruct((blocks,), jnp.int32)],
        scratch_shapes=[
            pltpu.VMEM((len(arrived), NOTE, LANES), jnp.bfloat16),
            pltpu.SemaphoreType.DMA((len(arrived),)),
        ],
        cost_estimate=NO_COST,
        compiler_params=PARAMS,
        name="late_weights",
    )(even, me, target, trace_taps, time_taps, *arrived, after)


def edge_picks(even, blocks):
    trace = lax.broadcasted_iota(jnp.int32, (2 * LANES, 2 * LANES), 0)
    lane = lax.broadcasted_iota(jnp.int32, (2 * LANES, 2 * LANES), 1)
    last = jnp.where(even, 1, 0)
    begin = jnp.where(lane < LANES, last, 1 - last) * (LANES - EDGE)
    lane = lane % LANES
    picks = []
    for pair in range(blocks // 2):
        at = lane - EDGE * (2 * pair + trace // LANES)
        pick = (at >= 0) & (at < EDGE) & (trace % LANES == at + begin)
        picks.append(jnp.where(pick, 1.0, 0.0).astype(jnp.bfloat16))
    return picks


def pick_part(picks, tiles_ref, start, stop):
    found = None
    for pair, pick in enumerate(picks):
        both = jnp.concatenate(
            [tiles_ref[2 * pair, start:stop, :], tiles_ref[2 * pair + 1, start:stop, :]], axis=1
        )
        one = jnp.dot(both, pick, preferred_element_type=jnp.float32)
        found = one if found is None else found + one
    return found


def pack_edges(picks, tiles_ref, packed_refs):
    blocks, rows = tiles_ref.shape[:2]
    fold = folded_rows(rows)
    totals = [None, None]
    for part in range(FOLD):
        start, stop = part * fold, min(rows, (part + 1) * fold)
        found = pick_part(picks, tiles_ref, start, stop)
        if stop - start < fold:
            found = jnp.concatenate(
                [found, jnp.zeros((fold - stop + start, 2 * LANES), jnp.float32)], axis=0
            )
        for way in range(2):
            piece = found[:, way * LANES : (way + 1) * LANES]
            if part:
                piece = pltpu.roll(piece, part * EDGE * blocks, 1)
            totals[way] = piece if totals[way] is None else totals[way] + piece
    for way in range(2):
        packed_refs[way][:fold, :] = totals[way].astype(jnp.bfloat16)


def unpack_edges(packed_refs, rows, blocks, start, stop, give):
    fold, width = folded_rows(rows), EDGE * blocks
    while start < stop:
        part = start // fold
        until = min(stop, (part + 1) * fold)
        pieces = []
        for way in range(2):
            piece = packed_refs[way][start - part * fold : until - part * fold, :]
            shift = (way - part) * width % LANES
            piece = piece.astype(jnp.float32)
            pieces.append(pltpu.roll(piece, shift, 1) if shift else piece)
        lane = lax.broadcasted_iota(jnp.int32, pieces[0].shape, 1)
        give(start, jnp.where(lane < width, pieces[0], pieces[1]).astype(jnp.bfloat16))
        start = until


def first_edges_kernel(even_ref, x_ref, out_a, out_b, picks_ref):
    blocks = x_ref.shape[0]
    picks = edge_picks(even_ref[0] == 1, blocks)
    for pair, pick in enumerate(picks):
        picks_ref[pair] = pick
    pack_edges(picks, x_ref, (out_a, out_b))


def first_edges(even, traces):
    blocks = traces.shape[0]
    packed = jax.ShapeDtypeStruct((folded_rows(traces.shape[1]), LANES), jnp.bfloat16)
    return pl.pallas_call(
        first_edges_kernel,
        in_specs=[SMEM, VMEM],
        out_specs=[VMEM] * 3,
        out_shape=[
            packed,
            packed,
            jax.ShapeDtypeStruct((blocks // 2, 2 * LANES, 2 * LANES), jnp.bfloat16),
        ],
        cost_estimate=NO_COST,
        compiler_params=PARAMS,
        name="first_edges",
    )(even, traces)


def gather_rows(slot_ref, parts, held_ref, sem, start):
    blocks, rows = held_ref.shape[:2]
    slot_cap = parts[0].shape[0]

    def begin():
        for block in range(blocks):
            slot = slot_ref[block]
            for offset, part in enumerate(parts):

                @pl.when(slot // slot_cap == offset)
                def _():
                    pltpu.make_async_copy(
                        part.at[slot % slot_cap, pl.ds(start, rows), :],
                        held_ref.at[block],
                        sem.at[block],
                    ).start()

    def wait():
        for block in range(blocks):
            pltpu.make_async_copy(
                parts[0].at[0, pl.ds(start, rows), :], held_ref.at[block], sem.at[block]
            ).wait()

    return begin, wait


def second_edges_kernel(even_ref, slot_ref, picks_ref, *refs):
    parts, (_, sorted_ref, out_a, out_b, rims_ref, sem, rim_sem) = refs[:-7], refs[-7:]
    blocks, rows = sorted_ref.shape[:2]
    begin, wait = gather_rows(slot_ref, parts, sorted_ref, sem, 0)
    begin()
    fold = folded_rows(rows)
    rimmed = out_a.shape[0] > fold
    if rimmed:
        rim_begin, rim_wait = gather_rows(slot_ref, parts, rims_ref, rim_sem, rows)
        rim_begin()
    wait()
    picks = [picks_ref[pair] for pair in range(blocks // 2)]
    pack_edges(picks, sorted_ref, (out_a, out_b))
    if rimmed:
        rim_wait()
        size = rims_ref.shape[1]
        even = even_ref[0] == 1
        lane = lax.broadcasted_iota(jnp.int32, (size, LANES), 1)
        low = lane % (2 * EDGE) < EDGE
        for pair in range(blocks // 2):
            one, two = (rims_ref[2 * pair + half].astype(jnp.float32) for half in range(2))
            first = jnp.where(low, one, pltpu.roll(two, EDGE, 1))
            last = jnp.where(low, pltpu.roll(one, LANES - EDGE, 1), two)
            span = slice(fold + pair * size, fold + (pair + 1) * size)
            out_a[span, :] = jnp.where(even, last, first).astype(jnp.bfloat16)
            out_b[span, :] = jnp.where(even, first, last).astype(jnp.bfloat16)


def second_edges(even, slots, picks, arrived, rows, rims, after, blocks):
    packed = jax.ShapeDtypeStruct((folded_rows(rows) + blocks // 2 * rims, LANES), jnp.bfloat16)
    return pl.pallas_call(
        second_edges_kernel,
        in_specs=[SMEM, SMEM, VMEM] + [ANY] * (len(arrived) + 1),
        out_specs=[VMEM] * 3,
        scratch_shapes=[
            pltpu.VMEM((blocks, rims or 16, LANES), jnp.bfloat16),
            pltpu.SemaphoreType.DMA((blocks,)),
            pltpu.SemaphoreType.DMA((blocks,)),
        ],
        out_shape=[jax.ShapeDtypeStruct((blocks, rows, LANES), jnp.bfloat16), packed, packed],
        cost_estimate=NO_COST,
        compiler_params=PARAMS,
        name="second_edges",
    )(even, slots, picks, *arrived, after)


def swap_edges(packed):
    count = lax.axis_size("shot")
    got = []
    for first, edges in enumerate(packed):
        pairs = []
        for low in range(first, count - 1, 2):
            pairs += [(low, low + 1), (low + 1, low)]
        got.append(lax.ppermute(edges, "shot", pairs))
    return got


def filter_window(pieces, merged, fans_ref, mats_ref, times_ref, rows, give, finish):
    fan_pairs = mats_ref.shape[1]
    blocks = mats_ref.shape[0]
    tall = fans_ref.shape[1]
    count, width = segment_plan(rows)
    covered = 0
    for at, size, _ in list(pieces) + [(tall, 0, None)]:
        if at > covered:
            fans_ref[:, covered:at, :] = jnp.zeros(
                (fans_ref.shape[0], at - covered, fans_ref.shape[2]), jnp.bfloat16
            )
        covered = at + size
    def do_pair(pair, carry):
        for half in range(2):
            block = 2 * pair + half
            cols = slice(half * LANES, (half + 1) * LANES)
            for at, size, load in pieces:
                lhs = jnp.concatenate([load(block), merged[at : at + size, :]], axis=1)
                for fan_pair in range(fan_pairs):
                    both = jnp.dot(
                        lhs, mats_ref[block, fan_pair], preferred_element_type=jnp.float32
                    ).astype(jnp.bfloat16)
                    fans_ref[2 * fan_pair, at : at + size, cols] = both[:, :LANES]
                    fans_ref[2 * fan_pair + 1, at : at + size, cols] = both[:, LANES:]
        for step in range(count):
            start = min(step * width, rows - width)
            total = None
            for fan in range(2 * fan_pairs):
                part = jnp.dot(
                    times_ref[:width, fan * SPAN : (fan + 1) * SPAN],
                    fans_ref[fan, start : start + SPAN, :],
                    preferred_element_type=jnp.float32,
                )
                total = part if total is None else total + part
            give(pair, start, total)
        finish(pair)
        return carry

    lax.fori_loop(0, blocks // 2, do_pair, 0)


def first_kernel(
    start, sizes, noted, owners, me_ref, target_ref, x_ref, edge_a, edge_b, mats_ref, times_ref,
    *refs
):
    outs = refs[-8 - owners * len(sizes) : -8]
    merged, fans_ref, done, note, rims, sem, note_sem, rim_sem = refs[-8:]
    blocks, rows = done.shape[:2]
    samples = x_ref.shape[1]
    window = start - REACH // 2
    begin, end = max(0, window), min(samples, start + rows + REACH // 2)
    homes, order = ranks([target_ref[block] for block in range(blocks)], blocks)
    groups, at = [], 0
    for group, size in enumerate(sizes):
        groups.append((at, size, outs[group * owners : (group + 1) * owners]))
        at += size

    def tell(offset):
        return pltpu.make_async_copy(
            note, groups[0][2][offset].at[0, pl.ds(sizes[0], NOTE), :], note_sem.at[offset]
        )

    if noted:
        lane = lax.broadcasted_iota(jnp.int32, note.shape, 1)
        row = jnp.zeros(note.shape, jnp.int32)
        for block in range(blocks):
            row = jnp.where(lane == block, target_ref[block], row)
        note[...] = row.astype(jnp.float32).astype(jnp.bfloat16)
        for offset in range(owners):
            tell(offset).start()

    def put(row, values):
        merged[row - window : row - window + values.shape[0], :] = values

    unpack_edges((edge_a, edge_b), samples, blocks, begin, end, put)

    def give(pair, at, values):
        values = values.astype(jnp.bfloat16)
        for half in range(2):
            done[2 * pair + half, at : at + values.shape[0], :] = values[
                :, half * LANES : (half + 1) * LANES
            ]

    def pick(values, pair, half):
        value = values[half]
        for other in range(1, blocks // 2):
            value = jnp.where(pair == other, values[2 * other + half], value)
        return value

    def pack_rim(block):
        at, size, _ = groups[-1]
        trace = lax.broadcasted_iota(jnp.int32, (LANES, LANES), 0)
        lane = lax.broadcasted_iota(jnp.int32, (LANES, LANES), 1)
        wanted = jnp.where(lane < EDGE, lane, lane + LANES - 2 * EDGE)
        chosen = jnp.where((lane < 2 * EDGE) & (trace == wanted), 1.0, 0.0).astype(jnp.bfloat16)
        found = jnp.dot(done[block, at : at + size, :], chosen, preferred_element_type=jnp.float32)
        fold, total = rims.shape[1], None
        for part in range(-(-size // fold)):
            piece = found[part * fold : (part + 1) * fold]
            if piece.shape[0] < fold:
                rest = jnp.zeros((fold - piece.shape[0], LANES), jnp.float32)
                piece = jnp.concatenate([piece, rest], axis=0)
            if part:
                piece = pltpu.roll(piece, 2 * EDGE * part, 1)
            total = piece if total is None else total + piece
        rims[block] = total.astype(jnp.bfloat16)

    rim_group = None if noted else len(groups) - 2

    def finish(pair):
        for half in range(2):
            block = 2 * pair + half
            if not noted:
                pack_rim(block)
            owner, rank = pick(homes, pair, half), pick(order, pair, half)
            away = lax.rem(owner - me_ref[0] + owners, owners)
            for group, (at, size, arrays) in enumerate(groups):
                part = done.at[block, pl.ds(at, size), :]
                for offset, out_ref in enumerate(arrays):

                    @pl.when(away == offset)
                    def _():
                        pltpu.make_async_copy(
                            part, out_ref.at[rank, pl.ds(0, size), :], sem.at[group, block]
                        ).start()
                        if group == rim_group:
                            pltpu.make_async_copy(
                                rims.at[block],
                                out_ref.at[rank, pl.ds(size, rims.shape[1]), :],
                                rim_sem.at[block],
                            ).start()

    pieces = [(begin - window, end - begin, lambda block: x_ref[block, begin:end, :])]
    filter_window(pieces, merged, fans_ref, mats_ref, times_ref, rows, give, finish)
    for group, (at, size, arrays) in enumerate(groups):
        for block in range(blocks):
            pltpu.make_async_copy(
                done.at[block, pl.ds(at, size), :],
                arrays[0].at[0, pl.ds(0, size), :],
                sem.at[group, block],
            ).wait()
    if noted:
        for offset in range(owners):
            tell(offset).wait()
    else:
        _, size, arrays = groups[rim_group]
        for block in range(blocks):
            pltpu.make_async_copy(
                rims.at[block],
                arrays[0].at[0, pl.ds(size, rims.shape[1]), :],
                rim_sem.at[block],
            ).wait()


def first_pass(me, target, owners, traces, edges, mats, times, after, start, sizes, noted):
    blocks = traces.shape[0]
    fans = 2 * mats.shape[1]
    rows = sum(sizes)
    tall = window_rows(rows)
    shapes = []
    for group, size in enumerate(sizes):
        size += NOTE if noted else rim_rows(sizes[-1]) if group == len(sizes) - 2 else 0
        shapes += [jax.ShapeDtypeStruct((blocks // 2, size, LANES), jnp.bfloat16)] * owners
    flat = pl.pallas_call(
        functools.partial(first_kernel, start, sizes, noted, owners),
        in_specs=[SMEM, SMEM] + [VMEM] * 5 + [ANY] * len(after),
        out_specs=[ANY] * len(shapes),
        scratch_shapes=[
            pltpu.VMEM((tall, LANES), jnp.bfloat16),
            pltpu.VMEM((fans, tall, 2 * LANES), jnp.bfloat16),
            pltpu.VMEM((blocks, rows, LANES), jnp.bfloat16),
            pltpu.VMEM((NOTE, LANES), jnp.bfloat16),
            pltpu.VMEM((blocks, rim_rows(sizes[-1]), LANES), jnp.bfloat16),
            pltpu.SemaphoreType.DMA((len(sizes), blocks)),
            pltpu.SemaphoreType.DMA((owners,)),
            pltpu.SemaphoreType.DMA((blocks,)),
        ],
        out_shape=shapes,
        cost_estimate=NO_COST,
        compiler_params=PARAMS,
        name="first_pass",
    )(me, target, traces, *edges, mats, times, *after)
    return [flat[group * owners : (group + 1) * owners] for group in range(len(sizes))]


def second_kernel(at, has_past, *refs):
    refs = list(refs)
    take = lambda: refs.pop(0)
    past = [take() for _ in range(3)] if has_past else None
    now = [take() for _ in range(3)]
    mats_ref, times_ref, _ = take(), take(), take()
    if has_past:
        take()
    out_ref, token_ref, merged, fans_ref, done, sem = refs
    token_ref[...] = jnp.zeros_like(token_ref)
    blocks, rows = done.shape[:2]
    lead = REACH if has_past else REACH // 2
    pieces = []

    def put(origin):
        def store(row, values):
            merged[row - origin : row - origin + values.shape[0], :] = values

        return store

    if has_past:
        held = past[0].shape[1]
        unpack_edges(past[1:], held, blocks, held - REACH, held, put(held - REACH))
        pieces.append((0, REACH, lambda block: past[0][block, held - REACH :, :]))
    size = now[0].shape[1]
    unpack_edges(now[1:], size, blocks, 0, size, put(-lead))
    pieces.append((lead, size, lambda block: now[0][block]))

    def copy(block):
        return pltpu.make_async_copy(
            done.at[block], out_ref.at[block, pl.ds(at, rows), :], sem.at[block]
        )

    def give(pair, start, values):
        for half in range(2):
            done[2 * pair + half, start : start + values.shape[0], :] = values[
                :, half * LANES : (half + 1) * LANES
            ]

    def finish(pair):
        for half in range(2):
            copy(2 * pair + half).start()

    filter_window(pieces, merged, fans_ref, mats_ref, times_ref, rows, give, finish)
    for block in range(blocks):
        copy(block).wait()


def second_pass(blocks, samples, past, now, mats, times, after, out, at, rows):
    fans = 2 * mats.shape[1]
    tall = window_rows(rows)
    operands = [*(past or ()), *now, mats, times, after]
    specs = [VMEM] * (len(operands) - 1) + [ANY]
    aliases = {}
    if out is not None:
        specs.append(ANY)
        operands.append(out)
        aliases = {len(operands) - 1: 0}
    return pl.pallas_call(
        functools.partial(second_kernel, at, past is not None),
        in_specs=specs,
        out_specs=[ANY, VMEM],
        scratch_shapes=[
            pltpu.VMEM((tall, LANES), jnp.bfloat16),
            pltpu.VMEM((fans, tall, 2 * LANES), jnp.bfloat16),
            pltpu.VMEM((blocks, rows, LANES), jnp.float32),
            pltpu.SemaphoreType.DMA((blocks,)),
        ],
        out_shape=[
            jax.ShapeDtypeStruct((blocks, samples, LANES), jnp.float32),
            jax.ShapeDtypeStruct((8, LANES), jnp.float32),
        ],
        input_output_aliases=aliases,
        cost_estimate=NO_COST,
        compiler_params=PARAMS,
        name="second_pass",
    )(*operands)


def last_kernel(
    at, slot_ref, past_ref, edge_a, edge_b, mats_ref, times_ref, _, *refs
):
    parts, (out_ref, merged, fans_ref, held, done, in_sem, sem) = refs[:-7], refs[-7:]
    blocks, rows = done.shape[:2]
    before, size = past_ref.shape[1], held.shape[1]
    begin, wait = gather_rows(slot_ref, parts, held, in_sem, 0)
    begin()
    origin = before - REACH

    def put(row, values):
        merged[row - origin : row - origin + values.shape[0], :] = values

    unpack_edges((edge_a, edge_b), before, blocks, origin, before, put)
    fold, base = rim_rows(size), folded_rows(before)
    for part in range(-(-size // fold)):
        count = min(fold, size - part * fold)
        lane = lax.broadcasted_iota(jnp.int32, (count, LANES), 1)
        total = jnp.zeros((count, LANES), jnp.float32)
        for way, edge in enumerate((edge_a, edge_b)):
            for block in range(blocks):
                to = EDGE * (way * blocks + block)
                top = base + block // 2 * fold
                piece = edge[top : top + count, :].astype(jnp.float32)
                shift = (to - EDGE * (2 * part + block % 2)) % LANES
                piece = pltpu.roll(piece, shift, 1) if shift else piece
                total = jnp.where((lane >= to) & (lane < to + EDGE), piece, total)
        row = REACH + part * fold
        merged[row : row + count, :] = total.astype(jnp.bfloat16)
    wait()

    def copy(block):
        return pltpu.make_async_copy(
            done.at[block], out_ref.at[block, pl.ds(at, rows), :], sem.at[block]
        )

    def give(pair, start, values):
        for half in range(2):
            done[2 * pair + half, start : start + values.shape[0], :] = values[
                :, half * LANES : (half + 1) * LANES
            ]

    def finish(pair):
        for half in range(2):
            copy(2 * pair + half).start()

    pieces = [
        (0, REACH, lambda block: past_ref[block, origin:, :]),
        (REACH, size, lambda block: held[block]),
    ]
    filter_window(pieces, merged, fans_ref, mats_ref, times_ref, rows, give, finish)
    for block in range(blocks):
        copy(block).wait()


def last_pass(slots, past, parts, size, mats, times, out, at, rows):
    blocks, samples, _ = out.shape
    fans = 2 * mats.shape[1]
    tall = window_rows(rows)
    return pl.pallas_call(
        functools.partial(last_kernel, at),
        in_specs=[SMEM] + [VMEM] * 5 + [ANY] * (1 + len(parts)),
        out_specs=ANY,
        scratch_shapes=[
            pltpu.VMEM((tall, LANES), jnp.bfloat16),
            pltpu.VMEM((fans, tall, 2 * LANES), jnp.bfloat16),
            pltpu.VMEM((blocks, size, LANES), jnp.bfloat16),
            pltpu.VMEM((blocks, rows, LANES), jnp.float32),
            pltpu.SemaphoreType.DMA((blocks,)),
            pltpu.SemaphoreType.DMA((blocks,)),
        ],
        out_shape=jax.ShapeDtypeStruct(out.shape, jnp.float32),
        input_output_aliases={6: 0},
        cost_estimate=NO_COST,
        compiler_params=PARAMS,
        name="last_pass",
    )(slots, *past, mats, times, out, *parts)


def per_device(
    traces, first_trace_taps, first_time_taps, second_trace_taps, second_time_taps, dest_row
):
    blocks, samples, _ = traces.shape
    owners = lax.axis_size("rcv")
    me = lax.axis_index("rcv").astype(jnp.int32).reshape(1)
    even = (1 - lax.axis_index("shot") % 2).astype(jnp.int32).reshape(1)
    target = dest_row.reshape(blocks)

    def send(values, offset):
        pairs = [(i, (i + offset) % owners) for i in range(owners)]
        return lax.ppermute(values, "rcv", pairs) if offset else values

    bounds = chunk_bounds(samples)
    count = len(bounds) - 1
    sizes = [bounds[step + 1] - bounds[step] for step in range(count)]
    *packed, picks = first_edges(even, traces)
    edges = swap_edges(packed)
    mats, times = weights(even, first_trace_taps, first_time_taps, traces, blocks)

    def first(after, start, sizes, noted):
        return first_pass(
            me, target, owners, traces, edges, mats, times, after, start, sizes, noted
        )

    def exchange(sent, before, *after):
        arrived = []
        for offset, part in enumerate(sent):
            if offset and before is not None:
                part, before[offset], *_ = lax.optimization_barrier(
                    (part, before[offset], *after)
                )
            arrived.append(send(part, offset))
        return arrived

    sent = first([], 0, sizes[:1], True)
    arrived = [exchange(sent[0], None)]
    sent += first([sent[0][0]], bounds[1], sizes[1:], False)
    second_mats, second_times, slots = late_weights(
        even, me, target, second_trace_taps, second_time_taps, arrived[0], sent[-1][0]
    )

    out, past, now, token, rims = None, None, None, None, None

    def second(step, after):
        at = max(0, bounds[step] - REACH // 2)
        stop = bounds[step + 1] - REACH // 2 if step + 1 < count else samples
        return second_pass(
            blocks, samples, past, now, second_mats, second_times, after, out, at, stop - at
        )

    for step in range(count - 1):
        ahead = [*now[1:]] if now else []
        ahead += [token] if token is not None else []
        arrived.append(exchange(sent[step + 1], arrived[step], *ahead))
        gathered, *packed = second_edges(
            even,
            slots,
            picks,
            arrived[step],
            sizes[step],
            rim_rows(sizes[-1]) if step == count - 2 else 0,
            slots if token is None else token,
            blocks,
        )
        rims = packed[0]
        coming = (gathered, *swap_edges(packed))
        if step:
            out, token = second(step - 1, rims)
            past = now
        now = coming
    out, token = second(count - 2, slots)
    at = bounds[count - 1] - REACH // 2
    return last_pass(
        slots, now, arrived[-1], sizes[-1], second_mats, second_times, out, at, samples - at
    )


def solution(mesh):
    in_specs = (P("rcv", None, "shot"), P(), P(), P(), P(), P("rcv", "shot"))
    out_specs = P("rcv", None, "shot")
    return jax.shard_map(
        per_device, mesh=mesh, in_specs=in_specs, out_specs=out_specs, check_vma=False
    )
```
